128 devices in a mesh: dom: 128 (over y, x, z, core).
Axes of the slice: x: 4, y: 4, z: 4, core: 2. Of those that a mesh axis runs over, the one named last changes fastest.
Arguments:
- block_vector: float32 [262144, 128], P('dom')
- tile_values: float32 [40960, 128, 128], P('dom')
- tile_rows: int32 [40960], P('dom'), may hold values from 0 to 15, as said below
- tile_cols: int32 [40960], P('dom'), may hold values from 0 to 143, as said below
- tile_counts: int32 [128, 2], P('dom'), may hold values from 16 to 320, as said below
- export_rows: int32 [128, 2], P('dom'), may hold values from 0 to 15, as said below
- send_pick: int32 [128, 128], P('dom'), may hold values from 0 to 1, as said below
Outputs:
- embedding: float32 [262144, 128], P('dom')
The draws below stay inside these ranges and needn't reach their ends.
Inputs may be any that keep to these rules, and one draw needn't show every extreme that they name: `tile_rows`: slot k < 16 of every partition adds into block row k. `tile_cols`: within each partition's 320 slots: slot k < 16 holds k; the other slots below the partition's interior count hold values below 16; slots from the interior count up to the live count hold 16 + q for partitions q other than the partition itself. `tile_counts`: column 0 is a partition's interior count, at least 16; column 1 its live count, larger than column 0. Exactly one partition has 320 live tiles, every other between 80 and 160. `export_rows`: each row holds 2 different block rows of that partition. `send_pick`: entry (p, q) picks which of partition p's hub block rows partition q receives.
All inputs are finite; a program needn't handle non-finite values.
Results may differ from the reference program's by a relative error of at most 0.00011.
Values sent between devices are 32-bit elements; how exact they have to be, the bound alone decides.
No kernel may reach another device: no remote copies, remote signals or barrier semaphores. Data moves between devices by JAX's collectives and lax.ppermute only.
A program may use at most 128 MiB of HBM per device.

```python
import math
import jax
import jax.numpy as jnp
from jax import lax

COLS = 128
BLK = 128
RB_DEV = 16
TMAX = 320
EXPORT = 2
NV = 262144
N_DOM = 128


def tile_layout(key):
    parts_count = N_DOM
    key_hub = jax.random.fold_in(key, 7001)
    key_total = jax.random.fold_in(key, 7002)
    key_inner = jax.random.fold_in(key, 7003)
    key_rows = jax.random.fold_in(key, 7004)
    key_local = jax.random.fold_in(key, 7005)
    key_offset = jax.random.fold_in(key, 7006)
    key_export = jax.random.fold_in(key, 7007)
    key_pick = jax.random.fold_in(key, 7008)
    hub_index = jax.random.randint(key_hub, (), 0, parts_count)
    partition = jnp.arange(parts_count, dtype=jnp.int32)
    live_total = jax.random.randint(key_total, (parts_count,), TMAX // 4, TMAX // 2 + 1)
    live_total = jnp.where(partition == hub_index, TMAX, live_total).astype(jnp.int32)
    inner_count = live_total // 4 + jax.random.randint(key_inner, (parts_count,), 0, live_total // 4 + 1)
    inner_count = inner_count.astype(jnp.int32)
    slot_index = jnp.arange(TMAX, dtype=jnp.int32)[None, :]
    random_rows = jax.random.randint(key_rows, (parts_count, TMAX), 0, RB_DEV)
    block_rows = jnp.where(slot_index < RB_DEV, slot_index, random_rows).astype(jnp.int32)
    local_cols = jax.random.randint(key_local, (parts_count, TMAX), 0, RB_DEV)
    offset = jax.random.randint(key_offset, (parts_count, 1), 0, parts_count - 1)
    peer = (partition[:, None] + 1 + jnp.mod(slot_index - inner_count[:, None] + offset, parts_count - 1)) % parts_count
    slot_cols = jnp.where(slot_index < RB_DEV, slot_index, jnp.where(slot_index < inner_count[:, None], local_cols, RB_DEV + peer)).astype(jnp.int32)
    scores = jax.random.randint(key_export, (parts_count, RB_DEV), 0, 1 << 20) * RB_DEV + jnp.arange(RB_DEV, dtype=jnp.int32)[None, :]
    exported = jnp.argsort(scores, axis=1)[:, :EXPORT].astype(jnp.int32)
    picks = jax.random.randint(key_pick, (parts_count, parts_count), 0, EXPORT).astype(jnp.int32)
    counts = jnp.stack([inner_count, live_total], axis=1).astype(jnp.int32)
    return (block_rows, slot_cols, counts, exported, picks)


def draw_tile_rows(key, part):
    return tile_layout(key)[0].reshape(-1)


def draw_tile_cols(key, part):
    return tile_layout(key)[1].reshape(-1)


def draw_tile_counts(key, part):
    return tile_layout(key)[2]


def draw_export_rows(key, part):
    return tile_layout(key)[3]


def draw_send_pick(key, part):
    return tile_layout(key)[4]


def draw_tile_values(key, part):
    block_rows = tile_layout(key)[0]
    key_scale = jax.random.fold_in(key, 8001)
    key_size = jax.random.fold_in(key, 8002)
    key_sign = jax.random.fold_in(key, 8003)
    row_scale = jnp.exp(jax.random.uniform(key_scale, (N_DOM, RB_DEV, BLK), minval=0.0, maxval=math.log(100.0)))
    index_grid = jnp.broadcast_to(block_rows[:, :, None], (N_DOM, TMAX, BLK))
    picked_scale = jnp.take_along_axis(row_scale, index_grid, axis=1)
    magnitude = jnp.exp(jax.random.uniform(key_size, (N_DOM, TMAX, BLK, BLK), minval=math.log(0.05), maxval=0.0))
    positive = jax.random.bernoulli(key_sign, 0.5, (N_DOM, TMAX, BLK, BLK))
    values = picked_scale[:, :, :, None] * jnp.where(positive, magnitude, -magnitude)
    return values.reshape(N_DOM * TMAX, BLK, BLK).astype(jnp.float32)


def draw_block_vector(key, part):
    key_columns = jax.random.fold_in(key, 9001)
    key_noise = jax.random.fold_in(key, 9002)
    column_scale = jnp.exp(jax.random.uniform(key_columns, (COLS,), minval=0.0, maxval=math.log(10.0)))
    values = jax.random.normal(key_noise, (NV, COLS)) * column_scale[None, :]
    return values.astype(jnp.float32)


def setup_inputs(seed: int = 0) -> dict:
    key_of = jax.random.split(jax.random.key(seed), 8)
    return {
        "block_vector": draw_block_vector(jax.random.fold_in(key_of[7], 71), 0),
        "tile_values": draw_tile_values(jax.random.fold_in(key_of[7], 71), 0),
        "tile_rows": draw_tile_rows(jax.random.fold_in(key_of[7], 71), 0),
        "tile_cols": draw_tile_cols(jax.random.fold_in(key_of[7], 71), 0),
        "tile_counts": draw_tile_counts(jax.random.fold_in(key_of[7], 71), 0),
        "export_rows": draw_export_rows(jax.random.fold_in(key_of[7], 71), 0),
        "send_pick": draw_send_pick(jax.random.fold_in(key_of[7], 71), 0),
    }


def reference(block_vector, tile_values, tile_rows, tile_cols, tile_counts, export_rows, send_pick):
    partition = jnp.arange(N_DOM, dtype=jnp.int32)
    slot_rows = tile_rows.reshape(N_DOM, TMAX)
    slot_cols = tile_cols.reshape(N_DOM, TMAX)
    weights_all = tile_values.reshape(N_DOM, TMAX, BLK, BLK)
    sent_rows = jnp.take_along_axis(export_rows, send_pick, axis=1).astype(jnp.int32)
    ghost_global = partition[None, :] * RB_DEV + jnp.transpose(sent_rows)
    ghost_index = jnp.clip(slot_cols - RB_DEV, 0, N_DOM - 1).astype(jnp.int32)
    global_cols = jnp.where(slot_cols < RB_DEV, partition[:, None] * RB_DEV + slot_cols, jnp.take_along_axis(ghost_global, ghost_index, axis=1)).astype(jnp.int32)
    live = jnp.arange(TMAX, dtype=jnp.int32)[None, :] < tile_counts[:, 1:2]
    row_ids = jnp.arange(RB_DEV, dtype=jnp.int32)
    placing = jnp.where((slot_rows[:, None, :] == row_ids[None, :, None]) & live[:, None, :], 1.0, 0.0).astype(jnp.float32)

    def degree_of(item):
        weights, place = item
        return jnp.dot(place, lax.optimization_barrier(jnp.sum(jnp.abs(weights), axis=2)), precision=lax.Precision.HIGHEST)
    degree = lax.map(degree_of, (weights_all, placing))
    scaling = lax.rsqrt(degree).reshape(N_DOM * RB_DEV, BLK, 1)

    def apply_once(field):
        scaled = scaling * field

        def one_partition(item):
            weights, place, columns = item
            picked = jnp.take(scaled, columns, axis=0)
            products = jnp.einsum('tij,tjc->tic', weights, picked, precision=lax.Precision.HIGHEST)
            return jnp.einsum('rt,tic->ric', place, products, precision=lax.Precision.HIGHEST)
        summed = lax.map(one_partition, (weights_all, placing, global_cols))
        return scaling * summed.reshape(N_DOM * RB_DEV, BLK, COLS)
    current = block_vector.reshape(N_DOM * RB_DEV, BLK, COLS)
    for application in range(2):
        current = apply_once(current)
    flat = current.reshape(NV, COLS)
    gram = jnp.einsum('rc,rd->cd', flat, flat, precision=lax.Precision.HIGHEST)
    lower = jnp.linalg.cholesky(gram)
    basis = lax.linalg.triangular_solve(lower, flat, left_side=False, lower=True, transpose_a=True)
    return basis * math.sqrt(NV)
```

```python
import functools
import math

import jax
import jax.numpy as jnp
from jax import lax
from jax.experimental import pallas as pl
from jax.experimental.pallas import tpu as pltpu
from jax.sharding import PartitionSpec as P

EXPORT = 2
SLOTS = 16
UNROLL = 4
F32 = jnp.float32
BF16 = jnp.bfloat16
VMEM = pl.BlockSpec(memory_space=pltpu.VMEM)
SMEM = pl.BlockSpec(memory_space=pltpu.SMEM)
ANY = pl.BlockSpec(memory_space=pl.ANY)


def halves(x):
    high = x.astype(BF16)
    low = (x - high.astype(F32)).astype(BF16)
    return jnp.concatenate([high, low], axis=1)


def product(left, right):
    both = jnp.dot(left, jnp.concatenate([right, right], axis=0), preferred_element_type=F32)
    width = both.shape[1] // 2
    return both[:, :width] + both[:, width:]


def stream(count, copies, work):
    rounds = (count + UNROLL - 1) // UNROLL
    total = rounds * UNROLL
    ahead = SLOTS - UNROLL

    def start(i):
        for copy in copies(jnp.minimum(i, count - 1), lax.rem(i, SLOTS)):
            copy.start()

    def prime(i, carry):
        start(i)
        return carry

    lax.fori_loop(0, jnp.minimum(ahead, total), prime, 0)

    def one_round(r, carry):
        base = r * UNROLL
        for u in range(UNROLL):
            i = base + u

            @pl.when(i + ahead < total)
            def _():
                start(i + ahead)

        for u in range(UNROLL):
            i = base + u
            for copy in copies(jnp.minimum(i, count - 1), lax.rem(i, SLOTS)):
                copy.wait()
        work([(jnp.minimum(base + u, count - 1), lax.rem(base + u, SLOTS), base + u < count) for u in range(UNROLL)])
        return carry

    lax.fori_loop(0, rounds, one_round, 0)


def degree_kernel(
    tiles, rows, counts, exports,
    split_out, scale_lane, scale_full, lists,
    buf, half, sem, out_sem,
):
    blocks = scale_full.shape[0]
    inner, live = counts[0, 0], counts[0, 1]
    scale_full[...] = jnp.zeros_like(scale_full)

    def out_copy(i, slot):
        return pltpu.make_async_copy(half.at[slot], split_out.at[i], out_sem.at[slot])

    def copies(i, slot):
        return (pltpu.make_async_copy(tiles.at[i], buf.at[slot], sem.at[slot]),)

    def work(steps):
        for i, slot, alive in steps:

            @pl.when(alive)
            def _():
                @pl.when(i >= SLOTS)
                def _():
                    out_copy(0, slot).wait()

                value = buf[slot]
                half[slot] = halves(value)
                out_copy(i, slot).start()
                row = rows[i]
                scale_full[row] = scale_full[row] + jnp.abs(value)

    stream(live, copies, work)

    def scale_block(r, carry):
        total = scale_full[r]
        full = jnp.broadcast_to(lax.rsqrt(jnp.sum(total, axis=1, keepdims=True)), total.shape)
        scale_full[r] = full
        scale_lane[pl.ds(r, 1), :] = jnp.transpose(full)[0:1, :]
        return carry

    lax.fori_loop(0, blocks, scale_block, 0)

    first_row, second_row = exports[0, 0], exports[0, 1]

    def sort(i, carry):
        near, far = carry
        row = rows[i]
        is_near = (row == first_row) | (row == second_row)

        @pl.when(is_near)
        def _():
            lists[2 + near] = i

        @pl.when(jnp.logical_not(is_near))
        def _():
            lists[2 + tiles.shape[0] + far] = i

        step = is_near.astype(jnp.int32)
        return near + step, far + 1 - step

    near, far = lax.fori_loop(inner, live, sort, (jnp.int32(0), jnp.int32(0)))
    lists[0] = near
    lists[1] = far

    def drain(i, carry):
        out_copy(0, lax.rem(i, SLOTS)).wait()
        return carry

    lax.fori_loop(jnp.maximum(live - SLOTS, 0), live, drain, 0)


def add_tiles(steps, left_of, right_of, row_of, total):
    parts = [product(left_of(i, slot), right_of(i, slot)) for i, slot, _ in steps]
    for (i, _, alive), part in zip(steps, parts):
        row = jnp.where(alive, row_of(i), total.shape[0] - 1)
        total[row] = total[row] + part


def inner_kernel(split, vec, scale_full, rows, cols, counts, total_out, half, scaled, total, sem):
    blocks = total_out.shape[0]
    total[...] = jnp.zeros_like(total)

    def scale_block(r, carry):
        scaled[r] = halves(scale_full[r] * vec[r])
        return carry

    lax.fori_loop(0, blocks, scale_block, 0)

    def copies(i, slot):
        return (pltpu.make_async_copy(split.at[i], half.at[slot], sem.at[slot]),)

    def work(steps):
        add_tiles(
            steps,
            lambda i, slot: half[slot],
            lambda i, slot: scaled[cols[i]],
            lambda i: rows[i],
            total,
        )

    stream(counts[0, 0], copies, work)
    total_out[...] = total[0:blocks]


def near_kernel(
    tiles, offered, rows, cols, exports, picks, lists, ghost_scale, scale_full, inner_sum,
    hub_out, buf, ghost, total, sem, ghost_sem,
):
    blocks = scale_full.shape[0]
    for k in range(EXPORT):
        total[k] = inner_sum[exports[0, k]]
    total[EXPORT] = jnp.zeros_like(total[EXPORT])

    def tile_of(i):
        return lists[2 + i]

    def copies(i, slot):
        t = tile_of(i)
        q = cols[t] - blocks
        return (
            pltpu.make_async_copy(tiles.at[t], buf.at[slot], sem.at[slot]),
            pltpu.make_async_copy(offered.at[q * EXPORT + picks[q]], ghost.at[slot], ghost_sem.at[slot]),
        )

    def left_of(i, slot):
        q = cols[tile_of(i)] - blocks
        return halves(buf[slot] * ghost_scale[pl.ds(q, 1), :])

    def row_of(i):
        return jnp.where(rows[tile_of(i)] == exports[0, 0], 0, 1)

    def work(steps):
        add_tiles(steps, left_of, lambda i, slot: halves(ghost[slot]), row_of, total)

    stream(lists[0], copies, work)
    for k in range(EXPORT):
        scale = scale_full[exports[0, k]]
        hub_out[k] = scale * (scale * total[k])


def far_kernel(
    tiles, split, offered, rows, cols, counts, exports, picks, lists, ghost_scale, scale_full, inner_sum, hub,
    total_out, buf, ghost, half, scaled, total, sem, ghost_sem,
):
    blocks = scale_full.shape[0]
    total[0:blocks] = inner_sum[...]
    total[blocks] = jnp.zeros_like(total[blocks])

    def tile_of(i):
        return lists[2 + tiles.shape[0] + i]

    def copies(i, slot):
        t = tile_of(i)
        q = cols[t] - blocks
        return (
            pltpu.make_async_copy(tiles.at[t], buf.at[slot], sem.at[slot]),
            pltpu.make_async_copy(offered.at[q * EXPORT + picks[q]], ghost.at[slot], ghost_sem.at[slot]),
        )

    def left_of(i, slot):
        q = cols[tile_of(i)] - blocks
        return halves(buf[slot] * ghost_scale[pl.ds(q, 1), :])

    def work(steps):
        add_tiles(steps, left_of, lambda i, slot: halves(ghost[slot]), lambda i: rows[tile_of(i)], total)

    stream(lists[1], copies, work)

    def next_block(r, carry):
        scale = scale_full[r]
        scaled[r] = halves(scale * (scale * total[r]))
        return carry

    lax.fori_loop(0, blocks, next_block, 0)
    for k in range(EXPORT):
        scaled[exports[0, k]] = halves(hub[k])
    total[...] = jnp.zeros_like(total)

    def inner_copies(i, slot):
        return (pltpu.make_async_copy(split.at[i], half.at[slot], sem.at[slot]),)

    def inner_work(steps):
        add_tiles(
            steps,
            lambda i, slot: half[slot],
            lambda i, slot: scaled[cols[i]],
            lambda i: rows[i],
            total,
        )

    stream(counts[0, 0], inner_copies, inner_work)
    total_out[...] = total[0:blocks]


def last_kernel(
    split, offered, rows, cols, counts, picks, scale_full, inner_sum,
    second, gram, half, ghost, total, both, sem, ghost_sem,
):
    blocks, side, width = scale_full.shape
    total[0:blocks] = inner_sum[...]
    total[blocks] = jnp.zeros_like(total[blocks])
    inner = counts[0, 0]

    def copies(i, slot):
        q = cols[inner + i] - blocks
        return (
            pltpu.make_async_copy(split.at[inner + i], half.at[slot], sem.at[slot]),
            pltpu.make_async_copy(offered.at[q * EXPORT + picks[q]], ghost.at[slot], ghost_sem.at[slot]),
        )

    def work(steps):
        add_tiles(
            steps,
            lambda i, slot: half[slot],
            lambda i, slot: halves(ghost[slot]),
            lambda i: rows[inner + i],
            total,
        )

    stream(counts[0, 1] - inner, copies, work)

    both[...] = jnp.zeros_like(both)

    def finish(g, carry):
        pieces = []
        for u in range(4):
            r = g * 4 + u
            value = scale_full[r] * total[r]
            second[r] = value
            pieces.append(halves(value))
        tall = jnp.concatenate(pieces, axis=0)
        both[...] += lax.dot_general(tall, tall, (((0,), (0,)), ((), ())), preferred_element_type=F32)
        return carry

    lax.fori_loop(0, blocks // 4, finish, 0)
    gram[...] = (both[0:width, 0:width] + both[width:, width:]) + (both[0:width, width:] + both[width:, 0:width])


def basis_kernel(gram, second, out, inverse, *, factor):
    size = gram.shape[0]
    groups = size // 8
    a = [gram[8 * g : 8 * g + 8, :] for g in range(groups)]
    lane = lax.broadcasted_iota(jnp.int32, (8, size), 1)
    sub = lax.broadcasted_iota(jnp.int32, (8, size), 0)
    b = [jnp.where(lane == sub + 8 * g, 1.0, 0.0).astype(F32) for g in range(groups)]
    for k in range(size):
        g, j = divmod(k, 8)
        pivot_row = jnp.broadcast_to(a[g][j : j + 1, :], (8, size))
        other_row = jnp.broadcast_to(b[g][j : j + 1, :], (8, size))
        reciprocal = 1.0 / jnp.broadcast_to(a[g][j : j + 1, k : k + 1], (8, size))
        pivot_row = pivot_row * reciprocal
        other_row = other_row * reciprocal
        for i in range(g, groups):
            column = jnp.broadcast_to(a[i][:, k : k + 1], (8, size))
            if i == g:
                if j == 7:
                    continue
                column = jnp.where(sub > j, column, 0.0)
            a[i] = a[i] - column * pivot_row
            b[i] = b[i] - column * other_row
    for g in range(groups):
        diagonal = jnp.sum(jnp.where(lane == sub + 8 * g, a[g], 0.0), axis=1, keepdims=True)
        inverse[8 * g : 8 * g + 8, :] = b[g] * (lax.rsqrt(diagonal) * factor)
    right = halves(jnp.transpose(inverse[...]))
    doubled = jnp.concatenate([right, right], axis=0)

    def one(r, carry):
        part = jnp.dot(halves(second[r]), doubled, preferred_element_type=F32)
        out[r] = part[:, :size] + part[:, size:]
        return carry

    lax.fori_loop(0, second.shape[0], one, 0)


def call(kernel, out_shape, in_specs, out_specs, scratch, flops, data):
    return pl.pallas_call(
        kernel,
        out_shape=out_shape,
        in_specs=in_specs,
        out_specs=out_specs,
        scratch_shapes=scratch,
        cost_estimate=pl.CostEstimate(flops=flops, bytes_accessed=data, transcendentals=0),
        compiler_params=pltpu.CompilerParams(vmem_limit_bytes=40 * 1024 * 1024),
    )


def shift_pairs(parts, stride, extent, step):
    pairs = []
    for device in range(parts):
        place = device // stride % extent
        pairs.append((device, device + ((place + step) % extent - place) * stride))
    return pairs


def sum_over_devices(value, parts):
    value = value + lax.ppermute(value, "dom", shift_pairs(parts, 1, 2, 1))
    stride = 2
    while stride < parts:
        across, left, right = (
            lax.ppermute(value, "dom", shift_pairs(parts, stride, 4, step)) for step in (2, 1, 3)
        )
        value = (value + across) + (left + right)
        stride *= 4
    return value


def shards(block_vector, tile_values, tile_rows, tile_cols, tile_counts, export_rows, send_pick):
    parts = lax.axis_size("dom")
    slots, side, _ = tile_values.shape
    width = block_vector.shape[1]
    blocks = block_vector.shape[0] // side
    vec = block_vector.reshape(blocks, side, width)
    block, wide = (side, width), (side, 2 * width)
    every = jax.ShapeDtypeStruct((blocks,) + block, F32)
    sums = pltpu.VMEM((blocks + 1,) + block, F32)
    spread = pltpu.VMEM((blocks,) + wide, BF16)
    whole = pltpu.VMEM((SLOTS,) + block, F32)
    halved = pltpu.VMEM((SLOTS,) + wide, BF16)
    sems = pltpu.SemaphoreType.DMA((SLOTS,))
    tile_bytes = side * side * 4
    tile_flops = 8 * side * side * width

    offered = lax.all_gather(
        vec.at[export_rows[0]].get(mode="promise_in_bounds"), "dom", axis=0, tiled=True
    )

    split, scale_lane, scale_full, lists = call(
        degree_kernel,
        (
            jax.ShapeDtypeStruct((slots,) + wide, BF16),
            jax.ShapeDtypeStruct((blocks, side), F32),
            every,
            jax.ShapeDtypeStruct((2 + 2 * slots,), jnp.int32),
        ),
        [ANY, SMEM, SMEM, SMEM],
        (ANY, VMEM, VMEM, SMEM),
        [whole, halved, sems, sems],
        slots * side * side * 4,
        2 * slots * tile_bytes,
    )(tile_values, tile_rows, tile_counts, export_rows)

    hub_scale = scale_lane.at[export_rows[0]].get(mode="promise_in_bounds")
    sent = jnp.where(send_pick[0][:, None] == 0, hub_scale[0], hub_scale[1])
    sent = jnp.concatenate(
        [sent, jnp.broadcast_to(send_pick[0][:, None], sent.shape).astype(F32)], axis=1
    )
    received = lax.all_to_all(sent, "dom", split_axis=0, concat_axis=0, tiled=True)
    ghost_scale = received[:, :side]
    picks = received[:, side].astype(jnp.int32)

    inner_sum = call(
        inner_kernel,
        every,
        [ANY, VMEM, VMEM, SMEM, SMEM, SMEM],
        VMEM,
        [halved, spread, sums, sems],
        slots // 4 * tile_flops,
        slots // 4 * tile_bytes,
    )(split, vec, scale_full, tile_rows, tile_cols, tile_counts)

    hub = call(
        near_kernel,
        jax.ShapeDtypeStruct((EXPORT,) + block, F32),
        [ANY, ANY] + [SMEM] * 5 + [VMEM] * 3,
        VMEM,
        [whole, whole, pltpu.VMEM((EXPORT + 1,) + block, F32), sems, sems],
        slots // 16 * tile_flops,
        slots // 8 * tile_bytes,
    )(
        tile_values, offered, tile_rows, tile_cols, export_rows, picks, lists,
        ghost_scale, scale_full, inner_sum,
    )
    offered_next = lax.all_gather(hub, "dom", axis=0, tiled=True)
    inner_next = call(
        far_kernel,
        every,
        [ANY, ANY, ANY] + [SMEM] * 6 + [VMEM] * 4,
        VMEM,
        [whole, whole, halved, spread, sums, sems, sems],
        slots // 2 * tile_flops,
        slots // 2 * tile_bytes,
    )(
        tile_values, split, offered, tile_rows, tile_cols, tile_counts, export_rows, picks, lists,
        ghost_scale, scale_full, inner_sum, hub,
    )
    second, gram = call(
        last_kernel,
        (every, jax.ShapeDtypeStruct((width, width), F32)),
        [ANY, ANY] + [SMEM] * 4 + [VMEM] * 2,
        (VMEM, VMEM),
        [halved, whole, sums, pltpu.VMEM((2 * width, 2 * width), F32), sems, sems],
        slots // 2 * tile_flops,
        slots * tile_bytes,
    )(split, offered_next, tile_rows, tile_cols, tile_counts, picks, scale_full, inner_next)
    basis = call(
        functools.partial(basis_kernel, factor=math.sqrt(blocks * side * parts)),
        every,
        [VMEM, VMEM],
        VMEM,
        [pltpu.VMEM((width, width), F32)],
        blocks * tile_flops,
        2 * blocks * tile_bytes,
    )(sum_over_devices(gram, parts), second)
    return basis.reshape(block_vector.shape)


def solution(mesh):
    in_specs = (
        P("dom", None),
        P("dom", None, None),
        P("dom"),
        P("dom"),
        P("dom", None),
        P("dom", None),
        P("dom", None),
    )
    out_specs = P("dom", None)
    return jax.shard_map(shards, mesh=mesh, in_specs=in_specs, out_specs=out_specs, check_vma=False)
```

```python
import functools
import math

import jax
import jax.numpy as jnp
from jax import lax
from jax.experimental import pallas as pl
from jax.experimental.pallas import tpu as pltpu
from jax.sharding import PartitionSpec as P

EXPORT = 2
SLOTS = 48
UNROLL = 4
F32 = jnp.float32
BF16 = jnp.bfloat16
VMEM = pl.BlockSpec(memory_space=pltpu.VMEM)
SMEM = pl.BlockSpec(memory_space=pltpu.SMEM)
ANY = pl.BlockSpec(memory_space=pl.ANY)


def halves(x):
    high = x.astype(BF16)
    low = (x - high.astype(F32)).astype(BF16)
    return jnp.concatenate([high, low], axis=1)


def product(left, right):
    both = jnp.dot(left, jnp.concatenate([right, right], axis=0), preferred_element_type=F32)
    width = both.shape[1] // 2
    return both[:, :width] + both[:, width:]


def stream(count, copies, work):
    rounds = (count + UNROLL - 1) // UNROLL
    total = rounds * UNROLL
    ahead = SLOTS - UNROLL

    def start(i):
        for copy in copies(jnp.minimum(i, count - 1), lax.rem(i, SLOTS)):
            copy.start()

    def prime(i, carry):
        start(i)
        return carry

    lax.fori_loop(0, jnp.minimum(ahead, total), prime, 0)

    def one_round(r, carry):
        base = r * UNROLL
        for u in range(UNROLL):
            i = base + u

            @pl.when(i + ahead < total)
            def _():
                start(i + ahead)

        for u in range(UNROLL):
            i = base + u
            for copy in copies(jnp.minimum(i, count - 1), lax.rem(i, SLOTS)):
                copy.wait()
        work([(jnp.minimum(base + u, count - 1), lax.rem(base + u, SLOTS), base + u < count) for u in range(UNROLL)])
        return carry

    lax.fori_loop(0, rounds, one_round, 0)


def hub_kernel(vec, exports, out, sem):
    copies = [pltpu.make_async_copy(vec.at[exports[0, k]], out.at[k], sem.at[k]) for k in range(EXPORT)]
    for copy in copies:
        copy.start()
    for copy in copies:
        copy.wait()


def degree_kernel(
    tiles, rows, counts, exports,
    split_out, scale_lane, scale_full, lists,
    buf, half, sem, out_sem,
):
    blocks = scale_full.shape[0]
    inner, live = counts[0, 0], counts[0, 1]
    scale_full[...] = jnp.zeros_like(scale_full)

    def out_copy(i, slot):
        return pltpu.make_async_copy(half.at[slot], split_out.at[i], out_sem.at[slot])

    def copies(i, slot):
        return (pltpu.make_async_copy(tiles.at[i], buf.at[slot], sem.at[slot]),)

    def work(steps):
        for i, slot, alive in steps:

            @pl.when(alive)
            def _():
                @pl.when(i >= SLOTS)
                def _():
                    out_copy(0, slot).wait()

                value = buf[slot]
                half[slot] = halves(value)
                out_copy(i, slot).start()
                row = rows[i]
                scale_full[row] = scale_full[row] + jnp.abs(value)

    stream(live, copies, work)

    def scale_block(r, carry):
        total = scale_full[r]
        full = jnp.broadcast_to(lax.rsqrt(jnp.sum(total, axis=1, keepdims=True)), total.shape)
        scale_full[r] = full
        scale_lane[pl.ds(r, 1), :] = jnp.transpose(full)[0:1, :]
        return carry

    lax.fori_loop(0, blocks, scale_block, 0)

    first_row, second_row = exports[0, 0], exports[0, 1]

    def sort(i, carry):
        near, far = carry
        row = rows[i]
        is_near = (row == first_row) | (row == second_row)

        @pl.when(is_near)
        def _():
            lists[2 + near] = i

        @pl.when(jnp.logical_not(is_near))
        def _():
            lists[2 + tiles.shape[0] + far] = i

        step = is_near.astype(jnp.int32)
        return near + step, far + 1 - step

    near, far = lax.fori_loop(inner, live, sort, (jnp.int32(0), jnp.int32(0)))
    lists[0] = near
    lists[1] = far

    def drain(i, carry):
        out_copy(0, lax.rem(i, SLOTS)).wait()
        return carry

    lax.fori_loop(jnp.maximum(live - SLOTS, 0), live, drain, 0)


def add_tiles(steps, left_of, right_of, row_of, total):
    parts = [product(left_of(i, slot), right_of(i, slot)) for i, slot, _ in steps]
    for (i, _, alive), part in zip(steps, parts):
        row = jnp.where(alive, row_of(i), total.shape[0] - 1)
        total[row] = total[row] + part


def inner_kernel(split, vec, scale_full, rows, cols, counts, total_out, half, scaled, total, sem):
    blocks = total_out.shape[0]
    total[...] = jnp.zeros_like(total)

    def scale_block(r, carry):
        scaled[r] = halves(scale_full[r] * vec[r])
        return carry

    lax.fori_loop(0, blocks, scale_block, 0)

    def copies(i, slot):
        return (pltpu.make_async_copy(split.at[i], half.at[slot], sem.at[slot]),)

    def work(steps):
        add_tiles(
            steps,
            lambda i, slot: half[slot],
            lambda i, slot: scaled[cols[i]],
            lambda i: rows[i],
            total,
        )

    stream(counts[0, 0], copies, work)
    total_out[...] = total[0:blocks]


def near_kernel(
    tiles, offered, rows, cols, exports, picks, lists, ghost_scale, scale_full, inner_sum,
    hub_out, buf, ghost, total, sem, ghost_sem,
):
    blocks = scale_full.shape[0]
    for k in range(EXPORT):
        total[k] = inner_sum[exports[0, k]]
    total[EXPORT] = jnp.zeros_like(total[EXPORT])

    def tile_of(i):
        return lists[2 + i]

    def copies(i, slot):
        t = tile_of(i)
        q = cols[t] - blocks
        return (
            pltpu.make_async_copy(tiles.at[t], buf.at[slot], sem.at[slot]),
            pltpu.make_async_copy(offered.at[q * EXPORT + picks[q]], ghost.at[slot], ghost_sem.at[slot]),
        )

    def left_of(i, slot):
        q = cols[tile_of(i)] - blocks
        return halves(buf[slot] * ghost_scale[pl.ds(q, 1), :])

    def row_of(i):
        return jnp.where(rows[tile_of(i)] == exports[0, 0], 0, 1)

    def work(steps):
        add_tiles(steps, left_of, lambda i, slot: halves(ghost[slot]), row_of, total)

    stream(lists[0], copies, work)
    for k in range(EXPORT):
        scale = scale_full[exports[0, k]]
        hub_out[k] = scale * (scale * total[k])


def far_kernel(
    tiles, split, offered, rows, cols, counts, exports, picks, lists, ghost_scale, scale_full, inner_sum, hub,
    total_out, buf, ghost, half, scaled, total, sem, ghost_sem,
):
    blocks = scale_full.shape[0]
    total[0:blocks] = inner_sum[...]
    total[blocks] = jnp.zeros_like(total[blocks])

    def tile_of(i):
        return lists[2 + tiles.shape[0] + i]

    def copies(i, slot):
        t = tile_of(i)
        q = cols[t] - blocks
        return (
            pltpu.make_async_copy(tiles.at[t], buf.at[slot], sem.at[slot]),
            pltpu.make_async_copy(offered.at[q * EXPORT + picks[q]], ghost.at[slot], ghost_sem.at[slot]),
        )

    def left_of(i, slot):
        q = cols[tile_of(i)] - blocks
        return halves(buf[slot] * ghost_scale[pl.ds(q, 1), :])

    def work(steps):
        add_tiles(steps, left_of, lambda i, slot: halves(ghost[slot]), lambda i: rows[tile_of(i)], total)

    stream(lists[1], copies, work)

    def next_block(r, carry):
        scale = scale_full[r]
        scaled[r] = halves(scale * (scale * total[r]))
        return carry

    lax.fori_loop(0, blocks, next_block, 0)
    for k in range(EXPORT):
        scaled[exports[0, k]] = halves(hub[k])
    total[...] = jnp.zeros_like(total)

    def inner_copies(i, slot):
        return (pltpu.make_async_copy(split.at[i], half.at[slot], sem.at[slot]),)

    def inner_work(steps):
        add_tiles(
            steps,
            lambda i, slot: half[slot],
            lambda i, slot: scaled[cols[i]],
            lambda i: rows[i],
            total,
        )

    stream(counts[0, 0], inner_copies, inner_work)
    total_out[...] = total[0:blocks]


def last_kernel(
    split, offered, rows, cols, counts, picks, scale_full, inner_sum,
    second, gram, half, ghost, total, both, sem, ghost_sem,
):
    blocks, side, width = scale_full.shape
    total[0:blocks] = inner_sum[...]
    total[blocks] = jnp.zeros_like(total[blocks])
    inner = counts[0, 0]

    def copies(i, slot):
        q = cols[inner + i] - blocks
        return (
            pltpu.make_async_copy(split.at[inner + i], half.at[slot], sem.at[slot]),
            pltpu.make_async_copy(offered.at[q * EXPORT + picks[q]], ghost.at[slot], ghost_sem.at[slot]),
        )

    def work(steps):
        add_tiles(
            steps,
            lambda i, slot: half[slot],
            lambda i, slot: halves(ghost[slot]),
            lambda i: rows[inner + i],
            total,
        )

    stream(counts[0, 1] - inner, copies, work)

    both[...] = jnp.zeros_like(both)

    def finish(g, carry):
        pieces = []
        for u in range(4):
            r = g * 4 + u
            value = scale_full[r] * total[r]
            second[r] = value
            pieces.append(halves(value))
        tall = jnp.concatenate(pieces, axis=0)
        both[...] += lax.dot_general(tall, tall, (((0,), (0,)), ((), ())), preferred_element_type=F32)
        return carry

    lax.fori_loop(0, blocks // 4, finish, 0)
    gram[...] = (both[0:width, 0:width] + both[width:, width:]) + (both[0:width, width:] + both[width:, 0:width])


def thirds(x):
    high = x.astype(BF16).astype(F32)
    rest = x - high
    middle = rest.astype(BF16).astype(F32)
    return high, middle, rest - middle


def inverse_factor(a, b, size):
    groups = size // 8
    sub = lax.broadcasted_iota(jnp.int32, (8, size), 0)
    masks = [sub == i for i in range(8)]
    rows = []
    for p in range(groups):
        block, other = a[p], b[p]
        s = [
            [jnp.broadcast_to(block[i : i + 1, 8 * p + j : 8 * p + j + 1], (8, size)) for j in range(i + 1)]
            for i in range(8)
        ]
        block_rows = [jnp.broadcast_to(block[i : i + 1, :], (8, size)) for i in range(8)]
        other_rows = [jnp.broadcast_to(other[i : i + 1, :], (8, size)) for i in range(8)]
        low = [[None] * 8 for _ in range(8)]
        reciprocals = []
        for k in range(8):
            reciprocal = 1.0 / s[k][k]
            reciprocals.append(reciprocal)
            for i in range(k + 1, 8):
                low[i][k] = s[i][k] * reciprocal
            for i in range(k + 1, 8):
                for j in range(k + 1, i + 1):
                    s[i][j] = s[i][j] - low[i][k] * s[j][k]
        inv = [[None] * 8 for _ in range(8)]
        for i in range(8):
            for j in range(i):
                total = low[i][j]
                for k in range(j + 1, i):
                    total = total + low[i][k] * inv[k][j]
                inv[i][j] = -total
        pivots, roots = reciprocals[0], s[0][0]
        for i in range(1, 8):
            pivots = jnp.where(masks[i], reciprocals[i], pivots)
            roots = jnp.where(masks[i], s[i][i], roots)
        new_block, new_other = block, other
        for j in range(7):
            coefficient = jnp.zeros((8, size), F32)
            for i in range(j + 1, 8):
                coefficient = jnp.where(masks[i], inv[i][j], coefficient)
            new_block = new_block + coefficient * block_rows[j]
            new_other = new_other + coefficient * other_rows[j]
        rows.append(new_other * lax.rsqrt(roots))
        if p + 1 == groups:
            break
        left = thirds(new_block)
        right = thirds(jnp.concatenate([new_block * pivots, new_other * pivots], axis=1))
        tall = jnp.concatenate([x for x in left for _ in range(3)] + [jnp.zeros((8, size), F32)], axis=0)
        wide = jnp.concatenate(list(right) * 3 + [jnp.zeros((8, 2 * size), F32)], axis=0)
        update = lax.dot_general(
            tall.astype(BF16), wide.astype(BF16), (((0,), (0,)), ((), ())), preferred_element_type=F32
        )
        for i in range(p + 1, groups):
            a[i] = a[i] - update[8 * i : 8 * i + 8, :size]
            b[i] = b[i] - update[8 * i : 8 * i + 8, size:]
    return rows


def basis_kernel(gram, second, out, inverse, *, factor):
    size = gram.shape[0]
    groups = size // 8
    lane = lax.broadcasted_iota(jnp.int32, (8, size), 1)
    sub = lax.broadcasted_iota(jnp.int32, (8, size), 0)
    a = [gram[8 * g : 8 * g + 8, :] for g in range(groups)]
    b = [jnp.where(lane == sub + 8 * g, 1.0, 0.0).astype(F32) for g in range(groups)]
    for g, row in enumerate(inverse_factor(a, b, size)):
        inverse[8 * g : 8 * g + 8, :] = row * factor
    right = halves(jnp.transpose(inverse[...]))
    doubled = jnp.concatenate([right, right], axis=0)

    def some(r, carry):
        for u in range(4):
            part = jnp.dot(halves(second[4 * r + u]), doubled, preferred_element_type=F32)
            out[4 * r + u] = part[:, :size] + part[:, size:]
        return carry

    lax.fori_loop(0, second.shape[0] // 4, some, 0)


def call(kernel, out_shape, in_specs, out_specs, scratch, flops, data):
    return pl.pallas_call(
        kernel,
        out_shape=out_shape,
        in_specs=in_specs,
        out_specs=out_specs,
        scratch_shapes=scratch,
        cost_estimate=pl.CostEstimate(flops=flops, bytes_accessed=data, transcendentals=0),
        compiler_params=pltpu.CompilerParams(vmem_limit_bytes=40 * 1024 * 1024),
    )


def shift_pairs(parts, stride, extent, step):
    pairs = []
    for device in range(parts):
        place = device // stride % extent
        pairs.append((device, device + ((place + step) % extent - place) * stride))
    return pairs


def sum_over_devices(value, parts):
    value = value + lax.ppermute(value, "dom", shift_pairs(parts, 1, 2, 1))
    stride = 2
    while stride < parts:
        across, left, right = (
            lax.ppermute(value, "dom", shift_pairs(parts, stride, 4, step)) for step in (2, 1, 3)
        )
        value = (value + across) + (left + right)
        stride *= 4
    return value


def shards(block_vector, tile_values, tile_rows, tile_cols, tile_counts, export_rows, send_pick):
    parts = lax.axis_size("dom")
    slots, side, _ = tile_values.shape
    width = block_vector.shape[1]
    blocks = block_vector.shape[0] // side
    vec = block_vector.reshape(blocks, side, width)
    block, wide = (side, width), (side, 2 * width)
    every = jax.ShapeDtypeStruct((blocks,) + block, F32)
    sums = pltpu.VMEM((blocks + 1,) + block, F32)
    spread = pltpu.VMEM((blocks,) + wide, BF16)
    whole = pltpu.VMEM((SLOTS,) + block, F32)
    halved = pltpu.VMEM((SLOTS,) + wide, BF16)
    sems = pltpu.SemaphoreType.DMA((SLOTS,))
    tile_bytes = side * side * 4
    tile_flops = 8 * side * side * width

    own = call(
        hub_kernel,
        jax.ShapeDtypeStruct((EXPORT,) + block, F32),
        [ANY, SMEM],
        VMEM,
        [pltpu.SemaphoreType.DMA((EXPORT,))],
        0,
        2 * EXPORT * tile_bytes,
    )(vec, export_rows)
    offered = lax.all_gather(own, "dom", axis=0, tiled=True)

    split, scale_lane, scale_full, lists = call(
        degree_kernel,
        (
            jax.ShapeDtypeStruct((slots,) + wide, BF16),
            jax.ShapeDtypeStruct((blocks, side), F32),
            every,
            jax.ShapeDtypeStruct((2 + 2 * slots,), jnp.int32),
        ),
        [ANY, SMEM, SMEM, SMEM],
        (ANY, VMEM, VMEM, SMEM),
        [whole, halved, sems, sems],
        slots * side * side * 4,
        2 * slots * tile_bytes,
    )(tile_values, tile_rows, tile_counts, export_rows)

    hub_scale = scale_lane.at[export_rows[0]].get(mode="promise_in_bounds")
    sent = jnp.where(send_pick[0][:, None] == 0, hub_scale[0], hub_scale[1])
    sent = jnp.concatenate(
        [sent, jnp.broadcast_to(send_pick[0][:, None], sent.shape).astype(F32)], axis=1
    )
    received = lax.all_to_all(sent, "dom", split_axis=0, concat_axis=0, tiled=True)
    ghost_scale = received[:, :side]
    picks = received[:, side].astype(jnp.int32)

    inner_sum = call(
        inner_kernel,
        every,
        [ANY, VMEM, VMEM, SMEM, SMEM, SMEM],
        VMEM,
        [halved, spread, sums, sems],
        slots // 4 * tile_flops,
        slots // 4 * tile_bytes,
    )(split, vec, scale_full, tile_rows, tile_cols, tile_counts)

    hub = call(
        near_kernel,
        jax.ShapeDtypeStruct((EXPORT,) + block, F32),
        [ANY, ANY] + [SMEM] * 5 + [VMEM] * 3,
        VMEM,
        [whole, whole, pltpu.VMEM((EXPORT + 1,) + block, F32), sems, sems],
        slots // 16 * tile_flops,
        slots // 8 * tile_bytes,
    )(
        tile_values, offered, tile_rows, tile_cols, export_rows, picks, lists,
        ghost_scale, scale_full, inner_sum,
    )
    offered_next = lax.all_gather(hub, "dom", axis=0, tiled=True)
    inner_next = call(
        far_kernel,
        every,
        [ANY, ANY, ANY] + [SMEM] * 6 + [VMEM] * 4,
        VMEM,
        [whole, whole, halved, spread, sums, sems, sems],
        slots // 2 * tile_flops,
        slots // 2 * tile_bytes,
    )(
        tile_values, split, offered, tile_rows, tile_cols, tile_counts, export_rows, picks, lists,
        ghost_scale, scale_full, inner_sum, hub,
    )
    second, gram = call(
        last_kernel,
        (every, jax.ShapeDtypeStruct((width, width), F32)),
        [ANY, ANY] + [SMEM] * 4 + [VMEM] * 2,
        (VMEM, VMEM),
        [halved, whole, sums, pltpu.VMEM((2 * width, 2 * width), F32), sems, sems],
        slots // 2 * tile_flops,
        slots * tile_bytes,
    )(split, offered_next, tile_rows, tile_cols, tile_counts, picks, scale_full, inner_next)
    basis = call(
        functools.partial(basis_kernel, factor=math.sqrt(blocks * side * parts)),
        every,
        [VMEM, VMEM],
        VMEM,
        [pltpu.VMEM((width, width), F32)],
        blocks * tile_flops,
        2 * blocks * tile_bytes,
    )(sum_over_devices(gram, parts), second)
    return basis.reshape(block_vector.shape)


def solution(mesh):
    in_specs = (
        P("dom", None),
        P("dom", None, None),
        P("dom"),
        P("dom"),
        P("dom", None),
        P("dom", None),
        P("dom", None),
    )
    out_specs = P("dom", None)
    return jax.shard_map(shards, mesh=mesh, in_specs=in_specs, out_specs=out_specs, check_vma=False)
```

```python
import functools
import math

import jax
import jax.numpy as jnp
from jax import lax
from jax.experimental import pallas as pl
from jax.experimental.pallas import tpu as pltpu
from jax.sharding import PartitionSpec as P

EXPORT = 2
SLOTS = 48
UNROLL = 8
F32 = jnp.float32
BF16 = jnp.bfloat16
VMEM = pl.BlockSpec(memory_space=pltpu.VMEM)
SMEM = pl.BlockSpec(memory_space=pltpu.SMEM)
ANY = pl.BlockSpec(memory_space=pl.ANY)


def halves(x):
    high = x.astype(BF16)
    low = (x - high.astype(F32)).astype(BF16)
    return jnp.concatenate([high, low], axis=1)


def product(left, right):
    both = jnp.dot(left, jnp.concatenate([right, right], axis=0), preferred_element_type=F32)
    width = both.shape[1] // 2
    return both[:, :width] + both[:, width:]


def stream(count, copies, work, group=None):
    rounds = (count + UNROLL - 1) // UNROLL
    ahead = SLOTS // UNROLL - 1

    def of_round(r):
        first = r * UNROLL
        found = [] if group is None else [group(first, lax.rem(first, SLOTS))]
        for u in range(UNROLL):
            found.extend(copies(jnp.minimum(first + u, count - 1), lax.rem(first + u, SLOTS)))
        return found

    def start(r, carry):
        for copy in of_round(r):
            copy.start()
        return carry

    lax.fori_loop(0, jnp.minimum(ahead, rounds), start, 0)

    def one_round(r, carry):
        @pl.when(r + ahead < rounds)
        def _():
            start(r + ahead, 0)

        for copy in of_round(r):
            copy.wait()
        first = r * UNROLL
        work(
            [
                (jnp.minimum(first + u, count - 1), lax.rem(first + u, SLOTS), first + u < count)
                for u in range(UNROLL)
            ]
        )
        return carry

    lax.fori_loop(0, rounds, one_round, 0)


def window(array, first):
    return jnp.minimum(first, array.shape[0] - UNROLL)


def hub_kernel(vec, exports, out, sem):
    copies = [pltpu.make_async_copy(vec.at[exports[0, k]], out.at[k], sem.at[k]) for k in range(EXPORT)]
    for copy in copies:
        copy.start()
    for copy in copies:
        copy.wait()


def degree_kernel(
    tiles, rows, counts, exports,
    split_out, scale_lane, scale_full, lists,
    buf, half, sem, out_sem,
):
    blocks = scale_full.shape[0]
    inner, live = counts[0, 0], counts[0, 1]
    scale_full[...] = jnp.zeros_like(scale_full)

    def out_copy(i, slot):
        return pltpu.make_async_copy(half.at[slot], split_out.at[i], out_sem.at[slot])

    def copies(i, slot):
        return (pltpu.make_async_copy(tiles.at[i], buf.at[slot], sem.at[slot]),)

    def work(steps):
        for i, slot, alive in steps:

            @pl.when(alive)
            def _():
                @pl.when(i >= SLOTS)
                def _():
                    out_copy(0, slot).wait()

                value = buf[slot]
                half[slot] = halves(value)
                out_copy(i, slot).start()
                row = rows[i]
                scale_full[row] = scale_full[row] + jnp.abs(value)

    stream(live, copies, work)

    def scale_block(r, carry):
        total = scale_full[r]
        full = jnp.broadcast_to(lax.rsqrt(jnp.sum(total, axis=1, keepdims=True)), total.shape)
        scale_full[r] = full
        scale_lane[pl.ds(r, 1), :] = jnp.transpose(full)[0:1, :]
        return carry

    lax.fori_loop(0, blocks, scale_block, 0)

    first_row, second_row = exports[0, 0], exports[0, 1]

    def sort(i, carry):
        near, far = carry
        row = rows[i]
        is_near = (row == first_row) | (row == second_row)

        @pl.when(is_near)
        def _():
            lists[2 + near] = i

        @pl.when(jnp.logical_not(is_near))
        def _():
            lists[2 + tiles.shape[0] + far] = i

        step = is_near.astype(jnp.int32)
        return near + step, far + 1 - step

    near, far = lax.fori_loop(inner, live, sort, (jnp.int32(0), jnp.int32(0)))
    lists[0] = near
    lists[1] = far

    def drain(i, carry):
        out_copy(0, lax.rem(i, SLOTS)).wait()
        return carry

    lax.fori_loop(jnp.maximum(live - SLOTS, 0), live, drain, 0)


def add_tiles(steps, left_of, right_of, row_of, total):
    parts = [product(left_of(i, slot), right_of(i, slot)) for i, slot, _ in steps]
    for (i, _, alive), part in zip(steps, parts):
        row = jnp.where(alive, row_of(i), total.shape[0] - 1)
        total[row] = total[row] + part


def halves_group(split, half, sem, begin):
    def group(first, slot):
        return pltpu.make_async_copy(
            split.at[pl.ds(window(split, begin + first), UNROLL)], half.at[pl.ds(slot, UNROLL)], sem.at[slot]
        )

    def tile(i, slot):
        first = i // UNROLL * UNROLL
        place = begin + i - window(split, begin + first)
        return half[slot // UNROLL * UNROLL + place]

    return group, tile


def add_inner(split, half, sem, scaled, rows, cols, count, total):
    group, tile = halves_group(split, half, sem, 0)

    def work(steps):
        add_tiles(steps, tile, lambda i, slot: scaled[cols[i]], lambda i: rows[i], total)

    stream(count, lambda i, slot: (), work, group)


def inner_kernel(split, vec, scale_full, rows, cols, counts, total_out, half, scaled, total, sem):
    blocks = total_out.shape[0]
    total[...] = jnp.zeros_like(total)

    def scale_block(r, carry):
        scaled[r] = halves(scale_full[r] * vec[r])
        return carry

    lax.fori_loop(0, blocks, scale_block, 0)

    add_inner(split, half, sem, scaled, rows, cols, counts[0, 0], total)
    total_out[...] = total[0:blocks]


def near_kernel(
    tiles, offered, rows, cols, exports, picks, lists, ghost_scale, scale_full, inner_sum,
    hub_out, buf, ghost, total, sem, ghost_sem,
):
    blocks = scale_full.shape[0]
    for k in range(EXPORT):
        total[k] = inner_sum[exports[0, k]]
    total[EXPORT] = jnp.zeros_like(total[EXPORT])

    def tile_of(i):
        return lists[2 + i]

    def copies(i, slot):
        t = tile_of(i)
        q = cols[t] - blocks
        return (
            pltpu.make_async_copy(tiles.at[t], buf.at[slot], sem.at[slot]),
            pltpu.make_async_copy(offered.at[q * EXPORT + picks[q]], ghost.at[slot], ghost_sem.at[slot]),
        )

    def left_of(i, slot):
        q = cols[tile_of(i)] - blocks
        return halves(buf[slot] * ghost_scale[pl.ds(q, 1), :])

    def row_of(i):
        return jnp.where(rows[tile_of(i)] == exports[0, 0], 0, 1)

    def work(steps):
        add_tiles(steps, left_of, lambda i, slot: halves(ghost[slot]), row_of, total)

    stream(lists[0], copies, work)
    for k in range(EXPORT):
        scale = scale_full[exports[0, k]]
        hub_out[k] = scale * (scale * total[k])


def far_kernel(
    tiles, split, offered, rows, cols, counts, exports, picks, lists, ghost_scale, scale_full, inner_sum, hub,
    total_out, buf, ghost, half, scaled, total, sem, ghost_sem,
):
    blocks = scale_full.shape[0]
    total[0:blocks] = inner_sum[...]
    total[blocks] = jnp.zeros_like(total[blocks])

    def tile_of(i):
        return lists[2 + tiles.shape[0] + i]

    def copies(i, slot):
        t = tile_of(i)
        q = cols[t] - blocks
        return (
            pltpu.make_async_copy(tiles.at[t], buf.at[slot], sem.at[slot]),
            pltpu.make_async_copy(offered.at[q * EXPORT + picks[q]], ghost.at[slot], ghost_sem.at[slot]),
        )

    def left_of(i, slot):
        q = cols[tile_of(i)] - blocks
        return halves(buf[slot] * ghost_scale[pl.ds(q, 1), :])

    def work(steps):
        add_tiles(steps, left_of, lambda i, slot: halves(ghost[slot]), lambda i: rows[tile_of(i)], total)

    stream(lists[1], copies, work)

    def next_block(r, carry):
        scale = scale_full[r]
        scaled[r] = halves(scale * (scale * total[r]))
        return carry

    lax.fori_loop(0, blocks, next_block, 0)
    for k in range(EXPORT):
        scaled[exports[0, k]] = halves(hub[k])
    total[...] = jnp.zeros_like(total)

    add_inner(split, half, sem, scaled, rows, cols, counts[0, 0], total)
    total_out[...] = total[0:blocks]


def last_kernel(
    split, offered, rows, cols, counts, picks, scale_full, inner_sum,
    second, gram, half, ghost, total, both, sem, ghost_sem,
):
    blocks, side, width = scale_full.shape
    total[0:blocks] = inner_sum[...]
    total[blocks] = jnp.zeros_like(total[blocks])
    inner = counts[0, 0]

    group, tile = halves_group(split, half, sem, inner)

    def copies(i, slot):
        q = cols[inner + i] - blocks
        return (pltpu.make_async_copy(offered.at[q * EXPORT + picks[q]], ghost.at[slot], ghost_sem.at[slot]),)

    def work(steps):
        add_tiles(
            steps,
            tile,
            lambda i, slot: halves(ghost[slot]),
            lambda i: rows[inner + i],
            total,
        )

    stream(counts[0, 1] - inner, copies, work, group)

    both[...] = jnp.zeros_like(both)

    def finish(g, carry):
        pieces = []
        for u in range(4):
            r = g * 4 + u
            value = scale_full[r] * total[r]
            second[r] = value
            pieces.append(halves(value))
        tall = jnp.concatenate(pieces, axis=0)
        both[...] += lax.dot_general(tall, tall, (((0,), (0,)), ((), ())), preferred_element_type=F32)
        return carry

    lax.fori_loop(0, blocks // 4, finish, 0)
    gram[...] = (both[0:width, 0:width] + both[width:, width:]) + (both[0:width, width:] + both[width:, 0:width])


def thirds(x):
    high = x.astype(BF16).astype(F32)
    rest = x - high
    middle = rest.astype(BF16).astype(F32)
    return high, middle, rest - middle


def inverse_factor(a, b, size):
    groups = size // 8
    sub = lax.broadcasted_iota(jnp.int32, (8, size), 0)
    masks = [sub == i for i in range(8)]
    rows = []
    for p in range(groups):
        block, other = a[p], b[p]
        s = [
            [jnp.broadcast_to(block[i : i + 1, 8 * p + j : 8 * p + j + 1], (8, size)) for j in range(i + 1)]
            for i in range(8)
        ]
        block_rows = [jnp.broadcast_to(block[i : i + 1, :], (8, size)) for i in range(8)]
        other_rows = [jnp.broadcast_to(other[i : i + 1, :], (8, size)) for i in range(8)]
        low = [[None] * 8 for _ in range(8)]
        reciprocals = []
        for k in range(8):
            reciprocal = 1.0 / s[k][k]
            reciprocals.append(reciprocal)
            for i in range(k + 1, 8):
                low[i][k] = s[i][k] * reciprocal
            for i in range(k + 1, 8):
                for j in range(k + 1, i + 1):
                    s[i][j] = s[i][j] - low[i][k] * s[j][k]
        inv = [[None] * 8 for _ in range(8)]
        for i in range(8):
            for j in range(i):
                total = low[i][j]
                for k in range(j + 1, i):
                    total = total + low[i][k] * inv[k][j]
                inv[i][j] = -total
        pivots, roots = reciprocals[0], s[0][0]
        for i in range(1, 8):
            pivots = jnp.where(masks[i], reciprocals[i], pivots)
            roots = jnp.where(masks[i], s[i][i], roots)
        new_block, new_other = block, other
        for j in range(7):
            coefficient = jnp.zeros((8, size), F32)
            for i in range(j + 1, 8):
                coefficient = jnp.where(masks[i], inv[i][j], coefficient)
            new_block = new_block + coefficient * block_rows[j]
            new_other = new_other + coefficient * other_rows[j]
        rows.append(new_other * lax.rsqrt(roots))
        if p + 1 == groups:
            break
        left = thirds(new_block)
        right = thirds(jnp.concatenate([new_block * pivots, new_other * pivots], axis=1))
        tall = jnp.concatenate([x for x in left for _ in range(3)] + [jnp.zeros((8, size), F32)], axis=0)
        wide = jnp.concatenate(list(right) * 3 + [jnp.zeros((8, 2 * size), F32)], axis=0)
        update = lax.dot_general(
            tall.astype(BF16), wide.astype(BF16), (((0,), (0,)), ((), ())), preferred_element_type=F32
        )
        for i in range(p + 1, groups):
            a[i] = a[i] - update[8 * i : 8 * i + 8, :size]
            b[i] = b[i] - update[8 * i : 8 * i + 8, size:]
    return rows


def basis_kernel(gram, second, out, inverse, *, factor):
    size = gram.shape[0]
    groups = size // 8
    lane = lax.broadcasted_iota(jnp.int32, (8, size), 1)
    sub = lax.broadcasted_iota(jnp.int32, (8, size), 0)
    a = [gram[8 * g : 8 * g + 8, :] for g in range(groups)]
    b = [jnp.where(lane == sub + 8 * g, 1.0, 0.0).astype(F32) for g in range(groups)]
    for g, row in enumerate(inverse_factor(a, b, size)):
        inverse[8 * g : 8 * g + 8, :] = row * factor
    high, middle, low = (x.astype(BF16) for x in thirds(jnp.transpose(inverse[...])))
    main = jnp.concatenate([jnp.concatenate([high, middle], axis=1)] * 2, axis=0)
    rest = jnp.concatenate([low, high], axis=0)

    def some(r, carry):
        for u in range(4):
            left = [x.astype(BF16) for x in thirds(second[4 * r + u])]
            part = jnp.dot(jnp.concatenate(left[:2], axis=1), main, preferred_element_type=F32)
            small = jnp.dot(jnp.concatenate(left[::2], axis=1), rest, preferred_element_type=F32)
            out[4 * r + u] = part[:, :size] + (part[:, size:] + small)
        return carry

    lax.fori_loop(0, second.shape[0] // 4, some, 0)


def call(kernel, out_shape, in_specs, out_specs, scratch, flops, data):
    return pl.pallas_call(
        kernel,
        out_shape=out_shape,
        in_specs=in_specs,
        out_specs=out_specs,
        scratch_shapes=scratch,
        cost_estimate=pl.CostEstimate(flops=flops, bytes_accessed=data, transcendentals=0),
        compiler_params=pltpu.CompilerParams(vmem_limit_bytes=40 * 1024 * 1024),
    )


def shift_pairs(parts, stride, extent, step):
    pairs = []
    for device in range(parts):
        place = device // stride % extent
        pairs.append((device, device + ((place + step) % extent - place) * stride))
    return pairs


def sum_over_devices(value, parts):
    value = value + lax.ppermute(value, "dom", shift_pairs(parts, 1, 2, 1))
    stride = 2
    while stride < parts:
        across, left, right = (
            lax.ppermute(value, "dom", shift_pairs(parts, stride, 4, step)) for step in (2, 1, 3)
        )
        value = (value + across) + (left + right)
        stride *= 4
    return value


def shards(block_vector, tile_values, tile_rows, tile_cols, tile_counts, export_rows, send_pick):
    parts = lax.axis_size("dom")
    slots, side, _ = tile_values.shape
    width = block_vector.shape[1]
    blocks = block_vector.shape[0] // side
    vec = block_vector.reshape(blocks, side, width)
    block, wide = (side, width), (side, 2 * width)
    every = jax.ShapeDtypeStruct((blocks,) + block, F32)
    sums = pltpu.VMEM((blocks + 1,) + block, F32)
    spread = pltpu.VMEM((blocks,) + wide, BF16)
    whole = pltpu.VMEM((SLOTS,) + block, F32)
    halved = pltpu.VMEM((SLOTS,) + wide, BF16)
    sems = pltpu.SemaphoreType.DMA((SLOTS,))
    tile_bytes = side * side * 4
    tile_flops = 8 * side * side * width

    own = call(
        hub_kernel,
        jax.ShapeDtypeStruct((EXPORT,) + block, F32),
        [ANY, SMEM],
        VMEM,
        [pltpu.SemaphoreType.DMA((EXPORT,))],
        0,
        2 * EXPORT * tile_bytes,
    )(vec, export_rows)
    offered = lax.all_gather(own, "dom", axis=0, tiled=True)

    split, scale_lane, scale_full, lists = call(
        degree_kernel,
        (
            jax.ShapeDtypeStruct((slots,) + wide, BF16),
            jax.ShapeDtypeStruct((blocks, side), F32),
            every,
            jax.ShapeDtypeStruct((2 + 2 * slots,), jnp.int32),
        ),
        [ANY, SMEM, SMEM, SMEM],
        (ANY, VMEM, VMEM, SMEM),
        [whole, halved, sems, sems],
        slots * side * side * 4,
        2 * slots * tile_bytes,
    )(tile_values, tile_rows, tile_counts, export_rows)

    hub_scale = scale_lane.at[export_rows[0]].get(mode="promise_in_bounds")
    sent = jnp.where(send_pick[0][:, None] == 0, hub_scale[0], hub_scale[1])
    sent = jnp.concatenate(
        [sent, jnp.broadcast_to(send_pick[0][:, None], sent.shape).astype(F32)], axis=1
    )
    received = lax.all_to_all(sent, "dom", split_axis=0, concat_axis=0, tiled=True)
    ghost_scale = received[:, :side]
    picks = received[:, side].astype(jnp.int32)

    inner_sum = call(
        inner_kernel,
        every,
        [ANY, VMEM, VMEM, SMEM, SMEM, SMEM],
        VMEM,
        [halved, spread, sums, sems],
        slots // 4 * tile_flops,
        slots // 4 * tile_bytes,
    )(split, vec, scale_full, tile_rows, tile_cols, tile_counts)

    hub = call(
        near_kernel,
        jax.ShapeDtypeStruct((EXPORT,) + block, F32),
        [ANY, ANY] + [SMEM] * 5 + [VMEM] * 3,
        VMEM,
        [whole, whole, pltpu.VMEM((EXPORT + 1,) + block, F32), sems, sems],
        slots // 16 * tile_flops,
        slots // 8 * tile_bytes,
    )(
        tile_values, offered, tile_rows, tile_cols, export_rows, picks, lists,
        ghost_scale, scale_full, inner_sum,
    )
    offered_next = lax.all_gather(hub, "dom", axis=0, tiled=True)
    inner_next = call(
        far_kernel,
        every,
        [ANY, ANY, ANY] + [SMEM] * 6 + [VMEM] * 4,
        VMEM,
        [whole, whole, halved, spread, sums, sems, sems],
        slots // 2 * tile_flops,
        slots // 2 * tile_bytes,
    )(
        tile_values, split, offered, tile_rows, tile_cols, tile_counts, export_rows, picks, lists,
        ghost_scale, scale_full, inner_sum, hub,
    )
    second, gram = call(
        last_kernel,
        (every, jax.ShapeDtypeStruct((width, width), F32)),
        [ANY, ANY] + [SMEM] * 4 + [VMEM] * 2,
        (VMEM, VMEM),
        [halved, whole, sums, pltpu.VMEM((2 * width, 2 * width), F32), sems, sems],
        slots // 2 * tile_flops,
        slots * tile_bytes,
    )(split, offered_next, tile_rows, tile_cols, tile_counts, picks, scale_full, inner_next)
    basis = call(
        functools.partial(basis_kernel, factor=math.sqrt(blocks * side * parts)),
        every,
        [VMEM, VMEM],
        VMEM,
        [pltpu.VMEM((width, width), F32)],
        blocks * tile_flops,
        2 * blocks * tile_bytes,
    )(sum_over_devices(gram, parts), second)
    return basis.reshape(block_vector.shape)


def solution(mesh):
    in_specs = (
        P("dom", None),
        P("dom", None, None),
        P("dom"),
        P("dom"),
        P("dom", None),
        P("dom", None),
        P("dom", None),
    )
    out_specs = P("dom", None)
    return jax.shard_map(shards, mesh=mesh, in_specs=in_specs, out_specs=out_specs, check_vma=False)
```

```python
import functools
import math

import jax
import jax.numpy as jnp
from jax import lax
from jax.experimental import pallas as pl
from jax.experimental.pallas import tpu as pltpu
from jax.sharding import PartitionSpec as P

EXPORT = 2
N_CHIPS = 64
STRIDES = (2, 8, 32)
PIECES = 10
PLANE = 32
SLOTS = 48
UNROLL = 8
F32 = jnp.float32
BF16 = jnp.bfloat16
VMEM = pl.BlockSpec(memory_space=pltpu.VMEM)
SMEM = pl.BlockSpec(memory_space=pltpu.SMEM)
ANY = pl.BlockSpec(memory_space=pl.ANY)


def halves(x):
    high = x.astype(BF16)
    low = (x - high.astype(F32)).astype(BF16)
    return jnp.concatenate([high, low], axis=1)


def product(left, right):
    both = jnp.dot(left, jnp.concatenate([right, right], axis=0), preferred_element_type=F32)
    width = both.shape[1] // 2
    return both[:, :width] + both[:, width:]


def stream(count, copies, work, group=None):
    rounds = (count + UNROLL - 1) // UNROLL
    ahead = SLOTS // UNROLL - 1

    def of_round(r):
        first = r * UNROLL
        found = [] if group is None else [group(first, lax.rem(first, SLOTS))]
        for u in range(UNROLL):
            found.extend(copies(jnp.minimum(first + u, count - 1), lax.rem(first + u, SLOTS)))
        return found

    def start(r, carry):
        for copy in of_round(r):
            copy.start()
        return carry

    lax.fori_loop(0, jnp.minimum(ahead, rounds), start, 0)

    def one_round(r, carry):
        @pl.when(r + ahead < rounds)
        def _():
            start(r + ahead, 0)

        for copy in of_round(r):
            copy.wait()
        first = r * UNROLL
        work(
            [
                (jnp.minimum(first + u, count - 1), lax.rem(first + u, SLOTS), first + u < count)
                for u in range(UNROLL)
            ]
        )
        return carry

    lax.fori_loop(0, rounds, one_round, 0)


def window(array, first):
    return jnp.minimum(first, array.shape[0] - UNROLL)


class GhostCopy:
    def __init__(self, pieces, code, target, sem):
        self.pieces, self.code, self.target, self.sem = pieces, code, target, sem

    def start(self):
        half = len(self.pieces) // 2
        piece, block = self.code // PLANE, lax.rem(self.code, PLANE)

        def some(low):
            for k in range(low, low + half):

                @pl.when(piece == k)
                def _():
                    pltpu.make_async_copy(self.pieces[k].at[block], self.target, self.sem).start()

        @pl.when(piece < half)
        def _():
            some(0)

        @pl.when(piece >= half)
        def _():
            some(half)

    def wait(self):
        pltpu.make_async_copy(self.pieces[0].at[0], self.target, self.sem).wait()


def hub_kernel(vec, exports, out, sem):
    copies = [pltpu.make_async_copy(vec.at[exports[0, k]], out.at[k], sem.at[k]) for k in range(EXPORT)]
    for copy in copies:
        copy.start()
    for copy in copies:
        copy.wait()


def degree_kernel(
    tiles, after, rows, counts, exports, me,
    split_out, scale_lane, scale_full, lists, places,
    buf, half, sem, out_sem,
):
    blocks = scale_full.shape[0]
    inner, live = counts[0, 0], counts[0, 1]
    scale_full[...] = jnp.zeros_like(scale_full)

    def out_copy(i, slot):
        return pltpu.make_async_copy(half.at[slot], split_out.at[i], out_sem.at[slot])

    def copies(i, slot):
        return (pltpu.make_async_copy(tiles.at[i], buf.at[slot], sem.at[slot]),)

    def work(steps):
        for i, slot, alive in steps:

            @pl.when(alive)
            def _():
                @pl.when(i >= SLOTS)
                def _():
                    out_copy(0, slot).wait()

                value = buf[slot]
                half[slot] = halves(value)
                out_copy(i, slot).start()
                row = rows[i]
                scale_full[row] = scale_full[row] + jnp.abs(value)

    stream(live, copies, work)

    def scale_block(r, carry):
        total = scale_full[r]
        full = jnp.broadcast_to(lax.rsqrt(jnp.sum(total, axis=1, keepdims=True)), total.shape)
        scale_full[r] = full
        scale_lane[pl.ds(r, 1), :] = jnp.transpose(full)[0:1, :]
        return carry

    lax.fori_loop(0, blocks, scale_block, 0)

    first_row, second_row = exports[0, 0], exports[0, 1]

    def sort(i, carry):
        near, far = carry
        row = rows[i]
        is_near = (row == first_row) | (row == second_row)

        @pl.when(is_near)
        def _():
            lists[2 + near] = i

        @pl.when(jnp.logical_not(is_near))
        def _():
            lists[2 + tiles.shape[0] + far] = i

        step = is_near.astype(jnp.int32)
        return near + step, far + 1 - step

    mine = me[0]

    def place(q, carry):
        ahead = [lax.rem(q // stride - mine // stride + 4 * N_CHIPS, 4) for stride in STRIDES]
        odd = lax.rem(q, 2)
        second = jnp.where(odd == 0, ahead[1], ahead[2])
        final = jnp.where(odd == 0, ahead[2], ahead[1])
        piece = jnp.where(final == 0, 0, jnp.where(final == 1, 1, jnp.where(final == 3, 2, jnp.where(second < 2, 3, 4))))
        second = jnp.where(piece == 4, second - 2, second)
        piece = piece + jnp.where(odd == lax.rem(mine, 2), 0, PIECES // 2)
        places[q] = piece * PLANE + (second * 4 + ahead[0]) * EXPORT
        return carry

    lax.fori_loop(0, places.shape[0], place, 0)

    near, far = lax.fori_loop(inner, live, sort, (jnp.int32(0), jnp.int32(0)))
    lists[0] = near
    lists[1] = far

    def drain(i, carry):
        out_copy(0, lax.rem(i, SLOTS)).wait()
        return carry

    lax.fori_loop(jnp.maximum(live - SLOTS, 0), live, drain, 0)


def add_tiles(steps, left_of, right_of, row_of, total):
    parts = [product(left_of(i, slot), right_of(i, slot)) for i, slot, _ in steps]
    for (i, _, alive), part in zip(steps, parts):
        row = jnp.where(alive, row_of(i), total.shape[0] - 1)
        total[row] = total[row] + part


def halves_group(split, half, sem, begin):
    def group(first, slot):
        return pltpu.make_async_copy(
            split.at[pl.ds(window(split, begin + first), UNROLL)], half.at[pl.ds(slot, UNROLL)], sem.at[slot]
        )

    def tile(i, slot):
        first = i // UNROLL * UNROLL
        place = begin + i - window(split, begin + first)
        return half[slot // UNROLL * UNROLL + place]

    return group, tile


def add_inner(split, half, sem, scaled, rows, cols, count, total):
    group, tile = halves_group(split, half, sem, 0)

    def work(steps):
        add_tiles(steps, tile, lambda i, slot: scaled[cols[i]], lambda i: rows[i], total)

    stream(count, lambda i, slot: (), work, group)


def inner_kernel(split, vec, scale_full, rows, cols, counts, total_out, half, scaled, total, sem):
    blocks = total_out.shape[0]
    total[...] = jnp.zeros_like(total)

    def scale_block(r, carry):
        scaled[r] = halves(scale_full[r] * vec[r])
        return carry

    lax.fori_loop(0, blocks, scale_block, 0)

    add_inner(split, half, sem, scaled, rows, cols, counts[0, 0], total)
    total_out[...] = total[0:blocks]


def near_kernel(tiles, *refs):
    pieces = refs[:PIECES]
    (
        rows, cols, exports, picks, places, lists, ghost_scale, scale_full, inner_sum,
        hub_out, buf, ghost, total, sem, ghost_sem,
    ) = refs[PIECES:]
    blocks = scale_full.shape[0]
    for k in range(EXPORT):
        total[k] = inner_sum[exports[0, k]]
    total[EXPORT] = jnp.zeros_like(total[EXPORT])

    def tile_of(i):
        return lists[2 + i]

    def copies(i, slot):
        t = tile_of(i)
        q = cols[t] - blocks
        return (
            pltpu.make_async_copy(tiles.at[t], buf.at[slot], sem.at[slot]),
            GhostCopy(pieces, places[q] + picks[q], ghost.at[slot], ghost_sem.at[slot]),
        )

    def left_of(i, slot):
        q = cols[tile_of(i)] - blocks
        return halves(buf[slot] * ghost_scale[pl.ds(q, 1), :])

    def row_of(i):
        return jnp.where(rows[tile_of(i)] == exports[0, 0], 0, 1)

    def work(steps):
        add_tiles(steps, left_of, lambda i, slot: halves(ghost[slot]), row_of, total)

    stream(lists[0], copies, work)
    for k in range(EXPORT):
        scale = scale_full[exports[0, k]]
        hub_out[k] = scale * (scale * total[k])


def far_kernel(tiles, split, after, *refs):
    pieces = refs[:PIECES]
    (
        rows, cols, counts, exports, picks, places, lists, ghost_scale, scale_full, inner_sum, hub,
        total_out, buf, ghost, half, scaled, total, sem, ghost_sem,
    ) = refs[PIECES:]
    blocks = scale_full.shape[0]
    total[0:blocks] = inner_sum[...]
    total[blocks] = jnp.zeros_like(total[blocks])

    def tile_of(i):
        return lists[2 + tiles.shape[0] + i]

    def copies(i, slot):
        t = tile_of(i)
        q = cols[t] - blocks
        return (
            pltpu.make_async_copy(tiles.at[t], buf.at[slot], sem.at[slot]),
            GhostCopy(pieces, places[q] + picks[q], ghost.at[slot], ghost_sem.at[slot]),
        )

    def left_of(i, slot):
        q = cols[tile_of(i)] - blocks
        return halves(buf[slot] * ghost_scale[pl.ds(q, 1), :])

    def work(steps):
        add_tiles(steps, left_of, lambda i, slot: halves(ghost[slot]), lambda i: rows[tile_of(i)], total)

    stream(lists[1], copies, work)

    def next_block(r, carry):
        scale = scale_full[r]
        scaled[r] = halves(scale * (scale * total[r]))
        return carry

    lax.fori_loop(0, blocks, next_block, 0)
    for k in range(EXPORT):
        scaled[exports[0, k]] = halves(hub[k])
    total[...] = jnp.zeros_like(total)

    add_inner(split, half, sem, scaled, rows, cols, counts[0, 0], total)
    total_out[...] = total[0:blocks]


def last_kernel(split, *refs):
    pieces = refs[:PIECES]
    (
        rows, cols, counts, picks, places, scale_full, inner_sum,
        second, gram, half, ghost, total, both, sem, ghost_sem,
    ) = refs[PIECES:]
    blocks, side, width = scale_full.shape
    total[0:blocks] = inner_sum[...]
    total[blocks] = jnp.zeros_like(total[blocks])
    inner = counts[0, 0]

    group, tile = halves_group(split, half, sem, inner)

    def copies(i, slot):
        q = cols[inner + i] - blocks
        return (GhostCopy(pieces, places[q] + picks[q], ghost.at[slot], ghost_sem.at[slot]),)

    def work(steps):
        add_tiles(
            steps,
            tile,
            lambda i, slot: halves(ghost[slot]),
            lambda i: rows[inner + i],
            total,
        )

    stream(counts[0, 1] - inner, copies, work, group)

    both[...] = jnp.zeros_like(both)

    def finish(g, carry):
        pieces = []
        for u in range(4):
            r = g * 4 + u
            value = scale_full[r] * total[r]
            second[r] = value
            pieces.append(halves(value))
        tall = jnp.concatenate(pieces, axis=0)
        both[...] += lax.dot_general(tall, tall, (((0,), (0,)), ((), ())), preferred_element_type=F32)
        return carry

    lax.fori_loop(0, blocks // 4, finish, 0)
    gram[...] = (both[0:width, 0:width] + both[width:, width:]) + (both[0:width, width:] + both[width:, 0:width])


def thirds(x):
    high = x.astype(BF16).astype(F32)
    rest = x - high
    middle = rest.astype(BF16).astype(F32)
    return high, middle, rest - middle


def inverse_factor(a, b, size):
    groups = size // 8
    sub = lax.broadcasted_iota(jnp.int32, (8, size), 0)
    masks = [sub == i for i in range(8)]
    rows = []
    for p in range(groups):
        block, other = a[p], b[p]
        s = [
            [jnp.broadcast_to(block[i : i + 1, 8 * p + j : 8 * p + j + 1], (8, size)) for j in range(i + 1)]
            for i in range(8)
        ]
        block_rows = [jnp.broadcast_to(block[i : i + 1, :], (8, size)) for i in range(8)]
        other_rows = [jnp.broadcast_to(other[i : i + 1, :], (8, size)) for i in range(8)]
        low = [[None] * 8 for _ in range(8)]
        reciprocals = []
        for k in range(8):
            reciprocal = 1.0 / s[k][k]
            reciprocals.append(reciprocal)
            for i in range(k + 1, 8):
                low[i][k] = s[i][k] * reciprocal
            for i in range(k + 1, 8):
                for j in range(k + 1, i + 1):
                    s[i][j] = s[i][j] - low[i][k] * s[j][k]
        inv = [[None] * 8 for _ in range(8)]
        for i in range(8):
            for j in range(i):
                total = low[i][j]
                for k in range(j + 1, i):
                    total = total + low[i][k] * inv[k][j]
                inv[i][j] = -total
        pivots, roots = reciprocals[0], s[0][0]
        for i in range(1, 8):
            pivots = jnp.where(masks[i], reciprocals[i], pivots)
            roots = jnp.where(masks[i], s[i][i], roots)
        new_block, new_other = block, other
        for j in range(7):
            coefficient = jnp.zeros((8, size), F32)
            for i in range(j + 1, 8):
                coefficient = jnp.where(masks[i], inv[i][j], coefficient)
            new_block = new_block + coefficient * block_rows[j]
            new_other = new_other + coefficient * other_rows[j]
        rows.append(new_other * lax.rsqrt(roots))
        if p + 1 == groups:
            break
        left = thirds(new_block)
        right = thirds(jnp.concatenate([new_block * pivots, new_other * pivots], axis=1))
        tall = jnp.concatenate([x for x in left for _ in range(3)] + [jnp.zeros((8, size), F32)], axis=0)
        wide = jnp.concatenate(list(right) * 3 + [jnp.zeros((8, 2 * size), F32)], axis=0)
        update = lax.dot_general(
            tall.astype(BF16), wide.astype(BF16), (((0,), (0,)), ((), ())), preferred_element_type=F32
        )
        for i in range(p + 1, groups):
            a[i] = a[i] - update[8 * i : 8 * i + 8, :size]
            b[i] = b[i] - update[8 * i : 8 * i + 8, size:]
    return rows


def basis_kernel(gram, second, out, inverse, *, factor):
    size = gram.shape[0]
    groups = size // 8
    lane = lax.broadcasted_iota(jnp.int32, (8, size), 1)
    sub = lax.broadcasted_iota(jnp.int32, (8, size), 0)
    a = [gram[8 * g : 8 * g + 8, :] for g in range(groups)]
    b = [jnp.where(lane == sub + 8 * g, 1.0, 0.0).astype(F32) for g in range(groups)]
    for g, row in enumerate(inverse_factor(a, b, size)):
        inverse[8 * g : 8 * g + 8, :] = row * factor
    high, middle, low = (x.astype(BF16) for x in thirds(jnp.transpose(inverse[...])))
    main = jnp.concatenate([jnp.concatenate([high, middle], axis=1)] * 2, axis=0)
    rest = jnp.concatenate([low, high], axis=0)

    def some(r, carry):
        for u in range(4):
            left = [x.astype(BF16) for x in thirds(second[4 * r + u])]
            part = jnp.dot(jnp.concatenate(left[:2], axis=1), main, preferred_element_type=F32)
            small = jnp.dot(jnp.concatenate(left[::2], axis=1), rest, preferred_element_type=F32)
            out[4 * r + u] = part[:, :size] + (part[:, size:] + small)
        return carry

    lax.fori_loop(0, second.shape[0] // 4, some, 0)


def call(kernel, out_shape, in_specs, out_specs, scratch, flops, data):
    return pl.pallas_call(
        kernel,
        out_shape=out_shape,
        in_specs=in_specs,
        out_specs=out_specs,
        scratch_shapes=scratch,
        cost_estimate=pl.CostEstimate(flops=flops, bytes_accessed=data, transcendentals=0),
        compiler_params=pltpu.CompilerParams(vmem_limit_bytes=40 * 1024 * 1024),
    )


def shift_pairs(parts, stride, extent, step):
    pairs = []
    for device in range(parts):
        place = device // stride % extent
        pairs.append((device, device + ((place + step) % extent - place) * stride))
    return pairs


def gather_hubs(hub, early, late):
    parts = lax.axis_size("dom")

    def move(value, even, odd, step):
        pairs = [
            shift_pairs(parts, (even, odd)[device % 2], 4, step)[device] for device in range(parts)
        ]
        return lax.ppermute(value, "dom", pairs)

    def all_four(value, even, odd):
        return jnp.concatenate([value] + [move(value, even, odd, step) for step in (3, 2, 1)], axis=0)

    z, x, y = STRIDES
    plane = all_four(all_four(hub, z, z), x, y)
    following, preceding = move(plane, y, x, 3), move(plane, y, x, 1)
    half = plane.shape[0] // 2
    following, preceding, done = lax.optimization_barrier((following, preceding, early(plane)))
    opposite = (move(following[:half], y, x, 3), move(preceding[half:], y, x, 1))
    opposite, done = lax.optimization_barrier((opposite, late(done)))
    pieces = [plane, following, preceding, *opposite]
    partner = shift_pairs(parts, 1, 2, 1)
    return pieces + [lax.ppermute(piece, "dom", partner) for piece in pieces], done


def sum_over_devices(value, parts):
    value = value + lax.ppermute(value, "dom", shift_pairs(parts, 1, 2, 1))
    stride = 2
    while stride < parts:
        across, left, right = (
            lax.ppermute(value, "dom", shift_pairs(parts, stride, 4, step)) for step in (2, 1, 3)
        )
        value = (value + across) + (left + right)
        stride *= 4
    return value


def shards(block_vector, tile_values, tile_rows, tile_cols, tile_counts, export_rows, send_pick):
    parts = lax.axis_size("dom")
    slots, side, _ = tile_values.shape
    width = block_vector.shape[1]
    blocks = block_vector.shape[0] // side
    vec = block_vector.reshape(blocks, side, width)
    block, wide = (side, width), (side, 2 * width)
    every = jax.ShapeDtypeStruct((blocks,) + block, F32)
    sums = pltpu.VMEM((blocks + 1,) + block, F32)
    spread = pltpu.VMEM((blocks,) + wide, BF16)
    whole = pltpu.VMEM((SLOTS,) + block, F32)
    halved = pltpu.VMEM((SLOTS,) + wide, BF16)
    sems = pltpu.SemaphoreType.DMA((SLOTS,))
    tile_bytes = side * side * 4
    tile_flops = 8 * side * side * width

    own = call(
        hub_kernel,
        jax.ShapeDtypeStruct((EXPORT,) + block, F32),
        [ANY, SMEM],
        VMEM,
        [pltpu.SemaphoreType.DMA((EXPORT,))],
        0,
        2 * EXPORT * tile_bytes,
    )(vec, export_rows)

    def early(plane):
        return call(
            degree_kernel,
            (
                jax.ShapeDtypeStruct((slots,) + wide, BF16),
                jax.ShapeDtypeStruct((blocks, side), F32),
                every,
                jax.ShapeDtypeStruct((2 + 2 * slots,), jnp.int32),
                jax.ShapeDtypeStruct((parts,), jnp.int32),
            ),
            [ANY, ANY, SMEM, SMEM, SMEM, SMEM],
            (ANY, VMEM, VMEM, SMEM, SMEM),
            [whole, halved, sems, sems],
            slots * side * side * 4,
            2 * slots * tile_bytes,
        )(tile_values, plane, tile_rows, tile_counts, export_rows, lax.axis_index("dom").reshape(1))

    def late(found):
        split, scale_lane, scale_full, lists, places = found
        hub_scale = scale_lane.at[export_rows[0]].get(mode="promise_in_bounds")
        sent = jnp.where(send_pick[0][:, None] == 0, hub_scale[0], hub_scale[1])
        sent = jnp.concatenate(
            [sent, jnp.broadcast_to(send_pick[0][:, None], sent.shape).astype(F32)], axis=1
        )
        received = lax.all_to_all(sent, "dom", split_axis=0, concat_axis=0, tiled=True)
        inner_sum = call(
            inner_kernel,
            every,
            [ANY, VMEM, VMEM, SMEM, SMEM, SMEM],
            VMEM,
            [halved, spread, sums, sems],
            slots // 4 * tile_flops,
            slots // 4 * tile_bytes,
        )(split, vec, scale_full, tile_rows, tile_cols, tile_counts)
        return split, scale_full, lists, places, received, inner_sum

    offered, (split, scale_full, lists, places, received, inner_sum) = gather_hubs(own, early, late)
    ghost_scale = received[:, :side]
    picks = received[:, side].astype(jnp.int32)

    hub = call(
        near_kernel,
        jax.ShapeDtypeStruct((EXPORT,) + block, F32),
        [ANY] * (1 + PIECES) + [SMEM] * 6 + [VMEM] * 3,
        VMEM,
        [whole, whole, pltpu.VMEM((EXPORT + 1,) + block, F32), sems, sems],
        slots // 16 * tile_flops,
        slots // 8 * tile_bytes,
    )(
        tile_values, *offered, tile_rows, tile_cols, export_rows, picks, places, lists,
        ghost_scale, scale_full, inner_sum,
    )

    def far(plane):
        return call(
            far_kernel,
            every,
            [ANY] * (3 + PIECES) + [SMEM] * 7 + [VMEM] * 4,
            VMEM,
            [whole, whole, halved, spread, sums, sems, sems],
            slots // 2 * tile_flops,
            slots // 2 * tile_bytes,
        )(
            tile_values, split, plane, *offered,
            tile_rows, tile_cols, tile_counts, export_rows, picks, places, lists,
            ghost_scale, scale_full, inner_sum, hub,
        )

    offered_next, inner_next = gather_hubs(hub, far, lambda done: done)
    second, gram = call(
        last_kernel,
        (every, jax.ShapeDtypeStruct((width, width), F32)),
        [ANY] * (1 + PIECES) + [SMEM] * 5 + [VMEM] * 2,
        (VMEM, VMEM),
        [halved, whole, sums, pltpu.VMEM((2 * width, 2 * width), F32), sems, sems],
        slots // 2 * tile_flops,
        slots * tile_bytes,
    )(split, *offered_next, tile_rows, tile_cols, tile_counts, picks, places, scale_full, inner_next)
    basis = call(
        functools.partial(basis_kernel, factor=math.sqrt(blocks * side * parts)),
        every,
        [VMEM, VMEM],
        VMEM,
        [pltpu.VMEM((width, width), F32)],
        blocks * tile_flops,
        2 * blocks * tile_bytes,
    )(sum_over_devices(gram, parts), second)
    return basis.reshape(block_vector.shape)


def solution(mesh):
    in_specs = (
        P("dom", None),
        P("dom", None, None),
        P("dom"),
        P("dom"),
        P("dom", None),
        P("dom", None),
        P("dom", None),
    )
    out_specs = P("dom", None)
    return jax.shard_map(shards, mesh=mesh, in_specs=in_specs, out_specs=out_specs, check_vma=False)
```

```python
import functools
import math

import jax
import jax.numpy as jnp
from jax import lax
from jax.experimental import pallas as pl
from jax.experimental.pallas import tpu as pltpu
from jax.sharding import PartitionSpec as P

EXPORT = 2
N_CHIPS = 64
STRIDES = (2, 8, 32)
PIECES = 10
PLANE = 32
T_MAX = 320
OWN, NEAR, FAR = 8, 8 + T_MAX, 8 + 2 * T_MAX
SLOTS = 48
UNROLL = 8
F32 = jnp.float32
BF16 = jnp.bfloat16
VMEM = pl.BlockSpec(memory_space=pltpu.VMEM)
SMEM = pl.BlockSpec(memory_space=pltpu.SMEM)
ANY = pl.BlockSpec(memory_space=pl.ANY)


def halves(x):
    high = x.astype(BF16)
    low = (x - high.astype(F32)).astype(BF16)
    return jnp.concatenate([high, low], axis=1)


def product(left, right):
    both = jnp.dot(left, jnp.concatenate([right, right], axis=0), preferred_element_type=F32)
    width = both.shape[1] // 2
    return both[:, :width] + both[:, width:]


def stream(count, copies, work, group=None, ready=lambda: None):
    rounds = (count + UNROLL - 1) // UNROLL
    ahead = SLOTS // UNROLL - 1

    def of_round(r):
        first = r * UNROLL
        found = [] if group is None else [group(first, lax.rem(first, SLOTS))]
        for u in range(UNROLL):
            found.extend(copies(jnp.minimum(first + u, count - 1), lax.rem(first + u, SLOTS)))
        return found

    def start(r, carry):
        for copy in of_round(r):
            copy.start()
        return carry

    lax.fori_loop(0, jnp.minimum(ahead, rounds), start, 0)
    ready()

    def one_round(r, carry):
        @pl.when(r + ahead < rounds)
        def _():
            start(r + ahead, 0)

        for copy in of_round(r):
            copy.wait()
        first = r * UNROLL
        work(
            [
                (jnp.minimum(first + u, count - 1), lax.rem(first + u, SLOTS), first + u < count)
                for u in range(UNROLL)
            ]
        )
        return carry

    lax.fori_loop(0, rounds, one_round, 0)


def window(array, first):
    return jnp.minimum(first, array.shape[0] - UNROLL)


def piece_starts(pieces):
    starts = [0]
    for piece in pieces:
        starts.append(starts[-1] + piece.shape[0])
    return starts


class GhostCopy:
    def __init__(self, pieces, place, target, sem):
        self.pieces, self.place, self.target, self.sem = pieces, place, target, sem

    def start(self):
        starts = piece_starts(self.pieces)
        for piece, low, high in zip(self.pieces, starts[:-1], starts[1:]):

            @pl.when((self.place >= low) & (self.place < high))
            def _():
                pltpu.make_async_copy(piece.at[self.place - low], self.target, self.sem).start()

    def wait(self):
        pltpu.make_async_copy(self.pieces[0].at[0], self.target, self.sem).wait()


def all_pieces(pieces, store, sem):
    return [
        pltpu.make_async_copy(piece, store.at[pl.ds(low, piece.shape[0])], sem.at[k])
        for k, (piece, low) in enumerate(zip(pieces, piece_starts(pieces)))
    ]


def hub_kernel(vec, exports, out, sem):
    copies = [pltpu.make_async_copy(vec.at[exports[0, k]], out.at[k], sem.at[k]) for k in range(EXPORT)]
    for copy in copies:
        copy.start()
    for copy in copies:
        copy.wait()


def degree_kernel(
    tiles, after, rows, counts, exports, me,
    split_out, scale_lane, scale_full, lists, places,
    buf, half, sem, out_sem,
):
    blocks = scale_full.shape[0]
    inner, live = counts[0, 0], counts[0, 1]
    scale_full[...] = jnp.zeros_like(scale_full)

    def out_copy(i, slot):
        return pltpu.make_async_copy(half.at[slot], split_out.at[i], out_sem.at[slot])

    def copies(i, slot):
        return (pltpu.make_async_copy(tiles.at[i], buf.at[slot], sem.at[slot]),)

    def work(steps):
        for i, slot, alive in steps:

            @pl.when(alive)
            def _():
                @pl.when(i >= SLOTS)
                def _():
                    out_copy(0, slot).wait()

                value = buf[slot]
                half[slot] = halves(value)
                out_copy(i, slot).start()
                row = rows[i]
                scale_full[row] = scale_full[row] + jnp.abs(value)

    stream(live, copies, work)

    def scale_block(r, carry):
        total = scale_full[r]
        full = jnp.broadcast_to(lax.rsqrt(jnp.sum(total, axis=1, keepdims=True)), total.shape)
        scale_full[r] = full
        scale_lane[pl.ds(r, 1), :] = jnp.transpose(full)[0:1, :]
        return carry

    lax.fori_loop(0, blocks, scale_block, 0)

    first_row, second_row = exports[0, 0], exports[0, 1]

    def sort(i, carry):
        near, far, own = carry
        row = rows[i]
        is_near = (row == first_row) | (row == second_row)
        is_own = i < inner

        @pl.when(is_near & is_own)
        def _():
            lists[OWN + own] = i

        @pl.when(is_near & jnp.logical_not(is_own))
        def _():
            lists[NEAR + near] = i

        @pl.when(jnp.logical_not(is_near | is_own))
        def _():
            lists[FAR + far] = i

        near_step, own_step = is_near.astype(jnp.int32), is_own.astype(jnp.int32)
        ghost_step = 1 - own_step
        return near + near_step * ghost_step, far + (1 - near_step) * ghost_step, own + near_step * own_step

    mine = me[0]

    def place(q, carry):
        ahead = [lax.rem(q // stride - mine // stride + 4 * N_CHIPS, 4) for stride in STRIDES]
        odd = lax.rem(q, 2)
        second = jnp.where(odd == 0, ahead[1], ahead[2])
        final = jnp.where(odd == 0, ahead[2], ahead[1])
        piece = jnp.where(final == 3, 2, jnp.where(final == 2, 3, final))
        piece = piece + jnp.where(odd == lax.rem(mine, 2), 0, 4)
        places[q] = piece * PLANE + (second * 4 + ahead[0]) * EXPORT
        return carry

    lax.fori_loop(0, places.shape[0], place, 0)

    near, far, own = lax.fori_loop(0, live, sort, (jnp.int32(0), jnp.int32(0), jnp.int32(0)))
    lists[0] = near
    lists[1] = far
    lists[2] = own

    def drain(i, carry):
        out_copy(0, lax.rem(i, SLOTS)).wait()
        return carry

    lax.fori_loop(jnp.maximum(live - SLOTS, 0), live, drain, 0)


def add_tiles(steps, left_of, right_of, row_of, total):
    parts = [product(left_of(i, slot), right_of(i, slot)) for i, slot, _ in steps]
    for (i, _, alive), part in zip(steps, parts):
        row = jnp.where(alive, row_of(i), total.shape[0] - 1)
        total[row] = total[row] + part


def halves_group(split, half, sem, begin):
    def group(first, slot):
        return pltpu.make_async_copy(
            split.at[pl.ds(window(split, begin + first), UNROLL)], half.at[pl.ds(slot, UNROLL)], sem.at[slot]
        )

    def tile(i, slot):
        first = i // UNROLL * UNROLL
        place = begin + i - window(split, begin + first)
        return half[slot // UNROLL * UNROLL + place]

    return group, tile


def add_inner(split, half, sem, scaled, rows, cols, count, total, row_of):
    group, tile = halves_group(split, half, sem, 0)

    def work(steps):
        add_tiles(steps, tile, lambda i, slot: scaled[cols[i]], row_of, total)

    stream(count, lambda i, slot: (), work, group)


def near_kernel(tiles, *refs):
    pieces = refs[:PIECES]
    (
        rows, cols, exports, picks, places, lists, ghost_scale, scale_lane, scale_full, vec,
        hub_out, buf, ghost, total, sem, ghost_sem,
    ) = refs[PIECES:]
    blocks = scale_full.shape[0]
    total[...] = jnp.zeros_like(total)

    def run(base, count, extra, scale_of, right_of):
        def copies(i, slot):
            t = lists[base + i]
            return [pltpu.make_async_copy(tiles.at[t], buf.at[slot], sem.at[slot])] + extra(t, slot)

        def work(steps):
            add_tiles(
                steps,
                lambda i, slot: halves(buf[slot] * scale_of(cols[lists[base + i]])),
                lambda i, slot: halves(right_of(cols[lists[base + i]], slot)),
                lambda i: jnp.where(rows[lists[base + i]] == exports[0, 0], 0, 1),
                total,
            )

        stream(count, copies, work)

    def ghost_copy(t, slot):
        q = cols[t] - blocks
        return [GhostCopy(pieces, places[q] + picks[q], ghost.at[slot], ghost_sem.at[slot])]

    run(OWN, lists[2], lambda t, slot: [], lambda c: scale_lane[pl.ds(c, 1), :], lambda c, slot: vec[c])
    run(NEAR, lists[0], ghost_copy, lambda c: ghost_scale[pl.ds(c - blocks, 1), :], lambda c, slot: ghost[slot])
    for k in range(EXPORT):
        scale = scale_full[exports[0, k]]
        hub_out[k] = scale * (scale * total[k])


def far_kernel(tiles, split, after, *refs):
    pieces = refs[:PIECES]
    (
        rows, cols, counts, exports, picks, places, lists, ghost_scale, scale_full, vec, hub,
        scaled_out, buf, half, store, scaled, total, sem, half_sem, store_sem,
    ) = refs[PIECES:]
    blocks = scale_full.shape[0]
    bulk = all_pieces(pieces, store, store_sem)
    for copy in bulk:
        copy.start()
    total[...] = jnp.zeros_like(total)

    def scale_block(r, carry):
        scaled[r] = halves(scale_full[r] * vec[r])
        return carry

    lax.fori_loop(0, blocks, scale_block, 0)

    def other_row(i):
        row = rows[i]
        return jnp.where((row == exports[0, 0]) | (row == exports[0, 1]), blocks, row)

    add_inner(split, half, half_sem, scaled, rows, cols, counts[0, 0], total, other_row)

    def ghost_of(i):
        return cols[lists[FAR + i]] - blocks

    def copies(i, slot):
        return [pltpu.make_async_copy(tiles.at[lists[FAR + i]], buf.at[slot], sem.at[slot])]

    def right_of(i, slot):
        q = ghost_of(i)
        return halves(store[places[q] + picks[q]])

    def work(steps):
        add_tiles(
            steps,
            lambda i, slot: halves(buf[slot] * ghost_scale[pl.ds(ghost_of(i), 1), :]),
            right_of,
            lambda i: rows[lists[FAR + i]],
            total,
        )

    def ready():
        for copy in bulk:
            copy.wait()

    stream(lists[1], copies, work, ready=ready)

    def next_block(r, carry):
        scale = scale_full[r]
        scaled_out[r] = halves(scale * (scale * total[r]))
        return carry

    lax.fori_loop(0, blocks, next_block, 0)
    for k in range(EXPORT):
        scaled_out[exports[0, k]] = halves(hub[k])


def inner_kernel(split, scaled, rows, cols, counts, total_out, half, total, sem):
    total[...] = jnp.zeros_like(total)
    add_inner(split, half, sem, scaled, rows, cols, counts[0, 0], total, lambda i: rows[i])
    total_out[...] = total[0 : total_out.shape[0]]


def last_kernel(split, *refs):
    pieces = refs[:PIECES]
    (
        rows, cols, counts, picks, places, scale_full, inner_sum,
        second, gram, half, store, total, both, sem, store_sem,
    ) = refs[PIECES:]
    blocks, side, width = scale_full.shape
    bulk = all_pieces(pieces, store, store_sem)
    for copy in bulk:
        copy.start()
    total[0:blocks] = inner_sum[...]
    total[blocks] = jnp.zeros_like(total[blocks])
    both[...] = jnp.zeros_like(both)
    inner = counts[0, 0]
    group, tile = halves_group(split, half, sem, inner)

    def right_of(i, slot):
        q = cols[inner + i] - blocks
        return halves(store[places[q] + picks[q]])

    def work(steps):
        add_tiles(steps, tile, right_of, lambda i: rows[inner + i], total)

    def ready():
        for copy in bulk:
            copy.wait()

    stream(counts[0, 1] - inner, lambda i, slot: (), work, group, ready)

    def finish(g, carry):
        pieces = []
        for u in range(4):
            r = g * 4 + u
            value = scale_full[r] * total[r]
            second[r] = value
            pieces.append(halves(value))
        tall = jnp.concatenate(pieces, axis=0)
        both[...] += lax.dot_general(tall, tall, (((0,), (0,)), ((), ())), preferred_element_type=F32)
        return carry

    lax.fori_loop(0, blocks // 4, finish, 0)
    gram[...] = (both[0:width, 0:width] + both[width:, width:]) + (both[0:width, width:] + both[width:, 0:width])


def thirds(x):
    high = x.astype(BF16).astype(F32)
    rest = x - high
    middle = rest.astype(BF16).astype(F32)
    return high, middle, rest - middle


def inverse_factor(a, b, size):
    groups = size // 8
    sub = lax.broadcasted_iota(jnp.int32, (8, size), 0)
    masks = [sub == i for i in range(8)]
    rows = []
    for p in range(groups):
        block, other = a[p], b[p]
        s = [
            [jnp.broadcast_to(block[i : i + 1, 8 * p + j : 8 * p + j + 1], (8, size)) for j in range(i + 1)]
            for i in range(8)
        ]
        block_rows = [jnp.broadcast_to(block[i : i + 1, :], (8, size)) for i in range(8)]
        other_rows = [jnp.broadcast_to(other[i : i + 1, :], (8, size)) for i in range(8)]
        low = [[None] * 8 for _ in range(8)]
        reciprocals = []
        for k in range(8):
            reciprocal = 1.0 / s[k][k]
            reciprocals.append(reciprocal)
            for i in range(k + 1, 8):
                low[i][k] = s[i][k] * reciprocal
            for i in range(k + 1, 8):
                for j in range(k + 1, i + 1):
                    s[i][j] = s[i][j] - low[i][k] * s[j][k]
        inv = [[None] * 8 for _ in range(8)]
        for i in range(8):
            for j in range(i):
                total = low[i][j]
                for k in range(j + 1, i):
                    total = total + low[i][k] * inv[k][j]
                inv[i][j] = -total
        pivots, roots = reciprocals[0], s[0][0]
        for i in range(1, 8):
            pivots = jnp.where(masks[i], reciprocals[i], pivots)
            roots = jnp.where(masks[i], s[i][i], roots)
        new_block, new_other = block, other
        for j in range(7):
            coefficient = jnp.zeros((8, size), F32)
            for i in range(j + 1, 8):
                coefficient = jnp.where(masks[i], inv[i][j], coefficient)
            new_block = new_block + coefficient * block_rows[j]
            new_other = new_other + coefficient * other_rows[j]
        rows.append(new_other * lax.rsqrt(roots))
        if p + 1 == groups:
            break
        left = thirds(new_block)
        right = thirds(jnp.concatenate([new_block * pivots, new_other * pivots], axis=1))
        tall = jnp.concatenate([x for x in left for _ in range(3)] + [jnp.zeros((8, size), F32)], axis=0)
        wide = jnp.concatenate(list(right) * 3 + [jnp.zeros((8, 2 * size), F32)], axis=0)
        update = lax.dot_general(
            tall.astype(BF16), wide.astype(BF16), (((0,), (0,)), ((), ())), preferred_element_type=F32
        )
        for i in range(p + 1, groups):
            a[i] = a[i] - update[8 * i : 8 * i + 8, :size]
            b[i] = b[i] - update[8 * i : 8 * i + 8, size:]
    return rows


def basis_kernel(gram, second, out, inverse, *, factor):
    size = gram.shape[0]
    groups = size // 8
    lane = lax.broadcasted_iota(jnp.int32, (8, size), 1)
    sub = lax.broadcasted_iota(jnp.int32, (8, size), 0)
    a = [gram[8 * g : 8 * g + 8, :] for g in range(groups)]
    b = [jnp.where(lane == sub + 8 * g, 1.0, 0.0).astype(F32) for g in range(groups)]
    for g, row in enumerate(inverse_factor(a, b, size)):
        inverse[8 * g : 8 * g + 8, :] = row * factor
    high, middle, low = (x.astype(BF16) for x in thirds(jnp.transpose(inverse[...])))
    main = jnp.concatenate([jnp.concatenate([high, middle], axis=1)] * 2, axis=0)
    rest = jnp.concatenate([low, high], axis=0)

    def some(r, carry):
        for u in range(4):
            left = [x.astype(BF16) for x in thirds(second[4 * r + u])]
            part = jnp.dot(jnp.concatenate(left[:2], axis=1), main, preferred_element_type=F32)
            small = jnp.dot(jnp.concatenate(left[::2], axis=1), rest, preferred_element_type=F32)
            out[4 * r + u] = part[:, :size] + (part[:, size:] + small)
        return carry

    lax.fori_loop(0, second.shape[0] // 4, some, 0)


def call(kernel, out_shape, in_specs, out_specs, scratch, flops, data, vmem=16):
    return pl.pallas_call(
        kernel,
        out_shape=out_shape,
        in_specs=in_specs,
        out_specs=out_specs,
        scratch_shapes=scratch,
        cost_estimate=pl.CostEstimate(flops=flops, bytes_accessed=data, transcendentals=0),
        compiler_params=pltpu.CompilerParams(vmem_limit_bytes=vmem * 1024 * 1024),
    )


def shift_pairs(parts, stride, extent, step):
    pairs = []
    for device in range(parts):
        place = device // stride % extent
        pairs.append((device, device + ((place + step) % extent - place) * stride))
    return pairs


def gather_hubs(hub, early, late):
    parts = lax.axis_size("dom")

    def move(value, even, odd, step):
        pairs = [
            shift_pairs(parts, (even, odd)[device % 2], 4, step)[device] for device in range(parts)
        ]
        return lax.ppermute(value, "dom", pairs)

    def all_four(value, even, odd):
        return jnp.concatenate([value] + [move(value, even, odd, step) for step in (3, 2, 1)], axis=0)

    z, x, y = STRIDES
    plane = all_four(all_four(hub, z, z), x, y)
    following, preceding = move(plane, y, x, 3), move(plane, y, x, 1)
    half = plane.shape[0] // 2
    following, preceding, done = lax.optimization_barrier((following, preceding, early(plane)))
    opposite = (move(following[:half], y, x, 3), move(preceding[half:], y, x, 1))
    opposite, done = lax.optimization_barrier((opposite, late(done)))
    pieces = [plane, following, preceding, *opposite]
    partner = shift_pairs(parts, 1, 2, 1)
    return pieces + [lax.ppermute(piece, "dom", partner) for piece in pieces], done


def sum_over_devices(value, parts):
    value = value + lax.ppermute(value, "dom", shift_pairs(parts, 1, 2, 1))
    stride = 2
    while stride < parts:
        across, left, right = (
            lax.ppermute(value, "dom", shift_pairs(parts, stride, 4, step)) for step in (2, 1, 3)
        )
        value = (value + across) + (left + right)
        stride *= 4
    return value


def shards(block_vector, tile_values, tile_rows, tile_cols, tile_counts, export_rows, send_pick):
    parts = lax.axis_size("dom")
    slots, side, _ = tile_values.shape
    width = block_vector.shape[1]
    blocks = block_vector.shape[0] // side
    vec = block_vector.reshape(blocks, side, width)
    block, wide = (side, width), (side, 2 * width)
    every = jax.ShapeDtypeStruct((blocks,) + block, F32)
    sums = pltpu.VMEM((blocks + 1,) + block, F32)
    spread = pltpu.VMEM((blocks,) + wide, BF16)
    whole = pltpu.VMEM((SLOTS,) + block, F32)
    halved = pltpu.VMEM((SLOTS,) + wide, BF16)
    sems = pltpu.SemaphoreType.DMA((SLOTS,))
    tile_bytes = side * side * 4
    tile_flops = 8 * side * side * width

    own = call(
        hub_kernel,
        jax.ShapeDtypeStruct((EXPORT,) + block, F32),
        [ANY, SMEM],
        VMEM,
        [pltpu.SemaphoreType.DMA((EXPORT,))],
        0,
        2 * EXPORT * tile_bytes,
    )(vec, export_rows)

    def early(plane):
        return call(
            degree_kernel,
            (
                jax.ShapeDtypeStruct((slots,) + wide, BF16),
                jax.ShapeDtypeStruct((blocks, side), F32),
                every,
                jax.ShapeDtypeStruct((FAR + slots,), jnp.int32),
                jax.ShapeDtypeStruct((parts,), jnp.int32),
            ),
            [ANY, ANY, SMEM, SMEM, SMEM, SMEM],
            (ANY, VMEM, VMEM, SMEM, SMEM),
            [whole, halved, sems, sems],
            slots * side * side * 4,
            2 * slots * tile_bytes,
        )(tile_values, plane, tile_rows, tile_counts, export_rows, lax.axis_index("dom").reshape(1))

    def late(found):
        split, scale_lane, scale_full, lists, places = found
        hub_scale = scale_lane.at[export_rows[0]].get(mode="promise_in_bounds")
        sent = jnp.where(send_pick[0][:, None] == 0, hub_scale[0], hub_scale[1])
        sent = jnp.concatenate(
            [sent, jnp.broadcast_to(send_pick[0][:, None], sent.shape).astype(F32)], axis=1
        )
        received = lax.all_to_all(sent, "dom", split_axis=0, concat_axis=0, tiled=True)
        return split, scale_lane, scale_full, lists, places, received

    offered, (split, scale_lane, scale_full, lists, places, received) = gather_hubs(own, early, late)
    ghost_scale = received[:, :side]
    picks = received[:, side].astype(jnp.int32)

    hub = call(
        near_kernel,
        jax.ShapeDtypeStruct((EXPORT,) + block, F32),
        [ANY] * (1 + PIECES) + [SMEM] * 6 + [VMEM] * 4,
        VMEM,
        [whole, whole, pltpu.VMEM((EXPORT + 1,) + block, F32), sems, sems],
        slots // 16 * tile_flops,
        slots // 8 * tile_bytes,
    )(
        tile_values, *offered, tile_rows, tile_cols, export_rows, picks, places, lists,
        ghost_scale, scale_lane, scale_full, vec,
    )
    store = pltpu.VMEM((EXPORT * parts,) + block, F32)
    store_sems = pltpu.SemaphoreType.DMA((PIECES,))

    def far(plane):
        return call(
            far_kernel,
            jax.ShapeDtypeStruct((blocks,) + wide, BF16),
            [ANY] * (3 + PIECES) + [SMEM] * 7 + [VMEM] * 4,
            VMEM,
            [whole, halved, store, spread, sums, sems, sems, store_sems],
            slots // 2 * tile_flops,
            slots // 2 * tile_bytes,
            40,
        )(
            tile_values, split, plane, *offered,
            tile_rows, tile_cols, tile_counts, export_rows, picks, places, lists,
            ghost_scale, scale_full, vec, hub,
        )

    def inner(scaled):
        return call(
            inner_kernel,
            every,
            [ANY, VMEM, SMEM, SMEM, SMEM],
            VMEM,
            [halved, sums, sems],
            slots // 4 * tile_flops,
            slots // 4 * tile_bytes,
        )(split, scaled, tile_rows, tile_cols, tile_counts)

    offered_next, inner_next = gather_hubs(hub, far, inner)
    second, gram = call(
        last_kernel,
        (every, jax.ShapeDtypeStruct((width, width), F32)),
        [ANY] * (1 + PIECES) + [SMEM] * 5 + [VMEM] * 2,
        (VMEM, VMEM),
        [halved, store, sums, pltpu.VMEM((2 * width, 2 * width), F32), sems, store_sems],
        slots // 2 * tile_flops,
        slots * tile_bytes,
        32,
    )(split, *offered_next, tile_rows, tile_cols, tile_counts, picks, places, scale_full, inner_next)
    basis = call(
        functools.partial(basis_kernel, factor=math.sqrt(blocks * side * parts)),
        every,
        [VMEM, VMEM],
        VMEM,
        [pltpu.VMEM((width, width), F32)],
        blocks * tile_flops,
        2 * blocks * tile_bytes,
    )(sum_over_devices(gram, parts), second)
    return basis.reshape(block_vector.shape)


def solution(mesh):
    in_specs = (
        P("dom", None),
        P("dom", None, None),
        P("dom"),
        P("dom"),
        P("dom", None),
        P("dom", None),
        P("dom", None),
    )
    out_specs = P("dom", None)
    return jax.shard_map(shards, mesh=mesh, in_specs=in_specs, out_specs=out_specs, check_vma=False)
```

```python
import functools
import math

import jax
import jax.numpy as jnp
from jax import lax
from jax.experimental import pallas as pl
from jax.experimental.pallas import tpu as pltpu
from jax.sharding import PartitionSpec as P

EXPORT = 2
N_CHIPS = 64
STRIDES = (2, 8, 32)
PIECES = 14
PLANE = 32
T_MAX = 320
NEAR, FAR = 8, 8 + T_MAX
SLOTS = 48
UNROLL = 8
F32 = jnp.float32
BF16 = jnp.bfloat16
VMEM = pl.BlockSpec(memory_space=pltpu.VMEM)
SMEM = pl.BlockSpec(memory_space=pltpu.SMEM)
ANY = pl.BlockSpec(memory_space=pltpu.HBM)


def halves(x):
    high = x.astype(BF16)
    low = (x - high.astype(F32)).astype(BF16)
    return jnp.concatenate([high, low], axis=1)


def product(left, right):
    both = jnp.dot(left, jnp.concatenate([right, right], axis=0), preferred_element_type=F32)
    width = both.shape[1] // 2
    return both[:, :width] + both[:, width:]


def stream(count, copies, work, group=None, ready=lambda: None):
    rounds = (count + UNROLL - 1) // UNROLL
    ahead = SLOTS // UNROLL - 1

    def of_round(r):
        first = r * UNROLL
        found = [] if group is None else [group(first, lax.rem(first, SLOTS))]
        for u in range(UNROLL):
            found.extend(copies(jnp.minimum(first + u, count - 1), lax.rem(first + u, SLOTS)))
        return found

    def start(r, carry):
        for copy in of_round(r):
            copy.start()
        return carry

    lax.fori_loop(0, jnp.minimum(ahead, rounds), start, 0)
    ready()

    def one_round(r, carry):
        @pl.when(r + ahead < rounds)
        def _():
            start(r + ahead, 0)

        for copy in of_round(r):
            copy.wait()
        first = r * UNROLL
        work(
            [
                (jnp.minimum(first + u, count - 1), lax.rem(first + u, SLOTS), first + u < count)
                for u in range(UNROLL)
            ]
        )
        return carry

    lax.fori_loop(0, rounds, one_round, 0)


def window(array, first):
    return jnp.minimum(first, array.shape[0] - UNROLL)


def piece_starts(pieces):
    starts = [0]
    for piece in pieces:
        starts.append(starts[-1] + piece.shape[0])
    return starts


class GhostCopy:
    def __init__(self, pieces, place, target, sem):
        self.pieces, self.place, self.target, self.sem = pieces, place, target, sem

    def start(self):
        starts = piece_starts(self.pieces)
        for piece, low, high in zip(self.pieces, starts[:-1], starts[1:]):

            @pl.when((self.place >= low) & (self.place < high))
            def _():
                pltpu.make_async_copy(piece.at[self.place - low], self.target, self.sem).start()

    def wait(self):
        pltpu.make_async_copy(self.pieces[0].at[0], self.target, self.sem).wait()


def all_pieces(pieces, store, sem):
    return [
        pltpu.make_async_copy(piece, store.at[pl.ds(low, piece.shape[0])], sem.at[k])
        for k, (piece, low) in enumerate(zip(pieces, piece_starts(pieces)))
    ]


def hub_kernel(vec, exports, out, sem):
    copies = [pltpu.make_async_copy(vec.at[exports[0, k]], out.at[k], sem.at[k]) for k in range(EXPORT)]
    for copy in copies:
        copy.start()
    for copy in copies:
        copy.wait()


def degree_kernel(
    tiles, after, rows, counts, exports, me,
    split_out, scale_lane, scale_full, lists, places,
    buf, half, sem, out_sem,
):
    blocks = scale_full.shape[0]
    inner, live = counts[0, 0], counts[0, 1]
    scale_full[...] = jnp.zeros_like(scale_full)

    rounds = (live + UNROLL - 1) // UNROLL
    depth = SLOTS // UNROLL

    def slots_of(r):
        return pl.ds(lax.rem(r, depth) * UNROLL, UNROLL)

    def in_copy(r):
        return pltpu.make_async_copy(tiles.at[pl.ds(r * UNROLL, UNROLL)], buf.at[slots_of(r)], sem.at[lax.rem(r, depth)])

    def out_copy(r):
        return pltpu.make_async_copy(
            half.at[slots_of(r)], split_out.at[pl.ds(r * UNROLL, UNROLL)], out_sem.at[lax.rem(r, depth)]
        )

    def prime(r, carry):
        in_copy(r).start()
        return carry

    lax.fori_loop(0, jnp.minimum(depth - 1, rounds), prime, 0)

    def one_round(r, carry):
        @pl.when(r + depth - 1 < rounds)
        def _():
            in_copy(r + depth - 1).start()

        @pl.when(r >= depth)
        def _():
            out_copy(r - depth).wait()

        in_copy(r).wait()
        base = lax.rem(r, depth) * UNROLL
        for u in range(UNROLL):
            half[base + u] = halves(buf[base + u])
        for u in range(UNROLL):
            i = r * UNROLL + u
            row = rows[i]
            scale_full[row] = scale_full[row] + jnp.where(i < live, jnp.abs(buf[base + u]), 0.0)
        out_copy(r).start()
        return carry

    lax.fori_loop(0, rounds, one_round, 0)

    def scale_block(r, carry):
        total = scale_full[r]
        full = jnp.broadcast_to(lax.rsqrt(jnp.sum(total, axis=1, keepdims=True)), total.shape)
        scale_full[r] = full
        scale_lane[pl.ds(r, 1), :] = jnp.transpose(full)[0:1, :]
        return carry

    lax.fori_loop(0, blocks, scale_block, 0)

    first_row, second_row = exports[0, 0], exports[0, 1]

    def sort(i, carry):
        near, far = carry
        row = rows[i]
        is_near = (row == first_row) | (row == second_row)
        is_far = jnp.logical_not(is_near) & (i >= inner)

        @pl.when(is_near)
        def _():
            lists[NEAR + near] = i

        @pl.when(is_far)
        def _():
            lists[FAR + far] = i

        return near + is_near.astype(jnp.int32), far + is_far.astype(jnp.int32)

    mine = me[0]

    def place(q, carry):
        ahead = [lax.rem(q // stride - mine // stride + 4 * N_CHIPS, 4) for stride in STRIDES]
        odd = lax.rem(q, 2)
        second = jnp.where(odd == 0, ahead[1], ahead[2])
        final = jnp.where(odd == 0, ahead[2], ahead[1])
        piece = jnp.where(final == 3, 2, jnp.where(final == 2, 3, final))
        piece = piece + jnp.where(odd == lax.rem(mine, 2), 0, 4)
        places[q] = piece * PLANE + (second * 4 + ahead[0]) * EXPORT
        return carry

    lax.fori_loop(0, places.shape[0], place, 0)

    near, far = lax.fori_loop(0, live, sort, (jnp.int32(0), jnp.int32(0)))
    lists[0] = near
    lists[1] = far

    def drain(r, carry):
        out_copy(r).wait()
        return carry

    lax.fori_loop(jnp.maximum(rounds - depth, 0), rounds, drain, 0)


def add_tiles(steps, left_of, right_of, row_of, total):
    parts = [product(left_of(i, slot), right_of(i, slot)) for i, slot, _ in steps]
    for (i, _, alive), part in zip(steps, parts):
        row = jnp.where(alive, row_of(i), total.shape[0] - 1)
        total[row] = total[row] + part


def halves_group(split, half, sem, begin):
    def group(first, slot):
        return pltpu.make_async_copy(
            split.at[pl.ds(window(split, begin + first), UNROLL)], half.at[pl.ds(slot, UNROLL)], sem.at[slot]
        )

    def tile(i, slot):
        first = i // UNROLL * UNROLL
        place = begin + i - window(split, begin + first)
        return half[slot // UNROLL * UNROLL + place]

    return group, tile


def add_inner(split, half, sem, scaled, rows, cols, count, total, row_of):
    group, tile = halves_group(split, half, sem, 0)

    def work(steps):
        add_tiles(steps, tile, lambda i, slot: scaled[cols[i]], row_of, total)

    stream(count, lambda i, slot: (), work, group)


def near_kernel(tiles, vec, *refs):
    pieces = refs[:PIECES]
    (
        rows, cols, exports, picks, places, lists, scales, scale_full,
        hub_out, buf, source, total, sem, source_sem,
    ) = refs[PIECES:]
    blocks = scale_full.shape[0]
    sources = pieces + (vec,)
    ghosts = piece_starts(pieces)[-1]
    total[...] = jnp.zeros_like(total)

    def copies(i, slot):
        t = lists[NEAR + i]
        col = cols[t]
        q = jnp.maximum(col - blocks, 0)
        place = jnp.where(col < blocks, ghosts + col, places[q] + picks[q])
        return (
            pltpu.make_async_copy(tiles.at[t], buf.at[slot], sem.at[slot]),
            GhostCopy(sources, place, source.at[slot], source_sem.at[slot]),
        )

    def work(steps):
        add_tiles(
            steps,
            lambda i, slot: halves(buf[slot] * scales[pl.ds(cols[lists[NEAR + i]], 1), :]),
            lambda i, slot: halves(source[slot]),
            lambda i: jnp.where(rows[lists[NEAR + i]] == exports[0, 0], 0, 1),
            total,
        )

    stream(lists[0], copies, work)
    for k in range(EXPORT):
        scale = scale_full[exports[0, k]]
        hub_out[k] = scale * (scale * total[k])


def far_kernel(tiles, split, after, *refs):
    pieces = refs[:PIECES]
    (
        rows, cols, counts, exports, picks, places, lists, scales, scale_full, vec, hub,
        scaled_out, buf, half, store, scaled, total, sem, half_sem, store_sem,
    ) = refs[PIECES:]
    blocks = scale_full.shape[0]
    bulk = all_pieces(pieces, store, store_sem)
    for copy in bulk:
        copy.start()
    total[...] = jnp.zeros_like(total)

    def scale_block(r, carry):
        scaled[r] = halves(scale_full[r] * vec[r])
        return carry

    lax.fori_loop(0, blocks, scale_block, 0)

    def other_row(i):
        row = rows[i]
        return jnp.where((row == exports[0, 0]) | (row == exports[0, 1]), blocks, row)

    add_inner(split, half, half_sem, scaled, rows, cols, counts[0, 0], total, other_row)

    def ghost_of(i):
        return cols[lists[FAR + i]] - blocks

    def copies(i, slot):
        return [pltpu.make_async_copy(tiles.at[lists[FAR + i]], buf.at[slot], sem.at[slot])]

    def right_of(i, slot):
        q = ghost_of(i)
        return halves(store[places[q] + picks[q]])

    def work(steps):
        add_tiles(
            steps,
            lambda i, slot: halves(buf[slot] * scales[pl.ds(blocks + ghost_of(i), 1), :]),
            right_of,
            lambda i: rows[lists[FAR + i]],
            total,
        )

    def ready():
        for copy in bulk:
            copy.wait()

    stream(lists[1], copies, work, ready=ready)

    def next_block(r, carry):
        scale = scale_full[r]
        scaled_out[r] = halves(scale * (scale * total[r]))
        return carry

    lax.fori_loop(0, blocks, next_block, 0)
    for k in range(EXPORT):
        scaled_out[exports[0, k]] = halves(hub[k])


def inner_kernel(split, scaled, rows, cols, counts, total_out, half, total, sem):
    total[...] = jnp.zeros_like(total)
    add_inner(split, half, sem, scaled, rows, cols, counts[0, 0], total, lambda i: rows[i])
    total_out[...] = total[0 : total_out.shape[0]]


def last_kernel(split, *refs):
    pieces = refs[:PIECES]
    (
        rows, cols, counts, picks, places, scale_full, inner_sum,
        second, gram, half, store, total, both, sem, store_sem,
    ) = refs[PIECES:]
    blocks, side, width = scale_full.shape
    bulk = all_pieces(pieces, store, store_sem)
    for copy in bulk:
        copy.start()
    total[0:blocks] = inner_sum[...]
    total[blocks] = jnp.zeros_like(total[blocks])
    both[...] = jnp.zeros_like(both)
    inner = counts[0, 0]
    group, tile = halves_group(split, half, sem, inner)

    def right_of(i, slot):
        q = cols[inner + i] - blocks
        return halves(store[places[q] + picks[q]])

    def work(steps):
        add_tiles(steps, tile, right_of, lambda i: rows[inner + i], total)

    def ready():
        for copy in bulk:
            copy.wait()

    stream(counts[0, 1] - inner, lambda i, slot: (), work, group, ready)

    def finish(g, carry):
        pieces = []
        for u in range(4):
            r = g * 4 + u
            value = scale_full[r] * total[r]
            second[r] = value
            pieces.append(halves(value))
        tall = jnp.concatenate(pieces, axis=0)
        both[...] += lax.dot_general(tall, tall, (((0,), (0,)), ((), ())), preferred_element_type=F32)
        return carry

    lax.fori_loop(0, blocks // 4, finish, 0)
    gram[...] = (both[0:width, 0:width] + both[width:, width:]) + (both[0:width, width:] + both[width:, 0:width])


def thirds(x):
    high = x.astype(BF16).astype(F32)
    rest = x - high
    middle = rest.astype(BF16).astype(F32)
    return high, middle, rest - middle


def inverse_factor(a, b, size):
    groups = size // 8
    sub = lax.broadcasted_iota(jnp.int32, (8, size), 0)
    masks = [sub == i for i in range(8)]
    rows = []
    for p in range(groups):
        block, other = a[p], b[p]
        s = [
            [jnp.broadcast_to(block[i : i + 1, 8 * p + j : 8 * p + j + 1], (8, size)) for j in range(i + 1)]
            for i in range(8)
        ]
        block_rows = [jnp.broadcast_to(block[i : i + 1, :], (8, size)) for i in range(8)]
        other_rows = [jnp.broadcast_to(other[i : i + 1, :], (8, size)) for i in range(8)]
        low = [[None] * 8 for _ in range(8)]
        reciprocals = []
        for k in range(8):
            reciprocal = 1.0 / s[k][k]
            reciprocals.append(reciprocal)
            for i in range(k + 1, 8):
                low[i][k] = s[i][k] * reciprocal
            for i in range(k + 1, 8):
                for j in range(k + 1, i + 1):
                    s[i][j] = s[i][j] - low[i][k] * s[j][k]
        inv = [[None] * 8 for _ in range(8)]
        for i in range(8):
            for j in range(i):
                total = low[i][j]
                for k in range(j + 1, i):
                    total = total + low[i][k] * inv[k][j]
                inv[i][j] = -total
        pivots, roots = reciprocals[0], s[0][0]
        for i in range(1, 8):
            pivots = jnp.where(masks[i], reciprocals[i], pivots)
            roots = jnp.where(masks[i], s[i][i], roots)
        new_block, new_other = block, other
        for j in range(7):
            coefficient = jnp.zeros((8, size), F32)
            for i in range(j + 1, 8):
                coefficient = jnp.where(masks[i], inv[i][j], coefficient)
            new_block = new_block + coefficient * block_rows[j]
            new_other = new_other + coefficient * other_rows[j]
        rows.append(new_other * lax.rsqrt(roots))
        if p + 1 == groups:
            break
        left = thirds(new_block)
        right = thirds(jnp.concatenate([new_block * pivots, new_other * pivots], axis=1))
        tall = jnp.concatenate([x for x in left for _ in range(3)] + [jnp.zeros((8, size), F32)], axis=0)
        wide = jnp.concatenate(list(right) * 3 + [jnp.zeros((8, 2 * size), F32)], axis=0)
        update = lax.dot_general(
            tall.astype(BF16), wide.astype(BF16), (((0,), (0,)), ((), ())), preferred_element_type=F32
        )
        for i in range(p + 1, groups):
            a[i] = a[i] - update[8 * i : 8 * i + 8, :size]
            b[i] = b[i] - update[8 * i : 8 * i + 8, size:]
    return rows


def basis_kernel(gram, second, out, inverse, *, factor):
    size = gram.shape[0]
    groups = size // 8
    lane = lax.broadcasted_iota(jnp.int32, (8, size), 1)
    sub = lax.broadcasted_iota(jnp.int32, (8, size), 0)
    a = [gram[8 * g : 8 * g + 8, :] for g in range(groups)]
    b = [jnp.where(lane == sub + 8 * g, 1.0, 0.0).astype(F32) for g in range(groups)]
    for g, row in enumerate(inverse_factor(a, b, size)):
        inverse[8 * g : 8 * g + 8, :] = row * factor
    high, middle, low = (x.astype(BF16) for x in thirds(jnp.transpose(inverse[...])))
    main = jnp.concatenate([jnp.concatenate([high, middle], axis=1)] * 2, axis=0)
    rest = jnp.concatenate([low, high], axis=0)

    def some(r, carry):
        for u in range(4):
            left = [x.astype(BF16) for x in thirds(second[4 * r + u])]
            part = jnp.dot(jnp.concatenate(left[:2], axis=1), main, preferred_element_type=F32)
            small = jnp.dot(jnp.concatenate(left[::2], axis=1), rest, preferred_element_type=F32)
            out[4 * r + u] = part[:, :size] + (part[:, size:] + small)
        return carry

    lax.fori_loop(0, second.shape[0] // 4, some, 0)


def call(kernel, out_shape, in_specs, out_specs, scratch, flops, data, vmem=16):
    return pl.pallas_call(
        kernel,
        out_shape=out_shape,
        in_specs=in_specs,
        out_specs=out_specs,
        scratch_shapes=scratch,
        cost_estimate=pl.CostEstimate(flops=flops, bytes_accessed=data, transcendentals=0),
        compiler_params=pltpu.CompilerParams(vmem_limit_bytes=vmem * 1024 * 1024),
    )


def shift_pairs(parts, stride, extent, step):
    pairs = []
    for device in range(parts):
        place = device // stride % extent
        pairs.append((device, device + ((place + step) % extent - place) * stride))
    return pairs


def gather_hubs(hub, early, late):
    parts = lax.axis_size("dom")

    def move(value, even, odd, step):
        pairs = [
            shift_pairs(parts, (even, odd)[device % 2], 4, step)[device] for device in range(parts)
        ]
        return lax.ppermute(value, "dom", pairs)

    def all_four(value, even, odd):
        return jnp.concatenate([value] + [move(value, even, odd, step) for step in (3, 2, 1)], axis=0)

    z, x, y = STRIDES
    plane = all_four(all_four(hub, z, z), x, y)
    half = plane.shape[0] // 2
    low, high = plane[:half], plane[half:]
    after_low, before_high = move(low, y, x, 3), move(high, y, x, 1)
    after_high, before_low = move(high, y, x, 3), move(low, y, x, 1)
    after_low, before_high, done = lax.optimization_barrier((after_low, before_high, early(plane)))
    opposite = (move(after_low, y, x, 3), move(before_high, y, x, 1))
    opposite, done = lax.optimization_barrier((opposite, late(done)))
    pieces = [plane, after_low, after_high, before_low, before_high, *opposite]
    partner = shift_pairs(parts, 1, 2, 1)
    return pieces + [lax.ppermute(piece, "dom", partner) for piece in pieces], done


def sum_over_devices(value, parts):
    value = value + lax.ppermute(value, "dom", shift_pairs(parts, 1, 2, 1))
    stride = 2
    while stride < parts:
        across, left, right = (
            lax.ppermute(value, "dom", shift_pairs(parts, stride, 4, step)) for step in (2, 1, 3)
        )
        value = (value + across) + (left + right)
        stride *= 4
    return value


def shards(block_vector, tile_values, tile_rows, tile_cols, tile_counts, export_rows, send_pick):
    parts = lax.axis_size("dom")
    slots, side, _ = tile_values.shape
    width = block_vector.shape[1]
    blocks = block_vector.shape[0] // side
    vec = block_vector.reshape(blocks, side, width)
    block, wide = (side, width), (side, 2 * width)
    every = jax.ShapeDtypeStruct((blocks,) + block, F32)
    sums = pltpu.VMEM((blocks + 1,) + block, F32)
    spread = pltpu.VMEM((blocks,) + wide, BF16)
    whole = pltpu.VMEM((SLOTS,) + block, F32)
    halved = pltpu.VMEM((SLOTS,) + wide, BF16)
    sems = pltpu.SemaphoreType.DMA((SLOTS,))
    tile_bytes = side * side * 4
    tile_flops = 8 * side * side * width

    own = call(
        hub_kernel,
        jax.ShapeDtypeStruct((EXPORT,) + block, F32),
        [ANY, SMEM],
        VMEM,
        [pltpu.SemaphoreType.DMA((EXPORT,))],
        0,
        2 * EXPORT * tile_bytes,
        63,
    )(vec, export_rows)

    def early(plane):
        return call(
            degree_kernel,
            (
                jax.ShapeDtypeStruct((slots,) + wide, BF16),
                jax.ShapeDtypeStruct((blocks, side), F32),
                every,
                jax.ShapeDtypeStruct((FAR + slots,), jnp.int32),
                jax.ShapeDtypeStruct((parts,), jnp.int32),
            ),
            [ANY, ANY, SMEM, SMEM, SMEM, SMEM],
            (ANY, VMEM, VMEM, SMEM, SMEM),
            [whole, halved, sems, sems],
            slots * side * side * 4,
            2 * slots * tile_bytes,
            48,
        )(tile_values, plane, tile_rows, tile_counts, export_rows, lax.axis_index("dom").reshape(1))

    def late(found):
        split, scale_lane, scale_full, lists, places = found
        hub_scale = scale_lane.at[export_rows[0]].get(mode="promise_in_bounds")
        sent = jnp.where(send_pick[0][:, None] == 0, hub_scale[0], hub_scale[1])
        sent = jnp.concatenate(
            [sent, jnp.broadcast_to(send_pick[0][:, None], sent.shape).astype(F32)], axis=1
        )
        received = lax.all_to_all(sent, "dom", split_axis=0, concat_axis=0, tiled=True)
        return split, scale_lane, scale_full, lists, places, received

    offered, (split, scale_lane, scale_full, lists, places, received) = gather_hubs(own, early, late)
    scales = jnp.concatenate([scale_lane, received[:, :side]], axis=0)
    picks = received[:, side].astype(jnp.int32)

    hub = call(
        near_kernel,
        jax.ShapeDtypeStruct((EXPORT,) + block, F32),
        [ANY] * (2 + PIECES) + [SMEM] * 6 + [VMEM] * 2,
        VMEM,
        [whole, whole, pltpu.VMEM((EXPORT + 1,) + block, F32), sems, sems],
        slots // 16 * tile_flops,
        slots // 8 * tile_bytes,
    )(
        tile_values, vec, *offered, tile_rows, tile_cols, export_rows, picks, places, lists,
        scales, scale_full,
    )
    store = pltpu.VMEM((EXPORT * parts,) + block, F32)
    store_sems = pltpu.SemaphoreType.DMA((PIECES,))

    def far(plane):
        return call(
            far_kernel,
            jax.ShapeDtypeStruct((blocks,) + wide, BF16),
            [ANY] * (3 + PIECES) + [SMEM] * 7 + [VMEM] * 4,
            VMEM,
            [whole, halved, store, spread, sums, sems, sems, store_sems],
            slots // 2 * tile_flops,
            slots // 2 * tile_bytes,
            34,
        )(
            tile_values, split, plane, *offered,
            tile_rows, tile_cols, tile_counts, export_rows, picks, places, lists,
            scales, scale_full, vec, hub,
        )

    def inner(scaled):
        return call(
            inner_kernel,
            every,
            [ANY, VMEM, SMEM, SMEM, SMEM],
            VMEM,
            [halved, sums, sems],
            slots // 4 * tile_flops,
            slots // 4 * tile_bytes,
            34,
        )(split, scaled, tile_rows, tile_cols, tile_counts)

    offered_next, inner_next = gather_hubs(hub, far, inner)
    second, gram = call(
        last_kernel,
        (every, jax.ShapeDtypeStruct((width, width), F32)),
        [ANY] * (1 + PIECES) + [SMEM] * 5 + [VMEM] * 2,
        (VMEM, VMEM),
        [halved, store, sums, pltpu.VMEM((2 * width, 2 * width), F32), sems, store_sems],
        slots // 2 * tile_flops,
        slots * tile_bytes,
        26,
    )(split, *offered_next, tile_rows, tile_cols, tile_counts, picks, places, scale_full, inner_next)
    basis = call(
        functools.partial(basis_kernel, factor=math.sqrt(blocks * side * parts)),
        every,
        [VMEM, VMEM],
        VMEM,
        [pltpu.VMEM((width, width), F32)],
        blocks * tile_flops,
        2 * blocks * tile_bytes,
    )(sum_over_devices(gram, parts), second)
    return basis.reshape(block_vector.shape)


def solution(mesh):
    in_specs = (
        P("dom", None),
        P("dom", None, None),
        P("dom"),
        P("dom"),
        P("dom", None),
        P("dom", None),
        P("dom", None),
    )
    out_specs = P("dom", None)
    return jax.shard_map(shards, mesh=mesh, in_specs=in_specs, out_specs=out_specs, check_vma=False)
```

```python
import functools
import math

import jax
import jax.numpy as jnp
from jax import lax
from jax.experimental import pallas as pl
from jax.experimental.pallas import tpu as pltpu
from jax.sharding import PartitionSpec as P

EXPORT = 2
N_CHIPS = 64
STRIDES = (2, 8, 32)
PIECES = 14
PLANE = 32
T_MAX = 320
NEAR, FAR = 8, 8 + T_MAX
SLOTS = 48
UNROLL = 8
F32 = jnp.float32
BF16 = jnp.bfloat16
VMEM = pl.BlockSpec(memory_space=pltpu.VMEM)
SMEM = pl.BlockSpec(memory_space=pltpu.SMEM)
ANY = pl.BlockSpec(memory_space=pltpu.HBM)


def halves(x):
    high = x.astype(BF16)
    low = (x - high.astype(F32)).astype(BF16)
    return jnp.concatenate([high, low], axis=1)


def product(left, right):
    both = jnp.dot(left, jnp.concatenate([right, right], axis=0), preferred_element_type=F32)
    width = both.shape[1] // 2
    return both[:, :width] + both[:, width:]


def stream(count, copies, work, group=None, ready=lambda: None):
    rounds = (count + UNROLL - 1) // UNROLL
    ahead = SLOTS // UNROLL - 1

    def of_round(r):
        first = r * UNROLL
        found = [] if group is None else [group(first, lax.rem(first, SLOTS))]
        for u in range(UNROLL):
            found.extend(copies(jnp.minimum(first + u, count - 1), lax.rem(first + u, SLOTS)))
        return found

    def start(r, carry):
        for copy in of_round(r):
            copy.start()
        return carry

    lax.fori_loop(0, jnp.minimum(ahead, rounds), start, 0)
    ready()

    def one_round(r, carry):
        @pl.when(r + ahead < rounds)
        def _():
            start(r + ahead, 0)

        for copy in of_round(r):
            copy.wait()
        first = r * UNROLL
        work(
            [
                (jnp.minimum(first + u, count - 1), lax.rem(first + u, SLOTS), first + u < count)
                for u in range(UNROLL)
            ]
        )
        return carry

    lax.fori_loop(0, rounds, one_round, 0)


def window(array, first):
    return jnp.minimum(first, array.shape[0] - UNROLL)


def piece_starts(pieces):
    starts = [0]
    for piece in pieces:
        starts.append(starts[-1] + piece.shape[0])
    return starts


class GhostCopy:
    def __init__(self, pieces, place, target, sem):
        self.pieces, self.place, self.target, self.sem = pieces, place, target, sem

    def start(self):
        starts = piece_starts(self.pieces)
        places = list(zip(self.pieces, starts[:-1], starts[1:]))

        def among(some):
            if len(some) == 1:
                piece, low, _ = some[0]
                pltpu.make_async_copy(piece.at[self.place - low], self.target, self.sem).start()
                return
            middle = len(some) // 2
            in_first = self.place < some[middle][1]
            pl.when(in_first)(lambda: among(some[:middle]))
            pl.when(jnp.logical_not(in_first))(lambda: among(some[middle:]))

        among(places)

    def wait(self):
        pltpu.make_async_copy(self.pieces[0].at[0], self.target, self.sem).wait()


def all_pieces(pieces, store, sem):
    return [
        pltpu.make_async_copy(piece, store.at[pl.ds(low, piece.shape[0])], sem.at[k])
        for k, (piece, low) in enumerate(zip(pieces, piece_starts(pieces)))
    ]


def hub_kernel(vec, exports, out, sem):
    copies = [pltpu.make_async_copy(vec.at[exports[0, k]], out.at[k], sem.at[k]) for k in range(EXPORT)]
    for copy in copies:
        copy.start()
    for copy in copies:
        copy.wait()


def index_kernel(rows, counts, exports, me, lists, places):
    inner, live = counts[0, 0], counts[0, 1]

    first_row, second_row = exports[0, 0], exports[0, 1]

    def sort(i, carry):
        near, far = carry
        row = rows[i]
        is_near = (row == first_row) | (row == second_row)
        is_far = jnp.logical_not(is_near) & (i >= inner)

        @pl.when(is_near)
        def _():
            lists[NEAR + near] = i

        @pl.when(is_far)
        def _():
            lists[FAR + far] = i

        return near + is_near.astype(jnp.int32), far + is_far.astype(jnp.int32)

    mine = me[0]

    def place(q, carry):
        ahead = [lax.rem(q // stride - mine // stride + 4 * N_CHIPS, 4) for stride in STRIDES]
        odd = lax.rem(q, 2)
        second = jnp.where(odd == 0, ahead[1], ahead[2])
        final = jnp.where(odd == 0, ahead[2], ahead[1])
        piece = jnp.where(final == 3, 2, jnp.where(final == 2, 3, final))
        piece = piece + jnp.where(odd == lax.rem(mine, 2), 0, 4)
        places[q] = piece * PLANE + (second * 4 + ahead[0]) * EXPORT
        return carry

    lax.fori_loop(0, places.shape[0], place, 0)

    near, far = lax.fori_loop(0, live, sort, (jnp.int32(0), jnp.int32(0)))
    lists[0] = near
    lists[1] = far


def degree_kernel(
    tiles, after, rows, counts,
    split_out, scale_lane, scale_full,
    buf, half, sem, out_sem,
):
    blocks = scale_full.shape[0]
    live = counts[0, 1]
    scale_full[...] = jnp.zeros_like(scale_full)

    rounds = (live + UNROLL - 1) // UNROLL
    depth = SLOTS // UNROLL

    def slots_of(r):
        return pl.ds(lax.rem(r, depth) * UNROLL, UNROLL)

    def in_copy(r):
        return pltpu.make_async_copy(tiles.at[pl.ds(r * UNROLL, UNROLL)], buf.at[slots_of(r)], sem.at[lax.rem(r, depth)])

    def out_copy(r):
        return pltpu.make_async_copy(
            half.at[slots_of(r)], split_out.at[pl.ds(r * UNROLL, UNROLL)], out_sem.at[lax.rem(r, depth)]
        )

    def prime(r, carry):
        in_copy(r).start()
        return carry

    lax.fori_loop(0, jnp.minimum(depth - 1, rounds), prime, 0)

    def one_round(r, carry):
        @pl.when(r + depth - 1 < rounds)
        def _():
            in_copy(r + depth - 1).start()

        @pl.when(r >= depth)
        def _():
            out_copy(r - depth).wait()

        in_copy(r).wait()
        base = lax.rem(r, depth) * UNROLL
        for u in range(UNROLL):
            half[base + u] = halves(buf[base + u])
        for u in range(UNROLL):
            i = r * UNROLL + u
            row = rows[i]
            scale_full[row] = scale_full[row] + jnp.where(i < live, jnp.abs(buf[base + u]), 0.0)
        out_copy(r).start()
        return carry

    lax.fori_loop(0, rounds, one_round, 0)

    def scale_blocks(g, carry):
        totals = [scale_full[4 * g + u] for u in range(4)]
        sums = [lax.rsqrt(jnp.sum(total, axis=1, keepdims=True)) for total in totals]
        for u, down in enumerate(sums):
            full = jnp.broadcast_to(down, totals[u].shape)
            scale_full[4 * g + u] = full
            scale_lane[pl.ds(4 * g + u, 1), :] = jnp.transpose(full)[0:1, :]
        return carry

    lax.fori_loop(0, blocks // 4, scale_blocks, 0)

    def drain(r, carry):
        out_copy(r).wait()
        return carry

    lax.fori_loop(jnp.maximum(rounds - depth, 0), rounds, drain, 0)


def add_tiles(steps, left_of, right_of, row_of, total):
    parts = [product(left_of(i, slot), right_of(i, slot)) for i, slot, _ in steps]
    for (i, _, alive), part in zip(steps, parts):
        row = jnp.where(alive, row_of(i), total.shape[0] - 1)
        total[row] = total[row] + part


def halves_group(split, half, sem, begin):
    def group(first, slot):
        return pltpu.make_async_copy(
            split.at[pl.ds(window(split, begin + first), UNROLL)], half.at[pl.ds(slot, UNROLL)], sem.at[slot]
        )

    def tile(i, slot):
        first = i // UNROLL * UNROLL
        place = begin + i - window(split, begin + first)
        return half[slot // UNROLL * UNROLL + place]

    return group, tile


def add_inner(split, half, sem, scaled, rows, cols, count, total, row_of):
    group, tile = halves_group(split, half, sem, 0)

    def work(steps):
        add_tiles(steps, tile, lambda i, slot: scaled[cols[i]], row_of, total)

    stream(count, lambda i, slot: (), work, group)


def near_kernel(tiles, vec, *refs):
    pieces = refs[:PIECES]
    (
        rows, cols, exports, picks, places, lists, scales, scale_full,
        hub_out, buf, source, total, sem, source_sem,
    ) = refs[PIECES:]
    blocks = scale_full.shape[0]
    sources = pieces + (vec,)
    ghosts = piece_starts(pieces)[-1]
    total[...] = jnp.zeros_like(total)

    def copies(i, slot):
        t = lists[NEAR + i]
        col = cols[t]
        q = jnp.maximum(col - blocks, 0)
        place = jnp.where(col < blocks, ghosts + col, places[q] + picks[q])
        return (
            pltpu.make_async_copy(tiles.at[t], buf.at[slot], sem.at[slot]),
            GhostCopy(sources, place, source.at[slot], source_sem.at[slot]),
        )

    def work(steps):
        add_tiles(
            steps,
            lambda i, slot: halves(buf[slot] * scales[pl.ds(cols[lists[NEAR + i]], 1), :]),
            lambda i, slot: halves(source[slot]),
            lambda i: jnp.where(rows[lists[NEAR + i]] == exports[0, 0], 0, 1),
            total,
        )

    stream(lists[0], copies, work)
    for k in range(EXPORT):
        scale = scale_full[exports[0, k]]
        hub_out[k] = scale * (scale * total[k])


def far_kernel(tiles, split, after, *refs):
    pieces = refs[:PIECES]
    (
        rows, cols, counts, exports, picks, places, lists, scales, scale_full, vec, hub,
        scaled_out, buf, half, store, scaled, total, sem, half_sem, store_sem,
    ) = refs[PIECES:]
    blocks = scale_full.shape[0]
    bulk = all_pieces(pieces, store, store_sem)
    for copy in bulk:
        copy.start()
    total[...] = jnp.zeros_like(total)

    def scale_block(r, carry):
        scaled[r] = halves(scale_full[r] * vec[r])
        return carry

    lax.fori_loop(0, blocks, scale_block, 0)

    def other_row(i):
        row = rows[i]
        return jnp.where((row == exports[0, 0]) | (row == exports[0, 1]), blocks, row)

    add_inner(split, half, half_sem, scaled, rows, cols, counts[0, 0], total, other_row)

    def ghost_of(i):
        return cols[lists[FAR + i]] - blocks

    def copies(i, slot):
        return [pltpu.make_async_copy(tiles.at[lists[FAR + i]], buf.at[slot], sem.at[slot])]

    def right_of(i, slot):
        q = ghost_of(i)
        return halves(store[places[q] + picks[q]])

    def work(steps):
        add_tiles(
            steps,
            lambda i, slot: halves(buf[slot] * scales[pl.ds(blocks + ghost_of(i), 1), :]),
            right_of,
            lambda i: rows[lists[FAR + i]],
            total,
        )

    def ready():
        for copy in bulk:
            copy.wait()

    stream(lists[1], copies, work, ready=ready)

    def next_block(r, carry):
        scale = scale_full[r]
        scaled_out[r] = halves(scale * (scale * total[r]))
        return carry

    lax.fori_loop(0, blocks, next_block, 0)
    for k in range(EXPORT):
        scaled_out[exports[0, k]] = halves(hub[k])


def inner_kernel(split, scaled, rows, cols, counts, total_out, half, total, sem):
    total[...] = jnp.zeros_like(total)
    add_inner(split, half, sem, scaled, rows, cols, counts[0, 0], total, lambda i: rows[i])
    total_out[...] = total[0 : total_out.shape[0]]


def last_kernel(split, *refs):
    pieces = refs[:PIECES]
    (
        rows, cols, counts, picks, places, scale_full, inner_sum,
        second, gram, half, store, total, both, sem, store_sem,
    ) = refs[PIECES:]
    blocks, side, width = scale_full.shape
    bulk = all_pieces(pieces, store, store_sem)
    for copy in bulk:
        copy.start()
    total[0:blocks] = inner_sum[...]
    total[blocks] = jnp.zeros_like(total[blocks])
    both[...] = jnp.zeros_like(both)
    inner = counts[0, 0]
    group, tile = halves_group(split, half, sem, inner)

    def right_of(i, slot):
        q = cols[inner + i] - blocks
        return halves(store[places[q] + picks[q]])

    def work(steps):
        add_tiles(steps, tile, right_of, lambda i: rows[inner + i], total)

    def ready():
        for copy in bulk:
            copy.wait()

    stream(counts[0, 1] - inner, lambda i, slot: (), work, group, ready)

    def finish(g, carry):
        pieces = []
        for u in range(4):
            r = g * 4 + u
            value = scale_full[r] * total[r]
            second[r] = value
            pieces.append(halves(value))
        tall = jnp.concatenate(pieces, axis=0)
        both[...] += lax.dot_general(tall, tall, (((0,), (0,)), ((), ())), preferred_element_type=F32)
        return carry

    lax.fori_loop(0, blocks // 4, finish, 0)
    gram[...] = (both[0:width, 0:width] + both[width:, width:]) + (both[0:width, width:] + both[width:, 0:width])


def thirds(x):
    high = x.astype(BF16).astype(F32)
    rest = x - high
    middle = rest.astype(BF16).astype(F32)
    return high, middle, rest - middle


def inverse_factor(a, b, size):
    groups = size // 8
    sub = lax.broadcasted_iota(jnp.int32, (8, size), 0)
    masks = [sub == i for i in range(8)]
    rows = []
    for p in range(groups):
        block, other = a[p], b[p]
        s = [
            [jnp.broadcast_to(block[i : i + 1, 8 * p + j : 8 * p + j + 1], (8, size)) for j in range(i + 1)]
            for i in range(8)
        ]
        block_rows = [jnp.broadcast_to(block[i : i + 1, :], (8, size)) for i in range(8)]
        other_rows = [jnp.broadcast_to(other[i : i + 1, :], (8, size)) for i in range(8)]
        low = [[None] * 8 for _ in range(8)]
        reciprocals = []
        for k in range(8):
            reciprocal = 1.0 / s[k][k]
            reciprocals.append(reciprocal)
            for i in range(k + 1, 8):
                low[i][k] = s[i][k] * reciprocal
            for i in range(k + 1, 8):
                for j in range(k + 1, i + 1):
                    s[i][j] = s[i][j] - low[i][k] * s[j][k]
        inv = [[None] * 8 for _ in range(8)]
        for i in range(8):
            for j in range(i):
                total = low[i][j]
                for k in range(j + 1, i):
                    total = total + low[i][k] * inv[k][j]
                inv[i][j] = -total
        pivots, roots = reciprocals[0], s[0][0]
        for i in range(1, 8):
            pivots = jnp.where(masks[i], reciprocals[i], pivots)
            roots = jnp.where(masks[i], s[i][i], roots)
        new_block, new_other = block, other
        for j in range(7):
            coefficient = jnp.zeros((8, size), F32)
            for i in range(j + 1, 8):
                coefficient = jnp.where(masks[i], inv[i][j], coefficient)
            new_block = new_block + coefficient * block_rows[j]
            new_other = new_other + coefficient * other_rows[j]
        rows.append(new_other * lax.rsqrt(roots))
        if p + 1 == groups:
            break
        left = thirds(new_block)
        right = thirds(jnp.concatenate([new_block * pivots, new_other * pivots], axis=1))
        tall = jnp.concatenate([x for x in left for _ in range(3)] + [jnp.zeros((8, size), F32)], axis=0)
        wide = jnp.concatenate(list(right) * 3 + [jnp.zeros((8, 2 * size), F32)], axis=0)
        update = lax.dot_general(
            tall.astype(BF16), wide.astype(BF16), (((0,), (0,)), ((), ())), preferred_element_type=F32
        )
        for i in range(p + 1, groups):
            a[i] = a[i] - update[8 * i : 8 * i + 8, :size]
            b[i] = b[i] - update[8 * i : 8 * i + 8, size:]
    return rows


def basis_kernel(gram, second, out, inverse, *, factor):
    size = gram.shape[0]
    groups = size // 8
    lane = lax.broadcasted_iota(jnp.int32, (8, size), 1)
    sub = lax.broadcasted_iota(jnp.int32, (8, size), 0)
    a = [gram[8 * g : 8 * g + 8, :] for g in range(groups)]
    b = [jnp.where(lane == sub + 8 * g, 1.0, 0.0).astype(F32) for g in range(groups)]
    for g, row in enumerate(inverse_factor(a, b, size)):
        inverse[8 * g : 8 * g + 8, :] = row * factor
    high, middle, low = (x.astype(BF16) for x in thirds(jnp.transpose(inverse[...])))
    main = jnp.concatenate([jnp.concatenate([high, middle], axis=1)] * 2, axis=0)
    rest = jnp.concatenate([low, high], axis=0)

    def some(r, carry):
        for u in range(4):
            left = [x.astype(BF16) for x in thirds(second[4 * r + u])]
            part = jnp.dot(jnp.concatenate(left[:2], axis=1), main, preferred_element_type=F32)
            small = jnp.dot(jnp.concatenate(left[::2], axis=1), rest, preferred_element_type=F32)
            out[4 * r + u] = part[:, :size] + (part[:, size:] + small)
        return carry

    lax.fori_loop(0, second.shape[0] // 4, some, 0)


def call(kernel, out_shape, in_specs, out_specs, scratch, flops, data, vmem=16):
    return pl.pallas_call(
        kernel,
        out_shape=out_shape,
        in_specs=in_specs,
        out_specs=out_specs,
        scratch_shapes=scratch,
        cost_estimate=pl.CostEstimate(flops=flops, bytes_accessed=data, transcendentals=0),
        compiler_params=pltpu.CompilerParams(vmem_limit_bytes=vmem * 1024 * 1024),
    )


def shift_pairs(parts, stride, extent, step):
    pairs = []
    for device in range(parts):
        place = device // stride % extent
        pairs.append((device, device + ((place + step) % extent - place) * stride))
    return pairs


def gather_hubs(hub, early, late):
    parts = lax.axis_size("dom")

    def move(value, even, odd, step):
        pairs = [
            shift_pairs(parts, (even, odd)[device % 2], 4, step)[device] for device in range(parts)
        ]
        return lax.ppermute(value, "dom", pairs)

    def all_four(value, even, odd):
        return jnp.concatenate([value] + [move(value, even, odd, step) for step in (3, 2, 1)], axis=0)

    z, x, y = STRIDES
    plane = lax.optimization_barrier(all_four(all_four(hub, z, z), x, y))
    half = plane.shape[0] // 2
    low, high = plane[:half], plane[half:]
    after_low, before_high = move(low, y, x, 3), move(high, y, x, 1)
    after_high, before_low = move(high, y, x, 3), move(low, y, x, 1)
    after_low, before_high, done = lax.optimization_barrier((after_low, before_high, early(plane)))
    opposite = (move(after_low, y, x, 3), move(before_high, y, x, 1))
    opposite, done = lax.optimization_barrier((opposite, late(done)))
    pieces = [plane, after_low, after_high, before_low, before_high, *opposite]
    partner = shift_pairs(parts, 1, 2, 1)
    return pieces + [lax.ppermute(piece, "dom", partner) for piece in pieces], done


def sum_over_devices(value, parts):
    value = value + lax.ppermute(value, "dom", shift_pairs(parts, 1, 2, 1))
    stride = 2
    while stride < parts:
        across, left, right = (
            lax.ppermute(value, "dom", shift_pairs(parts, stride, 4, step)) for step in (2, 1, 3)
        )
        value = (value + across) + (left + right)
        stride *= 4
    return value


def shards(block_vector, tile_values, tile_rows, tile_cols, tile_counts, export_rows, send_pick):
    parts = lax.axis_size("dom")
    slots, side, _ = tile_values.shape
    width = block_vector.shape[1]
    blocks = block_vector.shape[0] // side
    vec = block_vector.reshape(blocks, side, width)
    block, wide = (side, width), (side, 2 * width)
    every = jax.ShapeDtypeStruct((blocks,) + block, F32)
    sums = pltpu.VMEM((blocks + 1,) + block, F32)
    spread = pltpu.VMEM((blocks,) + wide, BF16)
    whole = pltpu.VMEM((SLOTS,) + block, F32)
    halved = pltpu.VMEM((SLOTS,) + wide, BF16)
    sems = pltpu.SemaphoreType.DMA((SLOTS,))
    tile_bytes = side * side * 4
    tile_flops = 8 * side * side * width

    own = call(
        hub_kernel,
        jax.ShapeDtypeStruct((EXPORT,) + block, F32),
        [ANY, SMEM],
        VMEM,
        [pltpu.SemaphoreType.DMA((EXPORT,))],
        0,
        2 * EXPORT * tile_bytes,
        63,
    )(vec, export_rows)
    def early(plane):
        return call(
            degree_kernel,
            (
                jax.ShapeDtypeStruct((slots,) + wide, BF16),
                jax.ShapeDtypeStruct((blocks, side), F32),
                every,
            ),
            [ANY, ANY, SMEM, SMEM],
            (ANY, VMEM, VMEM),
            [whole, halved, sems, sems],
            slots * side * side * 4,
            2 * slots * tile_bytes,
            44,
        )(tile_values, plane, tile_rows, tile_counts)

    def late(found):
        split, scale_lane, scale_full = found
        hub_scale = scale_lane.at[export_rows[0]].get(mode="promise_in_bounds")
        sent = jnp.where(send_pick[0][:, None] == 0, hub_scale[0], hub_scale[1])
        sent = jnp.concatenate(
            [sent, jnp.broadcast_to(send_pick[0][:, None], sent.shape).astype(F32)], axis=1
        )
        received = lax.all_to_all(sent, "dom", split_axis=0, concat_axis=0, tiled=True)
        lists, places = call(
            index_kernel,
            (jax.ShapeDtypeStruct((FAR + slots,), jnp.int32), jax.ShapeDtypeStruct((parts,), jnp.int32)),
            [SMEM] * 4,
            (SMEM, SMEM),
            [],
            slots * side * side // 4,
            4 * slots,
        )(tile_rows, tile_counts, export_rows, lax.axis_index("dom").reshape(1))
        return split, scale_lane, scale_full, received, lists, places

    offered, (split, scale_lane, scale_full, received, lists, places) = gather_hubs(own, early, late)
    scales = jnp.concatenate([scale_lane, received[:, :side]], axis=0)
    picks = received[:, side].astype(jnp.int32)

    hub = call(
        near_kernel,
        jax.ShapeDtypeStruct((EXPORT,) + block, F32),
        [ANY] * (2 + PIECES) + [SMEM] * 6 + [VMEM] * 2,
        VMEM,
        [whole, whole, pltpu.VMEM((EXPORT + 1,) + block, F32), sems, sems],
        slots // 16 * tile_flops,
        slots // 8 * tile_bytes,
        16,
    )(
        tile_values, vec, *offered, tile_rows, tile_cols, export_rows, picks, places, lists,
        scales, scale_full,
    )
    store = pltpu.VMEM((EXPORT * parts,) + block, F32)
    store_sems = pltpu.SemaphoreType.DMA((PIECES,))

    def far(plane):
        return call(
            far_kernel,
            jax.ShapeDtypeStruct((blocks,) + wide, BF16),
            [ANY] * (3 + PIECES) + [SMEM] * 7 + [VMEM] * 4,
            VMEM,
            [whole, halved, store, spread, sums, sems, sems, store_sems],
            slots // 2 * tile_flops,
            slots // 2 * tile_bytes,
            34,
        )(
            tile_values, split, plane, *offered,
            tile_rows, tile_cols, tile_counts, export_rows, picks, places, lists,
            scales, scale_full, vec, hub,
        )

    def inner(scaled):
        return call(
            inner_kernel,
            every,
            [ANY, VMEM, SMEM, SMEM, SMEM],
            VMEM,
            [halved, sums, sems],
            slots // 4 * tile_flops,
            slots // 4 * tile_bytes,
            34,
        )(split, scaled, tile_rows, tile_cols, tile_counts)

    offered_next, inner_next = gather_hubs(hub, far, inner)
    second, gram = call(
        last_kernel,
        (every, jax.ShapeDtypeStruct((width, width), F32)),
        [ANY] * (1 + PIECES) + [SMEM] * 5 + [VMEM] * 2,
        (VMEM, VMEM),
        [halved, store, sums, pltpu.VMEM((2 * width, 2 * width), F32), sems, store_sems],
        slots // 2 * tile_flops,
        slots * tile_bytes,
        26,
    )(split, *offered_next, tile_rows, tile_cols, tile_counts, picks, places, scale_full, inner_next)
    basis = call(
        functools.partial(basis_kernel, factor=math.sqrt(blocks * side * parts)),
        every,
        [VMEM, VMEM],
        VMEM,
        [pltpu.VMEM((width, width), F32)],
        blocks * tile_flops,
        2 * blocks * tile_bytes,
    )(sum_over_devices(gram, parts), second)
    return basis.reshape(block_vector.shape)


def solution(mesh):
    in_specs = (
        P("dom", None),
        P("dom", None, None),
        P("dom"),
        P("dom"),
        P("dom", None),
        P("dom", None),
        P("dom", None),
    )
    out_specs = P("dom", None)
    return jax.shard_map(shards, mesh=mesh, in_specs=in_specs, out_specs=out_specs, check_vma=False)
```

```python
import functools
import math

import jax
import jax.numpy as jnp
from jax import lax
from jax.experimental import pallas as pl
from jax.experimental.pallas import tpu as pltpu
from jax.sharding import PartitionSpec as P

EXPORT = 2
SHIFTS = (1, 3, 5)
PIECES = 14
PLANE = 32
T_MAX = 320
NEAR, FAR = 8, 8 + T_MAX
SLOTS = 32
UNROLL = 8
F32 = jnp.float32
BF16 = jnp.bfloat16
VMEM = pl.BlockSpec(memory_space=pltpu.VMEM)
SMEM = pl.BlockSpec(memory_space=pltpu.SMEM)
ANY = pl.BlockSpec(memory_space=pltpu.HBM)


def halves(x):
    high = x.astype(BF16)
    low = (x - high.astype(F32)).astype(BF16)
    return jnp.concatenate([high, low], axis=1)


def product(left, right):
    both = jnp.dot(left, jnp.concatenate([right, right], axis=0), preferred_element_type=F32)
    width = both.shape[1] // 2
    return both[:, :width] + both[:, width:]


def stream(count, copies, work, group=None, ready=lambda: None):
    rounds = (count + UNROLL - 1) // UNROLL
    ahead = SLOTS // UNROLL - 1

    def of_round(r):
        first = r * UNROLL
        found = [] if group is None else [group(first, first & (SLOTS - 1))]
        for u in range(UNROLL):
            found.extend(copies(jnp.minimum(first + u, count - 1), (first + u) & (SLOTS - 1)))
        return found

    def start(r, carry):
        for copy in of_round(r):
            copy.start()
        return carry

    lax.fori_loop(0, jnp.minimum(ahead, rounds), start, 0)
    ready()

    def one_round(r, carry):
        @pl.when(r + ahead < rounds)
        def _():
            start(r + ahead, 0)

        for copy in of_round(r):
            copy.wait()
        first = r * UNROLL
        work(
            [
                (jnp.minimum(first + u, count - 1), (first + u) & (SLOTS - 1), first + u < count)
                for u in range(UNROLL)
            ]
        )
        return carry

    lax.fori_loop(0, rounds, one_round, 0)


def window(array, first):
    return jnp.minimum(first, array.shape[0] - UNROLL)


def piece_starts(pieces):
    starts = [0]
    for piece in pieces:
        starts.append(starts[-1] + piece.shape[0])
    return starts


class GhostCopy:
    def __init__(self, pieces, place, target, sem):
        self.pieces, self.place, self.target, self.sem = pieces, place, target, sem

    def start(self):
        starts = piece_starts(self.pieces)
        places = list(zip(self.pieces, starts[:-1], starts[1:]))

        def among(some):
            if len(some) == 1:
                piece, low, _ = some[0]
                pltpu.make_async_copy(piece.at[self.place - low], self.target, self.sem).start()
                return
            middle = len(some) // 2
            in_first = self.place < some[middle][1]
            pl.when(in_first)(lambda: among(some[:middle]))
            pl.when(jnp.logical_not(in_first))(lambda: among(some[middle:]))

        among(places)

    def wait(self):
        pltpu.make_async_copy(self.pieces[0].at[0], self.target, self.sem).wait()


def all_pieces(pieces, store, sem):
    return [
        pltpu.make_async_copy(piece, store.at[pl.ds(low, piece.shape[0])], sem.at[k])
        for k, (piece, low) in enumerate(zip(pieces, piece_starts(pieces)))
    ]


def hub_kernel(vec, exports, out, sem):
    copies = [pltpu.make_async_copy(vec.at[exports[0, k]], out.at[k], sem.at[k]) for k in range(EXPORT)]
    for copy in copies:
        copy.start()
    for copy in copies:
        copy.wait()


def index_kernel(rows, counts, exports, me, lists, places):
    inner, live = counts[0, 0], counts[0, 1]

    first_row, second_row = exports[0, 0], exports[0, 1]

    def sort(i, carry):
        near, far = carry
        row = rows[i]
        is_near = (row == first_row) | (row == second_row)
        is_far = jnp.logical_not(is_near) & (i >= inner)

        @pl.when(is_near)
        def _():
            lists[NEAR + near] = i

        @pl.when(is_far)
        def _():
            lists[FAR + far] = i

        return near + is_near.astype(jnp.int32), far + is_far.astype(jnp.int32)

    mine = me[0]

    def place(q, carry):
        ahead = [((q >> shift) - (mine >> shift)) & 3 for shift in SHIFTS]
        odd = q & 1
        second = jnp.where(odd == 0, ahead[1], ahead[2])
        final = jnp.where(odd == 0, ahead[2], ahead[1])
        piece = jnp.where(final == 3, 2, jnp.where(final == 2, 3, final))
        piece = piece + jnp.where(odd == (mine & 1), 0, 4)
        places[q] = piece * PLANE + (second * 4 + ahead[0]) * EXPORT
        return carry

    lax.fori_loop(0, places.shape[0], place, 0)

    near, far = lax.fori_loop(0, live, sort, (jnp.int32(0), jnp.int32(0)))
    lists[0] = near
    lists[1] = far


def degree_kernel(
    tiles, after, rows, counts,
    split_out, scale_lane, scale_full,
    buf, half, sem, out_sem,
):
    blocks = scale_full.shape[0]
    live = counts[0, 1]
    scale_full[...] = jnp.zeros_like(scale_full)

    rounds = (live + UNROLL - 1) // UNROLL
    depth = SLOTS // UNROLL

    def slots_of(r):
        return pl.ds((r & (depth - 1)) * UNROLL, UNROLL)

    def in_copy(r):
        return pltpu.make_async_copy(tiles.at[pl.ds(r * UNROLL, UNROLL)], buf.at[slots_of(r)], sem.at[(r & (depth - 1))])

    def out_copy(r):
        return pltpu.make_async_copy(
            half.at[slots_of(r)], split_out.at[pl.ds(r * UNROLL, UNROLL)], out_sem.at[(r & (depth - 1))]
        )

    def prime(r, carry):
        in_copy(r).start()
        return carry

    lax.fori_loop(0, jnp.minimum(depth - 1, rounds), prime, 0)

    def one_round(r, carry):
        @pl.when(r + depth - 1 < rounds)
        def _():
            in_copy(r + depth - 1).start()

        @pl.when(r >= depth)
        def _():
            out_copy(r - depth).wait()

        in_copy(r).wait()
        base = (r & (depth - 1)) * UNROLL
        for u in range(UNROLL):
            half[base + u] = halves(buf[base + u])
        for u in range(UNROLL):
            i = r * UNROLL + u
            row = rows[i]
            scale_full[row] = scale_full[row] + jnp.where(i < live, jnp.abs(buf[base + u]), 0.0)
        out_copy(r).start()
        return carry

    lax.fori_loop(0, rounds, one_round, 0)

    def scale_blocks(g, carry):
        totals = [scale_full[4 * g + u] for u in range(4)]
        sums = [lax.rsqrt(jnp.sum(total, axis=1, keepdims=True)) for total in totals]
        for u, down in enumerate(sums):
            full = jnp.broadcast_to(down, totals[u].shape)
            scale_full[4 * g + u] = full
            scale_lane[pl.ds(4 * g + u, 1), :] = jnp.transpose(full)[0:1, :]
        return carry

    lax.fori_loop(0, blocks // 4, scale_blocks, 0)

    def drain(r, carry):
        out_copy(r).wait()
        return carry

    lax.fori_loop(jnp.maximum(rounds - depth, 0), rounds, drain, 0)


def add_tiles(steps, left_of, right_of, row_of, total):
    parts = [product(left_of(i, slot), right_of(i, slot)) for i, slot, _ in steps]
    for (i, _, alive), part in zip(steps, parts):
        row = jnp.where(alive, row_of(i), total.shape[0] - 1)
        total[row] = total[row] + part


def halves_group(split, half, sem, begin):
    def group(first, slot):
        return pltpu.make_async_copy(
            split.at[pl.ds(window(split, begin + first), UNROLL)], half.at[pl.ds(slot, UNROLL)], sem.at[slot]
        )

    def tile(i, slot):
        first = i & -UNROLL
        place = begin + i - window(split, begin + first)
        return half[(slot & -UNROLL) + place]

    return group, tile


def add_inner(split, half, sem, scaled, rows, cols, count, total, row_of):
    group, tile = halves_group(split, half, sem, 0)

    def work(steps):
        add_tiles(steps, tile, lambda i, slot: scaled[cols[i]], row_of, total)

    stream(count, lambda i, slot: (), work, group)


def near_kernel(tiles, vec, *refs):
    pieces = refs[:PIECES]
    (
        rows, cols, exports, picks, places, lists, scales, scale_full,
        hub_out, buf, source, total, sem, source_sem,
    ) = refs[PIECES:]
    blocks = scale_full.shape[0]
    sources = pieces + (vec,)
    ghosts = piece_starts(pieces)[-1]
    total[...] = jnp.zeros_like(total)

    def copies(i, slot):
        t = lists[NEAR + i]
        col = cols[t]
        q = jnp.maximum(col - blocks, 0)
        place = jnp.where(col < blocks, ghosts + col, places[q] + picks[q])
        return (
            pltpu.make_async_copy(tiles.at[t], buf.at[slot], sem.at[slot]),
            GhostCopy(sources, place, source.at[slot], source_sem.at[slot]),
        )

    def work(steps):
        add_tiles(
            steps,
            lambda i, slot: halves(buf[slot] * scales[pl.ds(cols[lists[NEAR + i]], 1), :]),
            lambda i, slot: halves(source[slot]),
            lambda i: jnp.where(rows[lists[NEAR + i]] == exports[0, 0], 0, 1),
            total,
        )

    stream(lists[0], copies, work)
    for k in range(EXPORT):
        scale = scale_full[exports[0, k]]
        hub_out[k] = scale * (scale * total[k])


def far_kernel(tiles, split, after, *refs):
    pieces = refs[:PIECES]
    (
        rows, cols, counts, exports, picks, places, lists, scales, scale_full, vec, hub,
        scaled_out, buf, half, store, scaled, total, sem, half_sem, store_sem,
    ) = refs[PIECES:]
    blocks = scale_full.shape[0]
    bulk = all_pieces(pieces, store, store_sem)
    for copy in bulk:
        copy.start()
    total[...] = jnp.zeros_like(total)

    def scale_block(r, carry):
        scaled[r] = halves(scale_full[r] * vec[r])
        return carry

    lax.fori_loop(0, blocks, scale_block, 0)

    def other_row(i):
        row = rows[i]
        return jnp.where((row == exports[0, 0]) | (row == exports[0, 1]), blocks, row)

    add_inner(split, half, half_sem, scaled, rows, cols, counts[0, 0], total, other_row)

    def ghost_of(i):
        return cols[lists[FAR + i]] - blocks

    def copies(i, slot):
        return [pltpu.make_async_copy(tiles.at[lists[FAR + i]], buf.at[slot], sem.at[slot])]

    def right_of(i, slot):
        q = ghost_of(i)
        return halves(store[places[q] + picks[q]])

    def work(steps):
        add_tiles(
            steps,
            lambda i, slot: halves(buf[slot] * scales[pl.ds(blocks + ghost_of(i), 1), :]),
            right_of,
            lambda i: rows[lists[FAR + i]],
            total,
        )

    def ready():
        for copy in bulk:
            copy.wait()

    stream(lists[1], copies, work, ready=ready)

    def next_block(r, carry):
        scale = scale_full[r]
        scaled_out[r] = halves(scale * (scale * total[r]))
        return carry

    lax.fori_loop(0, blocks, next_block, 0)
    for k in range(EXPORT):
        scaled_out[exports[0, k]] = halves(hub[k])


def inner_kernel(split, scaled, rows, cols, counts, total_out, half, total, sem):
    total[...] = jnp.zeros_like(total)
    add_inner(split, half, sem, scaled, rows, cols, counts[0, 0], total, lambda i: rows[i])
    total_out[...] = total[0 : total_out.shape[0]]


def last_kernel(split, *refs):
    pieces = refs[:PIECES]
    (
        rows, cols, counts, picks, places, scale_full, inner_sum,
        second, gram, half, store, total, both, sem, store_sem,
    ) = refs[PIECES:]
    blocks, side, width = scale_full.shape
    bulk = all_pieces(pieces, store, store_sem)
    for copy in bulk:
        copy.start()
    total[0:blocks] = inner_sum[...]
    total[blocks] = jnp.zeros_like(total[blocks])
    both[...] = jnp.zeros_like(both)
    inner = counts[0, 0]
    group, tile = halves_group(split, half, sem, inner)

    def right_of(i, slot):
        q = cols[inner + i] - blocks
        return halves(store[places[q] + picks[q]])

    def work(steps):
        add_tiles(steps, tile, right_of, lambda i: rows[inner + i], total)

    def ready():
        for copy in bulk:
            copy.wait()

    stream(counts[0, 1] - inner, lambda i, slot: (), work, group, ready)

    def finish(g, carry):
        pieces = []
        for u in range(4):
            r = g * 4 + u
            value = scale_full[r] * total[r]
            second[r] = value
            pieces.append(halves(value))
        tall = jnp.concatenate(pieces, axis=0)
        both[...] += lax.dot_general(tall, tall, (((0,), (0,)), ((), ())), preferred_element_type=F32)
        return carry

    lax.fori_loop(0, blocks // 4, finish, 0)
    gram[...] = (both[0:width, 0:width] + both[width:, width:]) + (both[0:width, width:] + both[width:, 0:width])


def thirds(x):
    high = x.astype(BF16).astype(F32)
    rest = x - high
    middle = rest.astype(BF16).astype(F32)
    return high, middle, rest - middle


def inverse_factor(a, b, size):
    groups = size // 8
    sub = lax.broadcasted_iota(jnp.int32, (8, size), 0)
    masks = [sub == i for i in range(8)]
    rows = []
    for p in range(groups):
        block, other = a[p], b[p]
        s = [
            [jnp.broadcast_to(block[i : i + 1, 8 * p + j : 8 * p + j + 1], (8, size)) for j in range(i + 1)]
            for i in range(8)
        ]
        block_rows = [jnp.broadcast_to(block[i : i + 1, :], (8, size)) for i in range(8)]
        other_rows = [jnp.broadcast_to(other[i : i + 1, :], (8, size)) for i in range(8)]
        low = [[None] * 8 for _ in range(8)]
        reciprocals = []
        for k in range(8):
            reciprocal = 1.0 / s[k][k]
            reciprocals.append(reciprocal)
            for i in range(k + 1, 8):
                low[i][k] = s[i][k] * reciprocal
            for i in range(k + 1, 8):
                for j in range(k + 1, i + 1):
                    s[i][j] = s[i][j] - low[i][k] * s[j][k]
        inv = [[None] * 8 for _ in range(8)]
        for i in range(8):
            for j in range(i):
                total = low[i][j]
                for k in range(j + 1, i):
                    total = total + low[i][k] * inv[k][j]
                inv[i][j] = -total
        pivots, roots = reciprocals[0], s[0][0]
        for i in range(1, 8):
            pivots = jnp.where(masks[i], reciprocals[i], pivots)
            roots = jnp.where(masks[i], s[i][i], roots)
        new_block, new_other = block, other
        for j in range(7):
            coefficient = jnp.zeros((8, size), F32)
            for i in range(j + 1, 8):
                coefficient = jnp.where(masks[i], inv[i][j], coefficient)
            new_block = new_block + coefficient * block_rows[j]
            new_other = new_other + coefficient * other_rows[j]
        rows.append(new_other * lax.rsqrt(roots))
        if p + 1 == groups:
            break
        left = thirds(new_block)
        right = thirds(jnp.concatenate([new_block * pivots, new_other * pivots], axis=1))
        tall = jnp.concatenate([x for x in left for _ in range(3)] + [jnp.zeros((8, size), F32)], axis=0)
        wide = jnp.concatenate(list(right) * 3 + [jnp.zeros((8, 2 * size), F32)], axis=0)
        update = lax.dot_general(
            tall.astype(BF16), wide.astype(BF16), (((0,), (0,)), ((), ())), preferred_element_type=F32
        )
        for i in range(p + 1, groups):
            a[i] = a[i] - update[8 * i : 8 * i + 8, :size]
            b[i] = b[i] - update[8 * i : 8 * i + 8, size:]
    return rows


def basis_kernel(gram, second, out, inverse, *, factor):
    size = gram.shape[0]
    groups = size // 8
    lane = lax.broadcasted_iota(jnp.int32, (8, size), 1)
    sub = lax.broadcasted_iota(jnp.int32, (8, size), 0)
    a = [gram[8 * g : 8 * g + 8, :] for g in range(groups)]
    b = [jnp.where(lane == sub + 8 * g, 1.0, 0.0).astype(F32) for g in range(groups)]
    for g, row in enumerate(inverse_factor(a, b, size)):
        inverse[8 * g : 8 * g + 8, :] = row * factor
    high, middle, low = (x.astype(BF16) for x in thirds(jnp.transpose(inverse[...])))
    main = jnp.concatenate([jnp.concatenate([high, middle], axis=1)] * 2, axis=0)
    rest = jnp.concatenate([low, high], axis=0)

    def some(r, carry):
        for u in range(4):
            left = [x.astype(BF16) for x in thirds(second[4 * r + u])]
            part = jnp.dot(jnp.concatenate(left[:2], axis=1), main, preferred_element_type=F32)
            small = jnp.dot(jnp.concatenate(left[::2], axis=1), rest, preferred_element_type=F32)
            out[4 * r + u] = part[:, :size] + (part[:, size:] + small)
        return carry

    lax.fori_loop(0, second.shape[0] // 4, some, 0)


def call(kernel, out_shape, in_specs, out_specs, scratch, flops, data, vmem=16):
    return pl.pallas_call(
        kernel,
        out_shape=out_shape,
        in_specs=in_specs,
        out_specs=out_specs,
        scratch_shapes=scratch,
        cost_estimate=pl.CostEstimate(flops=flops, bytes_accessed=data, transcendentals=0),
        compiler_params=pltpu.CompilerParams(vmem_limit_bytes=vmem * 1024 * 1024),
    )


def shift_pairs(parts, stride, extent, step):
    pairs = []
    for device in range(parts):
        place = device // stride % extent
        pairs.append((device, device + ((place + step) % extent - place) * stride))
    return pairs


def gather_hubs(hub, first, early, late):
    parts = lax.axis_size("dom")

    def move(value, even, odd, step):
        pairs = [
            shift_pairs(parts, (even, odd)[device % 2], 4, step)[device] for device in range(parts)
        ]
        return lax.ppermute(value, "dom", pairs)

    def all_four(value, even, odd):
        return jnp.concatenate([value] + [move(value, even, odd, step) for step in (3, 2, 1)], axis=0)

    z, x, y = (1 << shift for shift in SHIFTS)
    plane, begun = lax.optimization_barrier((all_four(all_four(hub, z, z), x, y), first()))
    half = plane.shape[0] // 2
    low, high = plane[:half], plane[half:]
    after_low, before_high = move(low, y, x, 3), move(high, y, x, 1)
    after_high, before_low = move(high, y, x, 3), move(low, y, x, 1)
    after_low, before_high, done = lax.optimization_barrier((after_low, before_high, early(plane)))
    opposite = (move(after_low, y, x, 3), move(before_high, y, x, 1))
    opposite, done = lax.optimization_barrier((opposite, late(done)))
    pieces = [plane, after_low, after_high, before_low, before_high, *opposite]
    partner = shift_pairs(parts, 1, 2, 1)
    return pieces + [lax.ppermute(piece, "dom", partner) for piece in pieces], begun, done


def sum_over_devices(value, parts):
    value = value + lax.ppermute(value, "dom", shift_pairs(parts, 1, 2, 1))
    stride = 2
    while stride < parts:
        across, left, right = (
            lax.ppermute(value, "dom", shift_pairs(parts, stride, 4, step)) for step in (2, 1, 3)
        )
        value = (value + across) + (left + right)
        stride *= 4
    return value


def shards(block_vector, tile_values, tile_rows, tile_cols, tile_counts, export_rows, send_pick):
    parts = lax.axis_size("dom")
    slots, side, _ = tile_values.shape
    width = block_vector.shape[1]
    blocks = block_vector.shape[0] // side
    vec = block_vector.reshape(blocks, side, width)
    block, wide = (side, width), (side, 2 * width)
    every = jax.ShapeDtypeStruct((blocks,) + block, F32)
    sums = pltpu.VMEM((blocks + 1,) + block, F32)
    spread = pltpu.VMEM((blocks,) + wide, BF16)
    whole = pltpu.VMEM((SLOTS,) + block, F32)
    halved = pltpu.VMEM((SLOTS,) + wide, BF16)
    sems = pltpu.SemaphoreType.DMA((SLOTS,))
    tile_bytes = side * side * 4
    tile_flops = 8 * side * side * width

    own = call(
        hub_kernel,
        jax.ShapeDtypeStruct((EXPORT,) + block, F32),
        [ANY, SMEM],
        VMEM,
        [pltpu.SemaphoreType.DMA((EXPORT,))],
        0,
        2 * EXPORT * tile_bytes,
        63,
    )(vec, export_rows)
    def first():
        return call(
            index_kernel,
            (jax.ShapeDtypeStruct((FAR + slots,), jnp.int32), jax.ShapeDtypeStruct((parts,), jnp.int32)),
            [SMEM] * 4,
            (SMEM, SMEM),
            [],
            slots * side * side // 4,
            4 * slots,
        )(tile_rows, tile_counts, export_rows, lax.axis_index("dom").reshape(1))

    def early(plane):
        return call(
            degree_kernel,
            (
                jax.ShapeDtypeStruct((slots,) + wide, BF16),
                jax.ShapeDtypeStruct((blocks, side), F32),
                every,
            ),
            [ANY, ANY, SMEM, SMEM],
            (ANY, VMEM, VMEM),
            [whole, halved, sems, sems],
            slots * side * side * 4,
            2 * slots * tile_bytes,
            44,
        )(tile_values, plane, tile_rows, tile_counts)

    def late(found):
        split, scale_lane, scale_full = found
        hub_scale = scale_lane.at[export_rows[0]].get(mode="promise_in_bounds")
        sent = jnp.where(send_pick[0][:, None] == 0, hub_scale[0], hub_scale[1])
        sent = jnp.concatenate(
            [sent, jnp.broadcast_to(send_pick[0][:, None], sent.shape).astype(F32)], axis=1
        )
        received = lax.all_to_all(sent, "dom", split_axis=0, concat_axis=0, tiled=True)
        return split, scale_lane, scale_full, received

    offered, (lists, places), (split, scale_lane, scale_full, received) = gather_hubs(own, first, early, late)
    scales = jnp.concatenate([scale_lane, received[:, :side]], axis=0)
    picks = received[:, side].astype(jnp.int32)

    hub = call(
        near_kernel,
        jax.ShapeDtypeStruct((EXPORT,) + block, F32),
        [ANY] * (2 + PIECES) + [SMEM] * 6 + [VMEM] * 2,
        VMEM,
        [whole, whole, pltpu.VMEM((EXPORT + 1,) + block, F32), sems, sems],
        slots // 16 * tile_flops,
        slots // 8 * tile_bytes,
        16,
    )(
        tile_values, vec, *offered, tile_rows, tile_cols, export_rows, picks, places, lists,
        scales, scale_full,
    )
    store = pltpu.VMEM((EXPORT * parts,) + block, F32)
    store_sems = pltpu.SemaphoreType.DMA((PIECES,))

    def far(plane):
        return call(
            far_kernel,
            jax.ShapeDtypeStruct((blocks,) + wide, BF16),
            [ANY] * (3 + PIECES) + [SMEM] * 7 + [VMEM] * 4,
            VMEM,
            [whole, halved, store, spread, sums, sems, sems, store_sems],
            slots // 2 * tile_flops,
            slots // 2 * tile_bytes,
            34,
        )(
            tile_values, split, plane, *offered,
            tile_rows, tile_cols, tile_counts, export_rows, picks, places, lists,
            scales, scale_full, vec, hub,
        )

    def inner(scaled):
        return call(
            inner_kernel,
            every,
            [ANY, VMEM, SMEM, SMEM, SMEM],
            VMEM,
            [halved, sums, sems],
            slots // 4 * tile_flops,
            slots // 4 * tile_bytes,
            34,
        )(split, scaled, tile_rows, tile_cols, tile_counts)

    offered_next, _, inner_next = gather_hubs(hub, tuple, far, inner)
    second, gram = call(
        last_kernel,
        (every, jax.ShapeDtypeStruct((width, width), F32)),
        [ANY] * (1 + PIECES) + [SMEM] * 5 + [VMEM] * 2,
        (VMEM, VMEM),
        [halved, store, sums, pltpu.VMEM((2 * width, 2 * width), F32), sems, store_sems],
        slots // 2 * tile_flops,
        slots * tile_bytes,
        26,
    )(split, *offered_next, tile_rows, tile_cols, tile_counts, picks, places, scale_full, inner_next)
    basis = call(
        functools.partial(basis_kernel, factor=math.sqrt(blocks * side * parts)),
        every,
        [VMEM, VMEM],
        VMEM,
        [pltpu.VMEM((width, width), F32)],
        blocks * tile_flops,
        2 * blocks * tile_bytes,
    )(sum_over_devices(gram, parts), second)
    return basis.reshape(block_vector.shape)


def solution(mesh):
    in_specs = (
        P("dom", None),
        P("dom", None, None),
        P("dom"),
        P("dom"),
        P("dom", None),
        P("dom", None),
        P("dom", None),
    )
    out_specs = P("dom", None)
    return jax.shard_map(shards, mesh=mesh, in_specs=in_specs, out_specs=out_specs, check_vma=False)
```

```python
import functools
import math

import jax
import jax.numpy as jnp
from jax import lax
from jax.experimental import pallas as pl
from jax.experimental.pallas import tpu as pltpu
from jax.sharding import PartitionSpec as P

EXPORT = 2
SHIFTS = (1, 3, 5)
PIECES = 14
PLANE = 32
T_MAX = 320
NEAR, FAR = 8, 8 + T_MAX
SLOTS = 32
UNROLL = 8
F32 = jnp.float32
BF16 = jnp.bfloat16
VMEM = pl.BlockSpec(memory_space=pltpu.VMEM)
SMEM = pl.BlockSpec(memory_space=pltpu.SMEM)
ANY = pl.BlockSpec(memory_space=pltpu.HBM)


def halves(x):
    high = x.astype(BF16)
    low = (x - high.astype(F32)).astype(BF16)
    return jnp.concatenate([high, low], axis=1)


def product(left, right):
    both = jnp.dot(left, jnp.concatenate([right, right], axis=0), preferred_element_type=F32)
    width = both.shape[1] // 2
    return both[:, :width] + both[:, width:]


def stream(count, copies, work, group=None, ready=lambda: None):
    rounds = (count + UNROLL - 1) // UNROLL
    ahead = SLOTS // UNROLL - 1

    def of_round(r):
        first = r * UNROLL
        found = [] if group is None else [group(first, first & (SLOTS - 1))]
        for u in range(UNROLL):
            found.extend(copies(jnp.minimum(first + u, count - 1), (first + u) & (SLOTS - 1)))
        return found

    def start(r, carry):
        for copy in of_round(r):
            copy.start()
        return carry

    lax.fori_loop(0, jnp.minimum(ahead, rounds), start, 0)
    ready()

    def one_round(r, carry):
        @pl.when(r + ahead < rounds)
        def _():
            start(r + ahead, 0)

        for copy in of_round(r):
            copy.wait()
        first = r * UNROLL
        work(
            [
                (jnp.minimum(first + u, count - 1), (first + u) & (SLOTS - 1), first + u < count)
                for u in range(UNROLL)
            ]
        )
        return carry

    lax.fori_loop(0, rounds, one_round, 0)


def window(array, first):
    return jnp.minimum(first, array.shape[0] - UNROLL)


def piece_starts(pieces):
    starts = [0]
    for piece in pieces:
        starts.append(starts[-1] + piece.shape[0])
    return starts


class GhostCopy:
    def __init__(self, pieces, place, target, sem):
        self.pieces, self.place, self.target, self.sem = pieces, place, target, sem

    def start(self):
        starts = piece_starts(self.pieces)
        places = list(zip(self.pieces, starts[:-1], starts[1:]))

        def among(some):
            if len(some) == 1:
                piece, low, _ = some[0]
                pltpu.make_async_copy(piece.at[self.place - low], self.target, self.sem).start()
                return
            middle = len(some) // 2
            in_first = self.place < some[middle][1]
            pl.when(in_first)(lambda: among(some[:middle]))
            pl.when(jnp.logical_not(in_first))(lambda: among(some[middle:]))

        among(places)

    def wait(self):
        pltpu.make_async_copy(self.pieces[0].at[0], self.target, self.sem).wait()


def all_pieces(pieces, store, sem):
    return [
        pltpu.make_async_copy(piece, store.at[pl.ds(low, piece.shape[0])], sem.at[k])
        for k, (piece, low) in enumerate(zip(pieces, piece_starts(pieces)))
    ]


def hub_kernel(vec, exports, out, sem):
    copies = [pltpu.make_async_copy(vec.at[exports[0, k]], out.at[k], sem.at[k]) for k in range(EXPORT)]
    for copy in copies:
        copy.start()
    for copy in copies:
        copy.wait()


def index_kernel(rows, counts, exports, me, lists, places):
    inner, live = counts[0, 0], counts[0, 1]

    first_row, second_row = exports[0, 0], exports[0, 1]

    def sort(i, carry):
        near, far = carry
        row = rows[i]
        is_near = (row == first_row) | (row == second_row)
        is_far = jnp.logical_not(is_near) & (i >= inner)

        @pl.when(is_near)
        def _():
            lists[NEAR + near] = i

        @pl.when(is_far)
        def _():
            lists[FAR + far] = i

        return near + is_near.astype(jnp.int32), far + is_far.astype(jnp.int32)

    mine = me[0]

    def place(q, carry):
        ahead = [((q >> shift) - (mine >> shift)) & 3 for shift in SHIFTS]
        odd = q & 1
        second = jnp.where(odd == 0, ahead[1], ahead[2])
        final = jnp.where(odd == 0, ahead[2], ahead[1])
        piece = jnp.where(final == 3, 2, jnp.where(final == 2, 3, final))
        piece = piece + jnp.where(odd == (mine & 1), 0, 4)
        places[q] = piece * PLANE + (second * 4 + ahead[0]) * EXPORT
        return carry

    lax.fori_loop(0, places.shape[0], place, 0)

    near, far = lax.fori_loop(0, live, sort, (jnp.int32(0), jnp.int32(0)))
    lists[0] = near
    lists[1] = far


def degree_kernel(
    tiles, after, rows, counts,
    split_out, scale_lane, scale_full,
    buf, half, sem, out_sem,
):
    blocks = scale_full.shape[0]
    live = counts[0, 1]
    scale_full[...] = jnp.zeros_like(scale_full)

    rounds = (live + UNROLL - 1) // UNROLL
    depth = SLOTS // UNROLL

    def slots_of(r):
        return pl.ds((r & (depth - 1)) * UNROLL, UNROLL)

    def in_copy(r):
        return pltpu.make_async_copy(tiles.at[pl.ds(r * UNROLL, UNROLL)], buf.at[slots_of(r)], sem.at[(r & (depth - 1))])

    def out_copy(r):
        return pltpu.make_async_copy(
            half.at[slots_of(r)], split_out.at[pl.ds(r * UNROLL, UNROLL)], out_sem.at[(r & (depth - 1))]
        )

    def prime(r, carry):
        in_copy(r).start()
        return carry

    lax.fori_loop(0, jnp.minimum(depth - 1, rounds), prime, 0)

    def one_round(r, carry):
        @pl.when(r + depth - 1 < rounds)
        def _():
            in_copy(r + depth - 1).start()

        @pl.when(r >= depth)
        def _():
            out_copy(r - depth).wait()

        in_copy(r).wait()
        base = (r & (depth - 1)) * UNROLL
        for u in range(UNROLL):
            half[base + u] = halves(buf[base + u])
        for u in range(UNROLL):
            i = r * UNROLL + u
            row = rows[i]
            scale_full[row] = scale_full[row] + jnp.where(i < live, jnp.abs(buf[base + u]), 0.0)
        out_copy(r).start()
        return carry

    lax.fori_loop(0, rounds, one_round, 0)

    def scale_blocks(g, carry):
        totals = [scale_full[4 * g + u] for u in range(4)]
        sums = [lax.rsqrt(jnp.sum(total, axis=1, keepdims=True)) for total in totals]
        for u, down in enumerate(sums):
            full = jnp.broadcast_to(down, totals[u].shape)
            scale_full[4 * g + u] = full
            scale_lane[pl.ds(4 * g + u, 1), :] = jnp.transpose(full)[0:1, :]
        return carry

    lax.fori_loop(0, blocks // 4, scale_blocks, 0)

    def drain(r, carry):
        out_copy(r).wait()
        return carry

    lax.fori_loop(jnp.maximum(rounds - depth, 0), rounds, drain, 0)


def add_tiles(steps, left_of, right_of, row_of, total):
    parts = [product(left_of(i, slot), right_of(i, slot)) for i, slot, _ in steps]
    for (i, _, alive), part in zip(steps, parts):
        row = jnp.where(alive, row_of(i), total.shape[0] - 1)
        total[row] = total[row] + part


def halves_group(split, half, sem, begin):
    def group(first, slot):
        return pltpu.make_async_copy(
            split.at[pl.ds(window(split, begin + first), UNROLL)], half.at[pl.ds(slot, UNROLL)], sem.at[slot]
        )

    def tile(i, slot):
        first = i & -UNROLL
        place = begin + i - window(split, begin + first)
        return half[(slot & -UNROLL) + place]

    return group, tile


def add_inner(split, half, sem, scaled, rows, cols, count, total, row_of):
    group, tile = halves_group(split, half, sem, 0)

    def work(steps):
        add_tiles(steps, tile, lambda i, slot: scaled[cols[i]], row_of, total)

    stream(count, lambda i, slot: (), work, group)


def near_kernel(tiles, vec, *refs):
    pieces = refs[:PIECES]
    (
        rows, cols, exports, picks, places, lists, scales, scale_full,
        hub_out, buf, source, total, sem, source_sem,
    ) = refs[PIECES:]
    blocks = scale_full.shape[0]
    sources = pieces + (vec,)
    ghosts = piece_starts(pieces)[-1]
    total[...] = jnp.zeros_like(total)

    def copies(i, slot):
        t = lists[NEAR + i]
        col = cols[t]
        q = jnp.maximum(col - blocks, 0)
        place = jnp.where(col < blocks, ghosts + col, places[q] + picks[q])
        return (
            pltpu.make_async_copy(tiles.at[t], buf.at[slot], sem.at[slot]),
            GhostCopy(sources, place, source.at[slot], source_sem.at[slot]),
        )

    def work(steps):
        add_tiles(
            steps,
            lambda i, slot: halves(buf[slot] * scales[pl.ds(cols[lists[NEAR + i]], 1), :]),
            lambda i, slot: halves(source[slot]),
            lambda i: jnp.where(rows[lists[NEAR + i]] == exports[0, 0], 0, 1),
            total,
        )

    stream(lists[0], copies, work)
    for k in range(EXPORT):
        scale = scale_full[exports[0, k]]
        hub_out[k] = scale * (scale * total[k])


def far_kernel(tiles, split, after, *refs):
    pieces = refs[:PIECES]
    (
        rows, cols, counts, exports, picks, places, lists, scales, scale_full, vec, hub,
        scaled_out, buf, half, store, scaled, total, sem, half_sem, store_sem,
    ) = refs[PIECES:]
    blocks = scale_full.shape[0]
    bulk = all_pieces(pieces, store, store_sem)
    for copy in bulk:
        copy.start()
    total[...] = jnp.zeros_like(total)

    def scale_block(r, carry):
        scaled[r] = halves(scale_full[r] * vec[r])
        return carry

    lax.fori_loop(0, blocks, scale_block, 0)

    def other_row(i):
        row = rows[i]
        return jnp.where((row == exports[0, 0]) | (row == exports[0, 1]), blocks, row)

    add_inner(split, half, half_sem, scaled, rows, cols, counts[0, 0], total, other_row)

    def ghost_of(i):
        return cols[lists[FAR + i]] - blocks

    def copies(i, slot):
        return [pltpu.make_async_copy(tiles.at[lists[FAR + i]], buf.at[slot], sem.at[slot])]

    def right_of(i, slot):
        q = ghost_of(i)
        return halves(store[places[q] + picks[q]])

    def work(steps):
        add_tiles(
            steps,
            lambda i, slot: halves(buf[slot] * scales[pl.ds(blocks + ghost_of(i), 1), :]),
            right_of,
            lambda i: rows[lists[FAR + i]],
            total,
        )

    def ready():
        for copy in bulk:
            copy.wait()

    stream(lists[1], copies, work, ready=ready)

    def next_block(r, carry):
        scale = scale_full[r]
        scaled_out[r] = halves(scale * (scale * total[r]))
        return carry

    lax.fori_loop(0, blocks, next_block, 0)
    for k in range(EXPORT):
        scaled_out[exports[0, k]] = halves(hub[k])


def inner_kernel(split, scaled, rows, cols, counts, total_out, half, total, sem):
    total[...] = jnp.zeros_like(total)
    add_inner(split, half, sem, scaled, rows, cols, counts[0, 0], total, lambda i: rows[i])
    total_out[...] = total[0 : total_out.shape[0]]


def last_kernel(split, *refs):
    pieces = refs[:PIECES]
    (
        rows, cols, counts, picks, places, scale_full, inner_sum,
        second, gram, half, store, total, both, sem, store_sem,
    ) = refs[PIECES:]
    blocks, side, width = scale_full.shape
    bulk = all_pieces(pieces, store, store_sem)
    for copy in bulk:
        copy.start()
    total[0:blocks] = inner_sum[...]
    total[blocks] = jnp.zeros_like(total[blocks])
    both[...] = jnp.zeros_like(both)
    inner = counts[0, 0]
    group, tile = halves_group(split, half, sem, inner)

    def right_of(i, slot):
        q = cols[inner + i] - blocks
        return halves(store[places[q] + picks[q]])

    def work(steps):
        add_tiles(steps, tile, right_of, lambda i: rows[inner + i], total)

    def ready():
        for copy in bulk:
            copy.wait()

    stream(counts[0, 1] - inner, lambda i, slot: (), work, group, ready)

    def finish(g, carry):
        pieces = []
        for u in range(4):
            r = g * 4 + u
            value = scale_full[r] * total[r]
            second[r] = value
            pieces.append(halves(value))
        tall = jnp.concatenate(pieces, axis=0)
        both[...] += lax.dot_general(tall, tall, (((0,), (0,)), ((), ())), preferred_element_type=F32)
        return carry

    lax.fori_loop(0, blocks // 4, finish, 0)
    gram[...] = (both[0:width, 0:width] + both[width:, width:]) + (both[0:width, width:] + both[width:, 0:width])


def thirds(x):
    high = x.astype(BF16).astype(F32)
    rest = x - high
    middle = rest.astype(BF16).astype(F32)
    return high, middle, rest - middle


def inverse_factor(a, b, size):
    groups = size // 8
    sub = lax.broadcasted_iota(jnp.int32, (8, size), 0)
    masks = [sub == i for i in range(8)]
    rows = []
    for p in range(groups):
        block, other = a[p], b[p]
        s = [
            [jnp.broadcast_to(block[i : i + 1, 8 * p + j : 8 * p + j + 1], (8, size)) for j in range(i + 1)]
            for i in range(8)
        ]
        block_rows = [jnp.broadcast_to(block[i : i + 1, :], (8, size)) for i in range(8)]
        other_rows = [jnp.broadcast_to(other[i : i + 1, :], (8, size)) for i in range(8)]
        low = [[None] * 8 for _ in range(8)]
        reciprocals = []
        for k in range(8):
            reciprocal = 1.0 / s[k][k]
            reciprocals.append(reciprocal)
            for i in range(k + 1, 8):
                low[i][k] = s[i][k] * reciprocal
            for i in range(k + 1, 8):
                for j in range(k + 1, i + 1):
                    s[i][j] = s[i][j] - low[i][k] * s[j][k]
        inv = [[None] * 8 for _ in range(8)]
        for i in range(8):
            for j in range(i):
                total = low[i][j]
                for k in range(j + 1, i):
                    total = total + low[i][k] * inv[k][j]
                inv[i][j] = -total
        pivots, roots = reciprocals[0], s[0][0]
        for i in range(1, 8):
            pivots = jnp.where(masks[i], reciprocals[i], pivots)
            roots = jnp.where(masks[i], s[i][i], roots)
        new_block, new_other = block, other
        for j in range(7):
            coefficient = jnp.zeros((8, size), F32)
            for i in range(j + 1, 8):
                coefficient = jnp.where(masks[i], inv[i][j], coefficient)
            new_block = new_block + coefficient * block_rows[j]
            new_other = new_other + coefficient * other_rows[j]
        rows.append(new_other * lax.rsqrt(roots))
        if p + 1 == groups:
            break
        left = thirds(new_block)
        right = thirds(jnp.concatenate([new_block * pivots, new_other * pivots], axis=1))
        tall = jnp.concatenate([x for x in left for _ in range(3)] + [jnp.zeros((8, size), F32)], axis=0)
        wide = jnp.concatenate(list(right) * 3 + [jnp.zeros((8, 2 * size), F32)], axis=0)
        update = lax.dot_general(
            tall.astype(BF16), wide.astype(BF16), (((0,), (0,)), ((), ())), preferred_element_type=F32
        )
        for i in range(p + 1, groups):
            a[i] = a[i] - update[8 * i : 8 * i + 8, :size]
            b[i] = b[i] - update[8 * i : 8 * i + 8, size:]
    return rows


def basis_kernel(gram, second, out, inverse, *, factor):
    size = gram.shape[0]
    groups = size // 8
    lane = lax.broadcasted_iota(jnp.int32, (8, size), 1)
    sub = lax.broadcasted_iota(jnp.int32, (8, size), 0)
    a = [gram[8 * g : 8 * g + 8, :] for g in range(groups)]
    b = [jnp.where(lane == sub + 8 * g, 1.0, 0.0).astype(F32) for g in range(groups)]
    for g, row in enumerate(inverse_factor(a, b, size)):
        inverse[8 * g : 8 * g + 8, :] = row * factor
    high, middle, low = (x.astype(BF16) for x in thirds(jnp.transpose(inverse[...])))
    main = jnp.concatenate([jnp.concatenate([high, middle], axis=1)] * 2, axis=0)
    rest = jnp.concatenate([low, high], axis=0)

    def some(r, carry):
        for u in range(4):
            left = [x.astype(BF16) for x in thirds(second[4 * r + u])]
            part = jnp.dot(jnp.concatenate(left[:2], axis=1), main, preferred_element_type=F32)
            small = jnp.dot(jnp.concatenate(left[::2], axis=1), rest, preferred_element_type=F32)
            out[4 * r + u] = part[:, :size] + (part[:, size:] + small)
        return carry

    lax.fori_loop(0, second.shape[0] // 4, some, 0)


def call(kernel, out_shape, in_specs, out_specs, scratch, flops, data, vmem=16):
    return pl.pallas_call(
        kernel,
        out_shape=out_shape,
        in_specs=in_specs,
        out_specs=out_specs,
        scratch_shapes=scratch,
        cost_estimate=pl.CostEstimate(flops=flops, bytes_accessed=data, transcendentals=0),
        compiler_params=pltpu.CompilerParams(vmem_limit_bytes=vmem * 1024 * 1024),
    )


def shift_pairs(parts, stride, extent, step):
    pairs = []
    for device in range(parts):
        place = device // stride % extent
        pairs.append((device, device + ((place + step) % extent - place) * stride))
    return pairs


def gather_hubs(hub, first, early, late):
    parts = lax.axis_size("dom")

    def move(value, even, odd, step):
        pairs = [
            shift_pairs(parts, (even, odd)[device % 2], 4, step)[device] for device in range(parts)
        ]
        return lax.ppermute(value, "dom", pairs)

    def all_four(value, even, odd):
        return jnp.concatenate([value] + [move(value, even, odd, step) for step in (3, 2, 1)], axis=0)

    z, x, y = (1 << shift for shift in SHIFTS)
    column = all_four(hub, z, z)
    plane, begun = lax.optimization_barrier((all_four(column, x, y), first(column)))
    half = plane.shape[0] // 2
    low, high = plane[:half], plane[half:]
    after_low, before_high = move(low, y, x, 3), move(high, y, x, 1)
    after_high, before_low = move(high, y, x, 3), move(low, y, x, 1)
    after_low, before_high, done = lax.optimization_barrier((after_low, before_high, early(plane, begun)))
    opposite = (move(after_low, y, x, 3), move(before_high, y, x, 1))
    opposite, done = lax.optimization_barrier((opposite, late(done)))
    pieces = [plane, after_low, after_high, before_low, before_high, *opposite]
    partner = shift_pairs(parts, 1, 2, 1)
    return pieces + [lax.ppermute(piece, "dom", partner) for piece in pieces], begun, done


def sum_over_devices(value, parts):
    value = value + lax.ppermute(value, "dom", shift_pairs(parts, 1, 2, 1))
    stride = 2
    while stride < parts:
        across, left, right = (
            lax.ppermute(value, "dom", shift_pairs(parts, stride, 4, step)) for step in (2, 1, 3)
        )
        value = (value + across) + (left + right)
        stride *= 4
    return value


def shards(block_vector, tile_values, tile_rows, tile_cols, tile_counts, export_rows, send_pick):
    parts = lax.axis_size("dom")
    slots, side, _ = tile_values.shape
    width = block_vector.shape[1]
    blocks = block_vector.shape[0] // side
    vec = block_vector.reshape(blocks, side, width)
    block, wide = (side, width), (side, 2 * width)
    every = jax.ShapeDtypeStruct((blocks,) + block, F32)
    sums = pltpu.VMEM((blocks + 1,) + block, F32)
    spread = pltpu.VMEM((blocks,) + wide, BF16)
    whole = pltpu.VMEM((SLOTS,) + block, F32)
    halved = pltpu.VMEM((SLOTS,) + wide, BF16)
    sems = pltpu.SemaphoreType.DMA((SLOTS,))
    tile_bytes = side * side * 4
    tile_flops = 8 * side * side * width

    own = call(
        hub_kernel,
        jax.ShapeDtypeStruct((EXPORT,) + block, F32),
        [ANY, SMEM],
        VMEM,
        [pltpu.SemaphoreType.DMA((EXPORT,))],
        0,
        2 * EXPORT * tile_bytes,
        63,
    )(vec, export_rows)
    def first(column):
        return call(
            degree_kernel,
            (
                jax.ShapeDtypeStruct((slots,) + wide, BF16),
                jax.ShapeDtypeStruct((blocks, side), F32),
                every,
            ),
            [ANY, ANY, SMEM, SMEM],
            (ANY, VMEM, VMEM),
            [whole, halved, sems, sems],
            slots * side * side * 4,
            2 * slots * tile_bytes,
            44,
        )(tile_values, column, tile_rows, tile_counts)

    def early(plane, found):
        _, scale_lane, _ = found
        hub_scale = scale_lane.at[export_rows[0]].get(mode="promise_in_bounds")
        sent = jnp.where(send_pick[0][:, None] == 0, hub_scale[0], hub_scale[1])
        sent = jnp.concatenate(
            [sent, jnp.broadcast_to(send_pick[0][:, None], sent.shape).astype(F32)], axis=1
        )
        received = lax.all_to_all(sent, "dom", split_axis=0, concat_axis=0, tiled=True)
        lists, places = call(
            index_kernel,
            (jax.ShapeDtypeStruct((FAR + slots,), jnp.int32), jax.ShapeDtypeStruct((parts,), jnp.int32)),
            [SMEM] * 4,
            (SMEM, SMEM),
            [],
            slots * side * side // 4,
            4 * slots,
        )(tile_rows, tile_counts, export_rows, lax.axis_index("dom").reshape(1))
        return received, lists, places

    offered, (split, scale_lane, scale_full), (received, lists, places) = gather_hubs(
        own, first, early, lambda done: done
    )
    scales = jnp.concatenate([scale_lane, received[:, :side]], axis=0)
    picks = received[:, side].astype(jnp.int32)

    hub = call(
        near_kernel,
        jax.ShapeDtypeStruct((EXPORT,) + block, F32),
        [ANY] * (2 + PIECES) + [SMEM] * 6 + [VMEM] * 2,
        VMEM,
        [whole, whole, pltpu.VMEM((EXPORT + 1,) + block, F32), sems, sems],
        slots // 16 * tile_flops,
        slots // 8 * tile_bytes,
        16,
    )(
        tile_values, vec, *offered, tile_rows, tile_cols, export_rows, picks, places, lists,
        scales, scale_full,
    )
    store = pltpu.VMEM((EXPORT * parts,) + block, F32)
    store_sems = pltpu.SemaphoreType.DMA((PIECES,))

    def far(plane, _):
        return call(
            far_kernel,
            jax.ShapeDtypeStruct((blocks,) + wide, BF16),
            [ANY] * (3 + PIECES) + [SMEM] * 7 + [VMEM] * 4,
            VMEM,
            [whole, halved, store, spread, sums, sems, sems, store_sems],
            slots // 2 * tile_flops,
            slots // 2 * tile_bytes,
            34,
        )(
            tile_values, split, plane, *offered,
            tile_rows, tile_cols, tile_counts, export_rows, picks, places, lists,
            scales, scale_full, vec, hub,
        )

    def inner(scaled):
        return call(
            inner_kernel,
            every,
            [ANY, VMEM, SMEM, SMEM, SMEM],
            VMEM,
            [halved, sums, sems],
            slots // 4 * tile_flops,
            slots // 4 * tile_bytes,
            34,
        )(split, scaled, tile_rows, tile_cols, tile_counts)

    offered_next, _, inner_next = gather_hubs(hub, lambda column: (), far, inner)
    second, gram = call(
        last_kernel,
        (every, jax.ShapeDtypeStruct((width, width), F32)),
        [ANY] * (1 + PIECES) + [SMEM] * 5 + [VMEM] * 2,
        (VMEM, VMEM),
        [halved, store, sums, pltpu.VMEM((2 * width, 2 * width), F32), sems, store_sems],
        slots // 2 * tile_flops,
        slots * tile_bytes,
        26,
    )(split, *offered_next, tile_rows, tile_cols, tile_counts, picks, places, scale_full, inner_next)
    basis = call(
        functools.partial(basis_kernel, factor=math.sqrt(blocks * side * parts)),
        every,
        [VMEM, VMEM],
        VMEM,
        [pltpu.VMEM((width, width), F32)],
        blocks * tile_flops,
        2 * blocks * tile_bytes,
    )(sum_over_devices(gram, parts), second)
    return basis.reshape(block_vector.shape)


def solution(mesh):
    in_specs = (
        P("dom", None),
        P("dom", None, None),
        P("dom"),
        P("dom"),
        P("dom", None),
        P("dom", None),
        P("dom", None),
    )
    out_specs = P("dom", None)
    return jax.shard_map(shards, mesh=mesh, in_specs=in_specs, out_specs=out_specs, check_vma=False)
```

```python
import functools
import math

import jax
import jax.numpy as jnp
from jax import lax
from jax.experimental import pallas as pl
from jax.experimental.pallas import tpu as pltpu
from jax.sharding import PartitionSpec as P

EXPORT = 2
SHIFTS = (1, 3, 5)
PIECES = 14
PLANE = 32
T_MAX = 320
NEAR, FAR = 8, 8 + T_MAX
SLOTS = 32
UNROLL = 8
F32 = jnp.float32
BF16 = jnp.bfloat16
VMEM = pl.BlockSpec(memory_space=pltpu.VMEM)
SMEM = pl.BlockSpec(memory_space=pltpu.SMEM)
ANY = pl.BlockSpec(memory_space=pltpu.HBM)


def halves(x):
    high = x.astype(BF16)
    low = (x - high.astype(F32)).astype(BF16)
    return jnp.concatenate([high, low], axis=1)


def product(left, right):
    both = jnp.dot(left, jnp.concatenate([right, right], axis=0), preferred_element_type=F32)
    width = both.shape[1] // 2
    return both[:, :width] + both[:, width:]


def stream(count, copies, work, group=None, ready=lambda: None):
    rounds = (count + UNROLL - 1) // UNROLL
    ahead = SLOTS // UNROLL - 1

    def of_round(r):
        first = r * UNROLL
        found = [] if group is None else [group(first, first & (SLOTS - 1))]
        for u in range(UNROLL):
            found.extend(copies(jnp.minimum(first + u, count - 1), (first + u) & (SLOTS - 1)))
        return found

    def start(r, carry):
        for copy in of_round(r):
            copy.start()
        return carry

    lax.fori_loop(0, jnp.minimum(ahead, rounds), start, 0)
    ready()

    def one_round(r, carry):
        @pl.when(r + ahead < rounds)
        def _():
            start(r + ahead, 0)

        for copy in of_round(r):
            copy.wait()
        first = r * UNROLL
        work(
            [
                (jnp.minimum(first + u, count - 1), (first + u) & (SLOTS - 1), first + u < count)
                for u in range(UNROLL)
            ]
        )
        return carry

    lax.fori_loop(0, rounds, one_round, 0)


def window(array, first):
    return jnp.minimum(first, array.shape[0] - UNROLL)


def piece_starts(pieces):
    starts = [0]
    for piece in pieces:
        starts.append(starts[-1] + piece.shape[0])
    return starts


class GhostCopy:
    def __init__(self, pieces, place, target, sem):
        self.pieces, self.place, self.target, self.sem = pieces, place, target, sem

    def start(self):
        starts = piece_starts(self.pieces)
        places = list(zip(self.pieces, starts[:-1], starts[1:]))

        def among(some):
            if len(some) == 1:
                piece, low, _ = some[0]
                pltpu.make_async_copy(piece.at[self.place - low], self.target, self.sem).start()
                return
            middle = len(some) // 2
            in_first = self.place < some[middle][1]
            pl.when(in_first)(lambda: among(some[:middle]))
            pl.when(jnp.logical_not(in_first))(lambda: among(some[middle:]))

        among(places)

    def wait(self):
        pltpu.make_async_copy(self.pieces[0].at[0], self.target, self.sem).wait()


def all_pieces(pieces, store, sem):
    return [
        pltpu.make_async_copy(piece, store.at[pl.ds(low, piece.shape[0])], sem.at[k])
        for k, (piece, low) in enumerate(zip(pieces, piece_starts(pieces)))
    ]


def hub_kernel(vec, exports, out, sem):
    copies = [pltpu.make_async_copy(vec.at[exports[0, k]], out.at[k], sem.at[k]) for k in range(EXPORT)]
    for copy in copies:
        copy.start()
    for copy in copies:
        copy.wait()


def index_kernel(rows, counts, exports, me, lists, places):
    inner, live = counts[0, 0], counts[0, 1]

    first_row, second_row = exports[0, 0], exports[0, 1]

    def sort(i, carry):
        near, far = carry
        row = rows[i]
        is_near = (row == first_row) | (row == second_row)
        is_far = jnp.logical_not(is_near) & (i >= inner)

        @pl.when(is_near)
        def _():
            lists[NEAR + near] = i

        @pl.when(is_far)
        def _():
            lists[FAR + far] = i

        return near + is_near.astype(jnp.int32), far + is_far.astype(jnp.int32)

    mine = me[0]

    def place(q, carry):
        ahead = [((q >> shift) - (mine >> shift)) & 3 for shift in SHIFTS]
        odd = q & 1
        second = jnp.where(odd == 0, ahead[1], ahead[2])
        final = jnp.where(odd == 0, ahead[2], ahead[1])
        piece = jnp.where(final == 3, 2, jnp.where(final == 2, 3, final))
        piece = piece + jnp.where(odd == (mine & 1), 0, 4)
        places[q] = piece * PLANE + (second * 4 + ahead[0]) * EXPORT
        return carry

    lax.fori_loop(0, places.shape[0], place, 0)

    near, far = lax.fori_loop(0, live, sort, (jnp.int32(0), jnp.int32(0)))
    lists[0] = near
    lists[1] = far


def degree_kernel(
    tiles, after, rows, counts,
    split_out, scale_lane, scale_full,
    buf, half, sem, out_sem,
):
    blocks = scale_full.shape[0]
    live = counts[0, 1]
    scale_full[...] = jnp.zeros_like(scale_full)

    rounds = (live + UNROLL - 1) // UNROLL
    depth = SLOTS // UNROLL

    def slots_of(r):
        return pl.ds((r & (depth - 1)) * UNROLL, UNROLL)

    def in_copy(r):
        return pltpu.make_async_copy(tiles.at[pl.ds(r * UNROLL, UNROLL)], buf.at[slots_of(r)], sem.at[(r & (depth - 1))])

    def out_copy(r):
        return pltpu.make_async_copy(
            half.at[slots_of(r)], split_out.at[pl.ds(r * UNROLL, UNROLL)], out_sem.at[(r & (depth - 1))]
        )

    def prime(r, carry):
        in_copy(r).start()
        return carry

    lax.fori_loop(0, jnp.minimum(depth - 1, rounds), prime, 0)

    def one_round(r, carry):
        @pl.when(r + depth - 1 < rounds)
        def _():
            in_copy(r + depth - 1).start()

        @pl.when(r >= depth)
        def _():
            out_copy(r - depth).wait()

        in_copy(r).wait()
        base = (r & (depth - 1)) * UNROLL
        for u in range(UNROLL):
            half[base + u] = halves(buf[base + u])
        for u in range(UNROLL):
            i = r * UNROLL + u
            row = rows[i]
            scale_full[row] = scale_full[row] + jnp.where(i < live, jnp.abs(buf[base + u]), 0.0)
        out_copy(r).start()
        return carry

    lax.fori_loop(0, rounds, one_round, 0)

    def scale_blocks(g, carry):
        totals = [scale_full[4 * g + u] for u in range(4)]
        sums = [lax.rsqrt(jnp.sum(total, axis=1, keepdims=True)) for total in totals]
        for u, down in enumerate(sums):
            full = jnp.broadcast_to(down, totals[u].shape)
            scale_full[4 * g + u] = full
            scale_lane[pl.ds(4 * g + u, 1), :] = jnp.transpose(full)[0:1, :]
        return carry

    lax.fori_loop(0, blocks // 4, scale_blocks, 0)

    def drain(r, carry):
        out_copy(r).wait()
        return carry

    lax.fori_loop(jnp.maximum(rounds - depth, 0), rounds, drain, 0)


def add_tiles(steps, left_of, right_of, row_of, total):
    parts = [product(left_of(i, slot), right_of(i, slot)) for i, slot, _ in steps]
    for (i, _, alive), part in zip(steps, parts):
        row = jnp.where(alive, row_of(i), total.shape[0] - 1)
        total[row] = total[row] + part


def halves_group(split, half, sem, begin):
    def group(first, slot):
        return pltpu.make_async_copy(
            split.at[pl.ds(window(split, begin + first), UNROLL)], half.at[pl.ds(slot, UNROLL)], sem.at[slot]
        )

    def tile(i, slot):
        first = i & -UNROLL
        place = begin + i - window(split, begin + first)
        return half[(slot & -UNROLL) + place]

    return group, tile


def add_inner(split, half, sem, scaled, rows, cols, count, total, row_of):
    group, tile = halves_group(split, half, sem, 0)

    def work(steps):
        add_tiles(steps, tile, lambda i, slot: scaled[cols[i]], row_of, total)

    stream(count, lambda i, slot: (), work, group)


def near_kernel(tiles, vec, *refs):
    pieces = refs[:PIECES]
    (
        rows, cols, exports, picks, places, lists, scales, scale_full,
        hub_out, buf, source, total, sem, source_sem,
    ) = refs[PIECES:]
    blocks = scale_full.shape[0]
    sources = pieces + (vec,)
    ghosts = piece_starts(pieces)[-1]
    total[...] = jnp.zeros_like(total)

    def copies(i, slot):
        t = lists[NEAR + i]
        col = cols[t]
        q = jnp.maximum(col - blocks, 0)
        place = jnp.where(col < blocks, ghosts + col, places[q] + picks[q])
        return (
            pltpu.make_async_copy(tiles.at[t], buf.at[slot], sem.at[slot]),
            GhostCopy(sources, place, source.at[slot], source_sem.at[slot]),
        )

    def work(steps):
        add_tiles(
            steps,
            lambda i, slot: halves(buf[slot] * scales[pl.ds(cols[lists[NEAR + i]], 1), :]),
            lambda i, slot: halves(source[slot]),
            lambda i: jnp.where(rows[lists[NEAR + i]] == exports[0, 0], 0, 1),
            total,
        )

    stream(lists[0], copies, work)
    for k in range(EXPORT):
        scale = scale_full[exports[0, k]]
        hub_out[k] = scale * (scale * total[k])


def far_kernel(tiles, split, after, *refs):
    pieces = refs[:PIECES]
    (
        rows, cols, counts, exports, picks, places, lists, scales, scale_full, vec, hub,
        scaled_out, buf, half, store, scaled, total, sem, half_sem, store_sem,
    ) = refs[PIECES:]
    blocks = scale_full.shape[0]
    bulk = all_pieces(pieces, store, store_sem)
    for copy in bulk:
        copy.start()
    total[...] = jnp.zeros_like(total)

    def scale_block(r, carry):
        scaled[r] = halves(scale_full[r] * vec[r])
        return carry

    lax.fori_loop(0, blocks, scale_block, 0)

    def other_row(i):
        row = rows[i]
        return jnp.where((row == exports[0, 0]) | (row == exports[0, 1]), blocks, row)

    add_inner(split, half, half_sem, scaled, rows, cols, counts[0, 0], total, other_row)

    def ghost_of(i):
        return cols[lists[FAR + i]] - blocks

    def copies(i, slot):
        return [pltpu.make_async_copy(tiles.at[lists[FAR + i]], buf.at[slot], sem.at[slot])]

    def right_of(i, slot):
        q = ghost_of(i)
        return halves(store[places[q] + picks[q]])

    def work(steps):
        add_tiles(
            steps,
            lambda i, slot: halves(buf[slot] * scales[pl.ds(blocks + ghost_of(i), 1), :]),
            right_of,
            lambda i: rows[lists[FAR + i]],
            total,
        )

    def ready():
        for copy in bulk:
            copy.wait()

    stream(lists[1], copies, work, ready=ready)

    def next_block(r, carry):
        scale = scale_full[r]
        scaled_out[r] = halves(scale * (scale * total[r]))
        return carry

    lax.fori_loop(0, blocks, next_block, 0)
    for k in range(EXPORT):
        scaled_out[exports[0, k]] = halves(hub[k])


def inner_kernel(split, scaled, rows, cols, counts, total_out, half, total, sem):
    total[...] = jnp.zeros_like(total)
    add_inner(split, half, sem, scaled, rows, cols, counts[0, 0], total, lambda i: rows[i])
    total_out[...] = total[0 : total_out.shape[0]]


def last_kernel(split, *refs):
    pieces = refs[:PIECES]
    (
        rows, cols, counts, picks, places, scale_full, inner_sum,
        second, gram, half, store, total, both, sem, store_sem,
    ) = refs[PIECES:]
    blocks, side, width = scale_full.shape
    bulk = all_pieces(pieces, store, store_sem)
    for copy in bulk:
        copy.start()
    total[0:blocks] = inner_sum[...]
    total[blocks] = jnp.zeros_like(total[blocks])
    both[...] = jnp.zeros_like(both)
    inner = counts[0, 0]
    group, tile = halves_group(split, half, sem, inner)

    def right_of(i, slot):
        q = cols[inner + i] - blocks
        return halves(store[places[q] + picks[q]])

    def work(steps):
        add_tiles(steps, tile, right_of, lambda i: rows[inner + i], total)

    def ready():
        for copy in bulk:
            copy.wait()

    stream(counts[0, 1] - inner, lambda i, slot: (), work, group, ready)

    def finish(g, carry):
        pieces = []
        for u in range(4):
            r = g * 4 + u
            value = scale_full[r] * total[r]
            second[r] = value
            pieces.append(halves(value))
        tall = jnp.concatenate(pieces, axis=0)
        both[...] += lax.dot_general(tall, tall, (((0,), (0,)), ((), ())), preferred_element_type=F32)
        return carry

    lax.fori_loop(0, blocks // 4, finish, 0)
    gram[...] = (both[0:width, 0:width] + both[width:, width:]) + (both[0:width, width:] + both[width:, 0:width])


def thirds(x):
    high = x.astype(BF16).astype(F32)
    rest = x - high
    middle = rest.astype(BF16).astype(F32)
    return high, middle, rest - middle


def inverse_factor(a, b, size):
    groups = size // 8
    sub = lax.broadcasted_iota(jnp.int32, (8, size), 0)
    masks = [sub == i for i in range(8)]
    rows = []
    for p in range(groups):
        block, other = a[p], b[p]
        s = [
            [jnp.broadcast_to(block[i : i + 1, 8 * p + j : 8 * p + j + 1], (8, size)) for j in range(i + 1)]
            for i in range(8)
        ]
        block_rows = [jnp.broadcast_to(block[i : i + 1, :], (8, size)) for i in range(8)]
        other_rows = [jnp.broadcast_to(other[i : i + 1, :], (8, size)) for i in range(8)]
        low = [[None] * 8 for _ in range(8)]
        reciprocals = []
        for k in range(8):
            reciprocal = 1.0 / s[k][k]
            reciprocals.append(reciprocal)
            for i in range(k + 1, 8):
                low[i][k] = s[i][k] * reciprocal
            for i in range(k + 1, 8):
                for j in range(k + 1, i + 1):
                    s[i][j] = s[i][j] - low[i][k] * s[j][k]
        inv = [[None] * 8 for _ in range(8)]
        for i in range(8):
            for j in range(i):
                total = low[i][j]
                for k in range(j + 1, i):
                    total = total + low[i][k] * inv[k][j]
                inv[i][j] = -total
        pivots, roots = reciprocals[0], s[0][0]
        for i in range(1, 8):
            pivots = jnp.where(masks[i], reciprocals[i], pivots)
            roots = jnp.where(masks[i], s[i][i], roots)
        new_block, new_other = block, other
        for j in range(7):
            coefficient = jnp.zeros((8, size), F32)
            for i in range(j + 1, 8):
                coefficient = jnp.where(masks[i], inv[i][j], coefficient)
            new_block = new_block + coefficient * block_rows[j]
            new_other = new_other + coefficient * other_rows[j]
        rows.append(new_other * lax.rsqrt(roots))
        if p + 1 == groups:
            break
        left = thirds(new_block)
        right = thirds(jnp.concatenate([new_block * pivots, new_other * pivots], axis=1))
        tall = jnp.concatenate([x for x in left for _ in range(3)] + [jnp.zeros((8, size), F32)], axis=0)
        wide = jnp.concatenate(list(right) * 3 + [jnp.zeros((8, 2 * size), F32)], axis=0)
        update = lax.dot_general(
            tall.astype(BF16), wide.astype(BF16), (((0,), (0,)), ((), ())), preferred_element_type=F32
        )
        for i in range(p + 1, groups):
            a[i] = a[i] - update[8 * i : 8 * i + 8, :size]
            b[i] = b[i] - update[8 * i : 8 * i + 8, size:]
    return rows


def basis_kernel(gram, second, out, inverse, *, factor):
    size = gram.shape[0]
    groups = size // 8
    lane = lax.broadcasted_iota(jnp.int32, (8, size), 1)
    sub = lax.broadcasted_iota(jnp.int32, (8, size), 0)
    a = [gram[8 * g : 8 * g + 8, :] for g in range(groups)]
    b = [jnp.where(lane == sub + 8 * g, 1.0, 0.0).astype(F32) for g in range(groups)]
    for g, row in enumerate(inverse_factor(a, b, size)):
        inverse[8 * g : 8 * g + 8, :] = row * factor
    high, middle, low = (x.astype(BF16) for x in thirds(jnp.transpose(inverse[...])))
    main = jnp.concatenate([jnp.concatenate([high, middle], axis=1)] * 2, axis=0)
    rest = jnp.concatenate([low, high], axis=0)

    def some(r, carry):
        for u in range(4):
            left = [x.astype(BF16) for x in thirds(second[4 * r + u])]
            part = jnp.dot(jnp.concatenate(left[:2], axis=1), main, preferred_element_type=F32)
            small = jnp.dot(jnp.concatenate(left[::2], axis=1), rest, preferred_element_type=F32)
            out[4 * r + u] = part[:, :size] + (part[:, size:] + small)
        return carry

    lax.fori_loop(0, second.shape[0] // 4, some, 0)


def call(kernel, out_shape, in_specs, out_specs, scratch, flops, data, vmem=16):
    return pl.pallas_call(
        kernel,
        out_shape=out_shape,
        in_specs=in_specs,
        out_specs=out_specs,
        scratch_shapes=scratch,
        cost_estimate=pl.CostEstimate(flops=flops, bytes_accessed=data, transcendentals=0),
        compiler_params=pltpu.CompilerParams(vmem_limit_bytes=vmem * 1024 * 1024),
    )


def shift_pairs(parts, stride, extent, step):
    pairs = []
    for device in range(parts):
        place = device // stride % extent
        pairs.append((device, device + ((place + step) % extent - place) * stride))
    return pairs


def gather_hubs(hub, first, early, late):
    parts = lax.axis_size("dom")

    def move(value, even, odd, step):
        pairs = [
            shift_pairs(parts, (even, odd)[device % 2], 4, step)[device] for device in range(parts)
        ]
        return lax.ppermute(value, "dom", pairs)

    def all_four(value, even, odd):
        return jnp.concatenate([value] + [move(value, even, odd, step) for step in (3, 2, 1)], axis=0)

    z, x, y = (1 << shift for shift in SHIFTS)
    column = all_four(hub, z, z)
    plane, begun = lax.optimization_barrier((all_four(column, x, y), first(column)))
    half = plane.shape[0] // 2
    low, high = plane[:half], plane[half:]
    after_low, before_high = move(low, y, x, 3), move(high, y, x, 1)
    after_high, before_low = move(high, y, x, 3), move(low, y, x, 1)
    after_low, before_high, done = lax.optimization_barrier((after_low, before_high, early(plane, begun)))
    opposite = (move(after_low, y, x, 3), move(before_high, y, x, 1))
    opposite, done = lax.optimization_barrier((opposite, late(done)))
    pieces = [plane, after_low, after_high, before_low, before_high, *opposite]
    partner = shift_pairs(parts, 1, 2, 1)
    return pieces + [lax.ppermute(piece, "dom", partner) for piece in pieces], begun, done


def sum_over_devices(value, parts):
    value = value + lax.ppermute(value, "dom", shift_pairs(parts, 1, 2, 1))
    stride = 2
    while stride < parts:
        across, left, right = (
            lax.ppermute(value, "dom", shift_pairs(parts, stride, 4, step)) for step in (2, 1, 3)
        )
        value = (value + across) + (left + right)
        stride *= 4
    return value


def shards(block_vector, tile_values, tile_rows, tile_cols, tile_counts, export_rows, send_pick):
    parts = lax.axis_size("dom")
    slots, side, _ = tile_values.shape
    width = block_vector.shape[1]
    blocks = block_vector.shape[0] // side
    vec = block_vector.reshape(blocks, side, width)
    block, wide = (side, width), (side, 2 * width)
    every = jax.ShapeDtypeStruct((blocks,) + block, F32)
    sums = pltpu.VMEM((blocks + 1,) + block, F32)
    spread = pltpu.VMEM((blocks,) + wide, BF16)
    whole = pltpu.VMEM((SLOTS,) + block, F32)
    halved = pltpu.VMEM((SLOTS,) + wide, BF16)
    sems = pltpu.SemaphoreType.DMA((SLOTS,))
    tile_bytes = side * side * 4
    tile_flops = 8 * side * side * width

    own = call(
        hub_kernel,
        jax.ShapeDtypeStruct((EXPORT,) + block, F32),
        [ANY, SMEM],
        VMEM,
        [pltpu.SemaphoreType.DMA((EXPORT,))],
        0,
        2 * EXPORT * tile_bytes,
        63,
    )(vec, export_rows)
    def first(column):
        return call(
            degree_kernel,
            (
                jax.ShapeDtypeStruct((slots,) + wide, BF16),
                jax.ShapeDtypeStruct((blocks, side), F32),
                every,
            ),
            [ANY, ANY, SMEM, SMEM],
            (ANY, VMEM, VMEM),
            [whole, halved, sems, sems],
            slots * side * side * 4,
            2 * slots * tile_bytes,
            44,
        )(tile_values, column, tile_rows, tile_counts)

    def early(plane, found):
        _, scale_lane, _ = found
        hub_scale = scale_lane.at[export_rows[0]].get(mode="promise_in_bounds")
        sent = jnp.where(send_pick[0][:, None] == 0, hub_scale[0], hub_scale[1])
        sent = jnp.concatenate(
            [sent, jnp.broadcast_to(send_pick[0][:, None], sent.shape).astype(F32)], axis=1
        )
        received = lax.all_to_all(sent, "dom", split_axis=0, concat_axis=0, tiled=True)
        return received

    def late(received):
        lists, places = call(
            index_kernel,
            (jax.ShapeDtypeStruct((FAR + slots,), jnp.int32), jax.ShapeDtypeStruct((parts,), jnp.int32)),
            [SMEM] * 4,
            (SMEM, SMEM),
            [],
            slots * side * side // 4,
            4 * slots,
        )(tile_rows, tile_counts, export_rows, lax.axis_index("dom").reshape(1))
        return received, lists, places

    offered, (split, scale_lane, scale_full), (received, lists, places) = gather_hubs(
        own, first, early, late
    )
    scales = jnp.concatenate([scale_lane, received[:, :side]], axis=0)
    picks = received[:, side].astype(jnp.int32)

    hub = call(
        near_kernel,
        jax.ShapeDtypeStruct((EXPORT,) + block, F32),
        [ANY] * (2 + PIECES) + [SMEM] * 6 + [VMEM] * 2,
        VMEM,
        [whole, whole, pltpu.VMEM((EXPORT + 1,) + block, F32), sems, sems],
        slots // 16 * tile_flops,
        slots // 8 * tile_bytes,
        16,
    )(
        tile_values, vec, *offered, tile_rows, tile_cols, export_rows, picks, places, lists,
        scales, scale_full,
    )
    store = pltpu.VMEM((EXPORT * parts,) + block, F32)
    store_sems = pltpu.SemaphoreType.DMA((PIECES,))

    def far(plane, _):
        return call(
            far_kernel,
            jax.ShapeDtypeStruct((blocks,) + wide, BF16),
            [ANY] * (3 + PIECES) + [SMEM] * 7 + [VMEM] * 4,
            VMEM,
            [whole, halved, store, spread, sums, sems, sems, store_sems],
            slots // 2 * tile_flops,
            slots // 2 * tile_bytes,
            34,
        )(
            tile_values, split, plane, *offered,
            tile_rows, tile_cols, tile_counts, export_rows, picks, places, lists,
            scales, scale_full, vec, hub,
        )

    def inner(scaled):
        return call(
            inner_kernel,
            every,
            [ANY, VMEM, SMEM, SMEM, SMEM],
            VMEM,
            [halved, sums, sems],
            slots // 4 * tile_flops,
            slots // 4 * tile_bytes,
            34,
        )(split, scaled, tile_rows, tile_cols, tile_counts)

    offered_next, _, inner_next = gather_hubs(hub, lambda column: (), far, inner)
    second, gram = call(
        last_kernel,
        (every, jax.ShapeDtypeStruct((width, width), F32)),
        [ANY] * (1 + PIECES) + [SMEM] * 5 + [VMEM] * 2,
        (VMEM, VMEM),
        [halved, store, sums, pltpu.VMEM((2 * width, 2 * width), F32), sems, store_sems],
        slots // 2 * tile_flops,
        slots * tile_bytes,
        26,
    )(split, *offered_next, tile_rows, tile_cols, tile_counts, picks, places, scale_full, inner_next)
    basis = call(
        functools.partial(basis_kernel, factor=math.sqrt(blocks * side * parts)),
        every,
        [VMEM, VMEM],
        VMEM,
        [pltpu.VMEM((width, width), F32)],
        blocks * tile_flops,
        2 * blocks * tile_bytes,
    )(sum_over_devices(gram, parts), second)
    return basis.reshape(block_vector.shape)


def solution(mesh):
    in_specs = (
        P("dom", None),
        P("dom", None, None),
        P("dom"),
        P("dom"),
        P("dom", None),
        P("dom", None),
        P("dom", None),
    )
    out_specs = P("dom", None)
    return jax.shard_map(shards, mesh=mesh, in_specs=in_specs, out_specs=out_specs, check_vma=False)
```
